128 devices in a mesh: dp: 8 (over z_lo, y), tensor: 16 (over x, z_hi, core).
Axes of the slice: x: 4, y: 4, z: 4 (z_hi: 2, z_lo: 2; z = z_hi * 2 + z_lo), core: 2. Of those that a mesh axis runs over, the one named last changes fastest.
Arguments:
- token_ids: int32 [1024], replicated, may hold values from 0 to 15999
- old_embed: bfloat16 [16000, 5120], P('tensor', 'dp'), as said below
- expand_in: bfloat16 [8192, 5120], P('dp'), may hold values from -0.078125 to 0.078125
- query_out: bfloat16 [4096, 5120], P('tensor'), may hold values from -0.078125 to 0.078125
- key_out: bfloat16 [4096, 5120], P('tensor'), may hold values from -0.078125 to 0.078125
- old_query: bfloat16 [5120, 5120], P('dp', 'tensor'), may hold values from -0.078125 to 0.078125
- old_key: bfloat16 [5120, 5120], P('dp', 'tensor'), may hold values from -0.078125 to 0.078125
Outputs:
- grown_embedding: bfloat16 [16000, 8192], P('tensor', 'dp')
- grown_query: bfloat16 [8192, 4096], P('dp', 'tensor')
- grown_key: bfloat16 [8192, 4096], P('dp', 'tensor')
- attention_entropy: float32 [1024, 32], P('dp', 'tensor')
The draws below stay inside these ranges and needn't reach their ends.
Inputs may be any that keep to these rules, and one draw needn't show every extreme that they name: `old_embed`: old embedding rows and features carry independent scales.
All inputs are finite; a program needn't handle non-finite values.
Results may differ from the reference program's by a relative error of at most 0.0097.
Values may be sent and summed in bfloat16 or wider, within the bound.
A program may use at most 128 MiB of HBM per device.

```python
import math
import jax
import jax.numpy as jnp
from jax import lax

D_OLD = 5120
D_NEW = 8192
VOCAB = 16000
HEADS = 32
HEAD = 128
TOK_DP = 128
TOKENS = 1024
N_DP = 8
N_TENSOR = 16


def draw_old_embed(key, part):
    first_key, second_key, third_key = jax.random.split(key, 3)
    row_scale = jnp.exp(jax.random.uniform(first_key, (VOCAB, 1), jnp.float32, math.log(0.3), math.log(3.0)))
    column_scale = jnp.exp(jax.random.uniform(second_key, (1, D_OLD), jnp.float32, math.log(0.4), math.log(4.0)))
    base_values = jax.random.normal(third_key, (VOCAB, D_OLD), jnp.float32)
    return (base_values * row_scale * column_scale).astype(jnp.bfloat16)


def plant(values, own_key, smallest, largest):
    longest = values.shape.index(max(values.shape))
    spots = []
    for shift in (0, 1):
        where = [jax.random.randint(jax.random.fold_in(own_key, axis), (), 0, length) for axis, length in enumerate(values.shape)]
        where[longest] = (where[longest] + shift) % values.shape[longest]
        spots.append(tuple(where))
    return values.at[spots[0]].set(smallest).at[spots[1]].set(largest)


def shard_levels(stream_key, extent, cuts, smallest, high):
    loudness, own = 1.0, jax.random.fold_in(stream_key, 6)
    for dim, shards_of in cuts:
        heights = jnp.exp(jax.random.uniform(jax.random.fold_in(own, dim), (shards_of,), jnp.float32, smallest / len(cuts), high / len(cuts)))
        loudness = loudness * jnp.repeat(heights, extent[dim] // shards_of).reshape([-1 if axis == dim else 1 for axis in range(len(extent))])
    return loudness


def centred(rng, shape, deviation, limit, pieces=(), held_as=jnp.bfloat16):
    loudness = shard_levels(rng, shape, pieces, -0.22, 0.18) if pieces else 1.0
    values = jax.random.normal(rng, shape, jnp.float32) * deviation * loudness
    return jnp.minimum(jnp.maximum(values, -limit), limit).astype(held_as)


def setup_inputs(seed: int = 0) -> dict:
    splits = jax.random.split(jax.random.key(seed), 8)
    return {
        "token_ids": plant(jax.random.randint(splits[0], (TOKENS,), 0, VOCAB), jax.random.fold_in(splits[0], 1), 0, VOCAB - 1).astype(jnp.int32),
        "old_embed": draw_old_embed(jax.random.fold_in(splits[7], 71), 0),
        "expand_in": centred(splits[2], (D_NEW, D_OLD), D_OLD ** -0.5, 0.078125, ((0, 8),)),
        "query_out": centred(splits[3], (HEADS * HEAD, D_OLD), D_OLD ** -0.5, 0.078125, ((0, 16),)),
        "key_out": centred(splits[4], (HEADS * HEAD, D_OLD), D_OLD ** -0.5, 0.078125, ((0, 16),)),
        "old_query": centred(splits[5], (D_OLD, D_OLD), D_OLD ** -0.5, 0.078125, ((0, 8), (1, 16))),
        "old_key": centred(splits[6], (D_OLD, D_OLD), D_OLD ** -0.5, 0.078125, ((0, 8), (1, 16))),
    }


EMBED_EPSILON = 1e-06
TOKEN_EPSILON = 1e-05

def grow_rows(row_block, expand_in):
    raw_rows = jnp.dot(row_block, expand_in.T, preferred_element_type=jnp.float32)
    old_ms = lax.optimization_barrier(jnp.mean(jnp.square(row_block.astype(jnp.float32)), axis=1))
    new_ms = lax.optimization_barrier(jnp.mean(jnp.square(raw_rows), axis=1))
    factor = jnp.sqrt((old_ms + EMBED_EPSILON) / (new_ms + EMBED_EPSILON))
    return (raw_rows * factor[:, None]).astype(jnp.bfloat16)

def rotate(values):
    half_size = HEAD // 2
    position = jnp.arange(TOK_DP).astype(jnp.float32)
    frequency = jnp.exp(-math.log(10000.0) * jnp.arange(half_size).astype(jnp.float32) * (2.0 / HEAD))
    angles = position[:, None] * frequency[None, :]
    cosine = jnp.cos(angles)[None, :, None, :]
    sine_table = jnp.sin(angles)[None, :, None, :]
    first_half = values[..., :half_size]
    second = values[..., half_size:]
    return jnp.concatenate([first_half * cosine - second * sine_table, second * cosine + first_half * sine_table], axis=-1)

def reference(token_ids, old_embed, expand_in, query_out, key_out, old_query, old_key):
    blocks = old_embed.reshape(N_TENSOR, VOCAB // N_TENSOR, D_OLD)
    grown_embedding = lax.map(lambda row_block: grow_rows(row_block, expand_in), blocks).reshape(VOCAB, D_NEW)
    inner_query = jnp.dot(query_out, old_query.T, preferred_element_type=jnp.float32).astype(jnp.bfloat16)
    inner_key = jnp.dot(key_out, old_key.T, preferred_element_type=jnp.float32).astype(jnp.bfloat16)
    grown_query = jnp.dot(expand_in, inner_query.T, preferred_element_type=jnp.float32).astype(jnp.bfloat16)
    grown_key = jnp.dot(expand_in, inner_key.T, preferred_element_type=jnp.float32).astype(jnp.bfloat16)
    hidden = jnp.take(grown_embedding, token_ids, axis=0)
    inverse_rms = lax.rsqrt(lax.optimization_barrier(jnp.mean(jnp.square(hidden.astype(jnp.float32)), axis=1)) + TOKEN_EPSILON)
    queries = jnp.dot(hidden, grown_query, preferred_element_type=jnp.float32) * inverse_rms[:, None]
    key_proj = jnp.dot(hidden, grown_key, preferred_element_type=jnp.float32) * inverse_rms[:, None]
    rotated_q = rotate(queries.reshape(N_DP, TOK_DP, HEADS, HEAD)).astype(jnp.bfloat16)
    rotated_k = rotate(key_proj.reshape(N_DP, TOK_DP, HEADS, HEAD)).astype(jnp.bfloat16)
    scores = jnp.einsum('sihd,sjhd->shij', rotated_q.astype(jnp.float32), rotated_k.astype(jnp.float32)) * HEAD ** (-0.5)
    causal = jnp.arange(TOK_DP)[:, None] >= jnp.arange(TOK_DP)[None, :]
    weights = jnp.where(causal[None, None], jnp.exp(scores), 0.0)
    weight_sum = lax.optimization_barrier(jnp.sum(weights, axis=-1))
    entropy = jnp.log(weight_sum) - lax.optimization_barrier(jnp.sum(weights * scores, axis=-1)) / weight_sum
    attention_entropy = jnp.transpose(entropy, (0, 2, 1)).reshape(TOKENS, HEADS)
    return (grown_embedding, grown_query, grown_key, attention_entropy)
```

```python
import heapq
import math

import jax
import jax.numpy as jnp
from jax import lax
from jax.experimental import pallas as pl
from jax.experimental.pallas import tpu as pltpu
from jax.sharding import PartitionSpec as P

D_NEW = 8192
HEAD = 128
N_DP = 8
N_TENSOR = 16

EMBED_EPSILON = 1e-06
TOKEN_EPSILON = 1e-05

MESH = pl.DeviceIdType.MESH
LAST = (((1,), (1,)), ((), ()))
VMEM_LIMIT = 66_000_000

STEP = {"y+": 1, "y-": -1, "x+": 1, "x-": -1}


class Place:
    def __init__(self):
        self.dp = lax.axis_index("dp")
        self.tensor = lax.axis_index("tensor")
        self.z_lo = self.dp // 4
        self.y = self.dp % 4
        self.x = self.tensor // 4
        self.z_hi = (self.tensor // 2) % 2
        self.core = self.tensor % 2

    def dp_at(self, rel):
        flip, shift = rel
        z_lo = 1 - self.z_lo if flip else self.z_lo
        return z_lo * 4 + (self.y + shift + 4) % 4

    def tensor_at(self, rel):
        flip, shift, core_flip = rel
        z_hi = 1 - self.z_hi if flip else self.z_hi
        core = 1 - self.core if core_flip else self.core
        return (((self.x + shift + 4) % 4) * 2 + z_hi) * 2 + core

    def across(self, link):
        if link in ("y+", "y-"):
            return (self.dp_at((0, STEP[link])), self.tensor)
        if link == "z":
            return (self.dp_at((1, 0)), self.tensor)
        if link in ("x+", "x-"):
            return (self.dp, self.tensor_at((0, STEP[link], 0)))
        if link == "h":
            return (self.dp, self.tensor_at((1, 0, 0)))
        return (self.dp, self.tensor_at((0, 0, 1)))


def seen_by_receiver(link, rel):
    if link in ("y+", "y-"):
        return (rel[0], (rel[1] - STEP[link]) % 4)
    if link == "z":
        return (1 - rel[0], rel[1])
    if link in ("x+", "x-"):
        return (rel[0], (rel[1] - STEP[link]) % 4, rel[2])
    if link == "h":
        return (1 - rel[0], rel[1], rel[2])
    return (rel[0], rel[1], 1 - rel[2])


def ring_tree(plus, minus, kind, rel, chunk, extra):
    near = (rel[0], (rel[1] - STEP[extra]) % 4) + tuple(rel[2:])
    return [(plus, kind, rel, chunk), (minus, kind, rel, chunk), (extra, kind, near, chunk)]


def gather_dp(kind, chunk, z_first, extra):
    other = "y-" if extra == "y+" else "y+"
    if z_first:
        sends = [("z", kind, (0, 0), chunk)]
        sends += ring_tree("y+", "y-", kind, (0, 0), chunk, extra)
        sends += ring_tree("y+", "y-", kind, (1, 0), chunk, other)
        return sends
    sends = ring_tree("y+", "y-", kind, (0, 0), chunk, extra)
    return sends + [("z", kind, (0, shift), chunk) for shift in (0, 1, 3, 2)]


def gather_tensor(kind, chunk, extra):
    other = "x-" if extra == "x+" else "x+"
    sends = [("h", kind, (0, 0, 0), chunk)]
    sends += ring_tree("x+", "x-", kind, (0, 0, 0), chunk, extra)
    sends += ring_tree("x+", "x-", kind, (1, 0, 0), chunk, other)
    sends += [("c", kind, (flip, shift, 0), chunk) for flip in (0, 1) for shift in (0, 1, 3, 2)]
    return sends


class Plan:
    def __init__(self, sends, megabytes, rates):
        self.sends = sends
        brought_by = {}
        for number, (link, kind, rel, chunk) in enumerate(sends):
            key = (kind, seen_by_receiver(link, rel), chunk)
            assert key not in brought_by
            brought_by[key] = number
        self.brought_by = brought_by
        self.keys = {number: key for key, number in brought_by.items()}
        self.after = {}
        self.first = []
        for number, (link, kind, rel, chunk) in enumerate(sends):
            source = brought_by.get((kind, rel, chunk))
            if source is None:
                assert not any(rel)
                self.first.append(number)
            else:
                self.after.setdefault(source, []).append(number)
        free, heap = {}, []

        def put(number, now):
            link, kind, _, chunk = sends[number]
            free[link] = max(free.get(link, 0.0), now) + megabytes[(kind, chunk)] / rates[link]
            heapq.heappush(heap, (free[link] + 1.5, number))

        for number in self.first:
            put(number, 0.0)
        self.order = []
        self.times = {}
        while heap:
            now, number = heapq.heappop(heap)
            self.order.append(number)
            self.times[number] = now
            for following in self.after.get(number, []):
                put(following, now)
        assert len(self.order) == len(sends)


RATES = {"y+": 0.0465, "y-": 0.0465, "z": 0.040, "x+": 0.0465, "x-": 0.0465, "h": 0.03, "c": 0.3}


def row_cuts(rows, pieces):
    step = -(-rows // (16 * pieces)) * 16
    return [(start, min(step, rows - start)) for start in range(0, rows, step)]


def greet(place, links):
    barrier = pltpu.get_barrier_semaphore()
    for link in links:
        pl.semaphore_signal(barrier, inc=1, device_id=place.across(link), device_id_type=MESH)
    pl.semaphore_wait(barrier, len(links))


X_CUTS = 5
X_MODES = ((True, "y+"), (True, "y-"), (True, "y+"), (False, "y+"), (False, "y-"))


def plan_first(vocab_rows, slab, out_slab, in_slab):
    cuts = row_cuts(vocab_rows, X_CUTS)
    sends = []
    for matrix in range(2):
        sends += gather_tensor("W", matrix, ("x+", "x-")[matrix])
    x_sends = []
    for chunk in (3, 4, 0, 1, 2):
        z_first, extra = X_MODES[chunk]
        x_sends += gather_dp("X", chunk, z_first, extra)
    x_sends.sort(key=lambda send: (send[0] == "z" and not X_MODES[send[3]][0]))
    sends += x_sends
    megabytes = {("X", chunk): cuts[chunk][1] * slab * 2e-6 for chunk in range(X_CUTS)}
    megabytes.update({("W", matrix): out_slab * in_slab * 2e-6 for matrix in range(2)})
    return cuts, Plan(sends, megabytes, RATES)


def first_kernel(
    plan, cuts, x_ref, w_ref, e_ref, q_ref, k_ref, raw_ref, inner_ref,
    x_all, w_all, e_all, o_all, total, send_sem, recv_sem, local_sem,
):
    place = Place()
    slab = x_ref.shape[1]
    greet(place, ("y+", "y-", "z", "x+", "x-", "h", "c"))

    def source(kind, rel, chunk):
        if kind == "X":
            start, size = cuts[chunk]
            if not any(rel):
                return x_ref.at[pl.ds(start, size), :]
            return x_all.at[place.dp_at(rel), pl.ds(start, size), :]
        if not any(rel):
            return w_ref.at[chunk]
        return w_all.at[chunk, place.tensor_at(rel)]

    def target(kind, rel, chunk):
        if kind == "X":
            start, size = cuts[chunk]
            return x_all.at[place.dp_at(rel), pl.ds(start, size), :]
        return w_all.at[chunk, place.tensor_at(rel)]

    def copy_of(number):
        link, kind, rel, chunk = plan.sends[number]
        return pltpu.make_async_remote_copy(
            src_ref=source(kind, rel, chunk),
            dst_ref=target(kind, rel, chunk),
            send_sem=send_sem.at[number],
            recv_sem=recv_sem.at[number],
            device_id=place.across(link),
            device_id_type=MESH,
        )

    def arrival_of(number):
        kind, rel, chunk = plan.keys[number]
        return pltpu.make_async_remote_copy(
            src_ref=target(kind, rel, chunk),
            dst_ref=target(kind, rel, chunk),
            send_sem=send_sem.at[number],
            recv_sem=recv_sem.at[number],
            device_id=place.across(plan.sends[number][0]),
            device_id_type=MESH,
        )

    for number in plan.first:
        copy_of(number).start()
    local = [
        pltpu.make_async_copy(x_ref, x_all.at[place.dp], local_sem.at[0]),
        pltpu.make_async_copy(w_ref.at[0], w_all.at[0, place.tensor], local_sem.at[1]),
        pltpu.make_async_copy(w_ref.at[1], w_all.at[1, place.tensor], local_sem.at[2]),
        pltpu.make_async_copy(e_ref, e_all, local_sem.at[3]),
        pltpu.make_async_copy(q_ref, o_all.at[0], local_sem.at[4]),
        pltpu.make_async_copy(k_ref, o_all.at[1], local_sem.at[5]),
    ]
    for copy in local:
        copy.start()
    for copy in local:
        copy.wait()

    tile = 256
    tiles = e_all.shape[0] // tile

    def add_raw(rel, fresh, half):
        at = place.dp_at(rel)
        columns = pl.ds(pl.multiple_of(at * slab, 128), slab)

        def body(number, _):
            rows = pl.ds(pl.multiple_of(number * tile, tile), tile)
            part = lax.dot_general(
                x_all[at], e_all[rows, columns], LAST, preferred_element_type=jnp.float32
            )
            if fresh:
                raw_ref[:, rows] = part
            else:
                raw_ref[:, rows] += part
            return 0

        lax.fori_loop(half * tiles // 2, (half + 1) * tiles // 2, body, 0)

    pair = 2 * w_all.shape[2]

    def add_inner(rel, matrix, fresh):
        chip = place.tensor_at((rel[0], rel[1], 0)) // 2
        columns = pl.ds(pl.multiple_of(chip * pair, 128), pair)
        slabs = w_all[matrix, pl.ds(chip * 2, 2)].reshape(pair, w_all.shape[3])
        part = jnp.dot(o_all[matrix, :, columns], slabs, preferred_element_type=jnp.float32)
        if fresh:
            total[matrix] = part
        else:
            total[matrix] += part

    landed = {("X", (0, 0), chunk) for chunk in range(len(cuts))}
    landed |= {("W", (0, 0, 0), matrix) for matrix in range(2)}
    waiting = []
    for rel in [(flip, shift) for flip in (0, 1) for shift in range(4)]:
        needs = {("X", rel, chunk) for chunk in range(len(cuts))}
        waiting += [(needs, ("raw", rel, half)) for half in range(2)]
    for matrix in range(2):
        for flip in (0, 1):
            for shift in range(4):
                needs = {("W", (flip, shift, core), matrix) for core in (0, 1)}
                waiting.append((needs, ("inner", (flip, shift), matrix)))
    done = set()

    def work(limit):
        for item in list(waiting):
            if limit == 0:
                return
            needs, (what, rel, which) = item
            if needs <= landed:
                waiting.remove(item)
                fresh = (what, which) not in done
                done.add((what, which))
                if what == "raw":
                    add_raw(rel, fresh, which)
                else:
                    add_inner(rel, which, fresh)
                limit -= 1

    work(1)
    for number in plan.order:
        arrival_of(number).wait_recv()
        for following in plan.after.get(number, []):
            copy_of(following).start()
        landed.add(plan.keys[number])
        work(1)
    work(-1)
    assert not waiting
    inner_ref[...] = total[...].astype(inner_ref.dtype)
    for number in range(len(plan.sends)):
        copy_of(number).wait_send()


def gather_and_grow(old_embed, expand_in, query_out, key_out, old_query, old_key):
    vocab_rows, slab = old_embed.shape
    in_slab, out_slab = old_query.shape
    head_cols = query_out.shape[0]
    turned = jnp.stack([old_query.T, old_key.T])
    cuts, plan = plan_first(vocab_rows, slab, out_slab, in_slab)
    count = len(plan.sends)
    anywhere = pl.BlockSpec(memory_space=pl.ANY)
    inside = pl.BlockSpec(memory_space=pltpu.VMEM)
    return pl.pallas_call(
        lambda *refs: first_kernel(plan, cuts, *refs),
        out_shape=(
            jax.ShapeDtypeStruct((vocab_rows, expand_in.shape[0]), jnp.float32),
            jax.ShapeDtypeStruct((2, head_cols, in_slab), jnp.bfloat16),
        ),
        in_specs=[anywhere] * 5,
        out_specs=(inside, inside),
        scratch_shapes=[
            pltpu.VMEM((N_DP, vocab_rows, slab), jnp.bfloat16),
            pltpu.VMEM((2, N_TENSOR, out_slab, in_slab), jnp.bfloat16),
            pltpu.VMEM(expand_in.shape, jnp.bfloat16),
            pltpu.VMEM((2,) + query_out.shape, jnp.bfloat16),
            pltpu.VMEM((2, head_cols, in_slab), jnp.float32),
            pltpu.SemaphoreType.DMA((count,)),
            pltpu.SemaphoreType.DMA((count,)),
            pltpu.SemaphoreType.DMA((6,)),
        ],
        compiler_params=pltpu.CompilerParams(
            collective_id=1, has_side_effects=True, vmem_limit_bytes=VMEM_LIMIT
        ),
        name="gather_and_grow",
    )(old_embed, turned, expand_in, query_out, key_out)


def contract_last(left_side, right_side):
    return lax.dot_general(left_side, right_side, LAST, preferred_element_type=jnp.float32)


def rotate(values, head_count):
    row_count = values.shape[0]
    shaped = values.reshape(row_count, head_count, HEAD)
    half_size = HEAD // 2
    position = jnp.arange(row_count).astype(jnp.float32)
    frequency = jnp.exp(
        -math.log(10000.0) * jnp.arange(half_size).astype(jnp.float32) * (2.0 / HEAD)
    )
    angles = position[:, None] * frequency[None, :]
    cosine = jnp.cos(angles)[:, None, :]
    sine_table = jnp.sin(angles)[:, None, :]
    first_half = shaped[..., :half_size]
    second = shaped[..., half_size:]
    return jnp.concatenate(
        [first_half * cosine - second * sine_table, second * cosine + first_half * sine_table],
        axis=-1,
    )


def entropy_of(queries, key_proj, head_count):
    rotated_q = rotate(queries, head_count).astype(jnp.bfloat16)
    rotated_k = rotate(key_proj, head_count).astype(jnp.bfloat16)
    scores = jnp.einsum(
        "ihd,jhd->hij", rotated_q, rotated_k, preferred_element_type=jnp.float32
    ) * HEAD ** (-0.5)
    row_count = queries.shape[0]
    causal = jnp.arange(row_count)[:, None] >= jnp.arange(row_count)[None, :]
    weights = jnp.where(causal[None], jnp.exp(scores), 0.0)
    weight_sum = jnp.sum(weights, axis=-1)
    entropy = jnp.log(weight_sum) - jnp.sum(weights * scores, axis=-1) / weight_sum
    return entropy.T


def on_device(token_ids, old_embed, expand_in, query_out, key_out, old_query, old_key):
    vocab_rows = old_embed.shape[0]
    old_width = expand_in.shape[1]
    head_cols = query_out.shape[0]
    head_count = head_cols // HEAD
    raw_rows, inner = gather_and_grow(old_embed, expand_in, query_out, key_out, old_query, old_key)
    squares = jnp.stack(
        [
            jnp.sum(jnp.square(old_embed.astype(jnp.float32)), axis=1),
            jnp.sum(jnp.square(raw_rows), axis=1),
        ]
    )
    squares = lax.psum(squares, "dp")
    factor = jnp.sqrt(
        (squares[0] / old_width + EMBED_EPSILON) / (squares[1] / D_NEW + EMBED_EPSILON)
    )
    grown_embedding = (raw_rows * factor[:, None]).astype(jnp.bfloat16)
    inner = lax.all_gather(inner, "dp", axis=2, tiled=True)
    grown_query = contract_last(expand_in, inner[0]).astype(jnp.bfloat16)
    grown_key = contract_last(expand_in, inner[1]).astype(jnp.bfloat16)
    offset_ids = token_ids - lax.axis_index("tensor") * vocab_rows
    chosen = (offset_ids[:, None] == jnp.arange(vocab_rows)[None, :]).astype(jnp.bfloat16)
    partial_rows = jnp.dot(chosen, grown_embedding, preferred_element_type=jnp.float32)
    hidden_cols = lax.psum(partial_rows.astype(jnp.bfloat16), "tensor")
    square_sum = jnp.sum(jnp.square(hidden_cols.astype(jnp.float32)), axis=1)
    queries = jnp.dot(hidden_cols, grown_query, preferred_element_type=jnp.float32)
    key_proj = jnp.dot(hidden_cols, grown_key, preferred_element_type=jnp.float32)
    both = jnp.concatenate([queries, key_proj], axis=1).astype(jnp.bfloat16)
    both = lax.psum_scatter(both, "dp", scatter_dimension=0, tiled=True).astype(jnp.float32)
    square_sum = lax.psum(square_sum, "dp")
    square_sum = lax.dynamic_slice(
        square_sum, (lax.axis_index("dp") * both.shape[0],), (both.shape[0],)
    )
    inverse_rms = lax.rsqrt(square_sum / D_NEW + TOKEN_EPSILON)
    both = both * inverse_rms[:, None]
    attention_entropy = entropy_of(both[:, :head_cols], both[:, head_cols:], head_count)
    return (grown_embedding, grown_query, grown_key, attention_entropy)


def solution(mesh):
    placed = (
        P(),
        P("tensor", "dp"),
        P("dp", None),
        P("tensor", None),
        P("tensor", None),
        P("dp", "tensor"),
        P("dp", "tensor"),
    )
    return jax.shard_map(
        on_device,
        mesh=mesh,
        in_specs=placed,
        out_specs=(P("tensor", "dp"), P("dp", "tensor"), P("dp", "tensor"), P("dp", "tensor")),
        check_vma=False,
    )
```

```python
import heapq
import math

import jax
import jax.numpy as jnp
from jax import lax
from jax.experimental import pallas as pl
from jax.experimental.pallas import tpu as pltpu
from jax.sharding import PartitionSpec as P

D_NEW = 8192
HEAD = 128
N_DP = 8
N_TENSOR = 16

EMBED_EPSILON = 1e-06
TOKEN_EPSILON = 1e-05

MESH = pl.DeviceIdType.MESH
LAST = (((1,), (1,)), ((), ()))
VMEM_LIMIT = 66_000_000

STEP = {"y+": 1, "y-": -1, "x+": 1, "x-": -1}


class Place:
    def __init__(self):
        self.dp = lax.axis_index("dp")
        self.tensor = lax.axis_index("tensor")
        self.z_lo = self.dp // 4
        self.y = self.dp % 4
        self.x = self.tensor // 4
        self.z_hi = (self.tensor // 2) % 2
        self.core = self.tensor % 2

    def dp_at(self, rel):
        flip, shift = rel
        z_lo = 1 - self.z_lo if flip else self.z_lo
        return z_lo * 4 + (self.y + shift + 4) % 4

    def tensor_at(self, rel):
        flip, shift, core_flip = rel
        z_hi = 1 - self.z_hi if flip else self.z_hi
        core = 1 - self.core if core_flip else self.core
        return (((self.x + shift + 4) % 4) * 2 + z_hi) * 2 + core

    def across(self, link):
        if link in ("y+", "y-"):
            return (self.dp_at((0, STEP[link])), self.tensor)
        if link == "z":
            return (self.dp_at((1, 0)), self.tensor)
        if link in ("x+", "x-"):
            return (self.dp, self.tensor_at((0, STEP[link], 0)))
        if link == "h":
            return (self.dp, self.tensor_at((1, 0, 0)))
        return (self.dp, self.tensor_at((0, 0, 1)))


def seen_by_receiver(link, rel):
    if link in ("y+", "y-"):
        return (rel[0], (rel[1] - STEP[link]) % 4)
    if link == "z":
        return (1 - rel[0], rel[1])
    if link in ("x+", "x-"):
        return (rel[0], (rel[1] - STEP[link]) % 4, rel[2])
    if link == "h":
        return (1 - rel[0], rel[1], rel[2])
    return (rel[0], rel[1], 1 - rel[2])


def ring_tree(plus, minus, kind, rel, chunk, extra):
    near = (rel[0], (rel[1] - STEP[extra]) % 4) + tuple(rel[2:])
    return [(plus, kind, rel, chunk), (minus, kind, rel, chunk), (extra, kind, near, chunk)]


def gather_dp(kind, chunk, z_first, extra):
    other = "y-" if extra == "y+" else "y+"
    if z_first:
        sends = [("z", kind, (0, 0), chunk)]
        sends += ring_tree("y+", "y-", kind, (0, 0), chunk, extra)
        sends += ring_tree("y+", "y-", kind, (1, 0), chunk, other)
        return sends
    sends = ring_tree("y+", "y-", kind, (0, 0), chunk, extra)
    return sends + [("z", kind, (0, shift), chunk) for shift in (0, 1, 3, 2)]


def gather_tensor(kind, chunk, extra):
    other = "x-" if extra == "x+" else "x+"
    sends = [("h", kind, (0, 0, 0), chunk)]
    sends += ring_tree("x+", "x-", kind, (0, 0, 0), chunk, extra)
    sends += ring_tree("x+", "x-", kind, (1, 0, 0), chunk, other)
    sends += [("c", kind, (flip, shift, 0), chunk) for flip in (0, 1) for shift in (0, 1, 3, 2)]
    return sends


class Plan:
    def __init__(self, sends, megabytes, rates):
        self.sends = sends
        brought_by = {}
        for number, (link, kind, rel, chunk) in enumerate(sends):
            key = (kind, seen_by_receiver(link, rel), chunk)
            assert key not in brought_by
            brought_by[key] = number
        self.brought_by = brought_by
        self.keys = {number: key for key, number in brought_by.items()}
        self.after = {}
        self.first = []
        for number, (link, kind, rel, chunk) in enumerate(sends):
            source = brought_by.get((kind, rel, chunk))
            if source is None:
                assert not any(rel)
                self.first.append(number)
            else:
                self.after.setdefault(source, []).append(number)
        free, heap = {}, []

        def put(number, now):
            link, kind, _, chunk = sends[number]
            free[link] = max(free.get(link, 0.0), now) + megabytes[(kind, chunk)] / rates[link]
            heapq.heappush(heap, (free[link] + 1.5, number))

        for number in self.first:
            put(number, 0.0)
        self.order = []
        self.times = {}
        while heap:
            now, number = heapq.heappop(heap)
            self.order.append(number)
            self.times[number] = now
            for following in self.after.get(number, []):
                put(following, now)
        assert len(self.order) == len(sends)


RATES = {"y+": 0.0465, "y-": 0.0465, "z": 0.040, "x+": 0.0465, "x-": 0.0465, "h": 0.03, "c": 0.3}


def row_cuts(rows, pieces):
    step = -(-rows // (16 * pieces)) * 16
    return [(start, min(step, rows - start)) for start in range(0, rows, step)]


def greet(place, links):
    barrier = pltpu.get_barrier_semaphore()
    for link in links:
        pl.semaphore_signal(barrier, inc=1, device_id=place.across(link), device_id_type=MESH)
    pl.semaphore_wait(barrier, len(links))


X_CUTS = 5
X_MODES = ((True, "y+"), (True, "y-"), (True, "y+"), (False, "y+"), (False, "y-"))


def plan_first(vocab_rows, slab, out_slab, in_slab):
    cuts = row_cuts(vocab_rows, X_CUTS)
    sends = []
    for matrix in range(2):
        sends += gather_tensor("W", matrix, ("x+", "x-")[matrix])
    x_sends = []
    for chunk in (3, 4, 0, 1, 2):
        z_first, extra = X_MODES[chunk]
        x_sends += gather_dp("X", chunk, z_first, extra)
    x_sends.sort(key=lambda send: (send[0] == "z" and not X_MODES[send[3]][0]))
    sends += x_sends
    megabytes = {("X", chunk): cuts[chunk][1] * slab * 2e-6 for chunk in range(X_CUTS)}
    megabytes.update({("W", matrix): out_slab * in_slab * 2e-6 for matrix in range(2)})
    return cuts, Plan(sends, megabytes, RATES)


def first_kernel(
    plan, cuts, x_ref, w_ref, e_ref, q_ref, k_ref, raw_ref, inner_ref,
    x_all, w_all, e_all, o_all, total, send_sem, recv_sem, local_sem,
):
    place = Place()
    slab = x_ref.shape[1]
    greet(place, ("y+", "y-", "z", "x+", "x-", "h", "c"))

    def source(kind, rel, chunk):
        if kind == "X":
            start, size = cuts[chunk]
            if not any(rel):
                return x_ref.at[pl.ds(start, size), :]
            return x_all.at[place.dp_at(rel), pl.ds(start, size), :]
        if not any(rel):
            return w_ref.at[chunk]
        return w_all.at[chunk, place.tensor_at(rel)]

    def target(kind, rel, chunk):
        if kind == "X":
            start, size = cuts[chunk]
            return x_all.at[place.dp_at(rel), pl.ds(start, size), :]
        return w_all.at[chunk, place.tensor_at(rel)]

    def copy_of(number):
        link, kind, rel, chunk = plan.sends[number]
        return pltpu.make_async_remote_copy(
            src_ref=source(kind, rel, chunk),
            dst_ref=target(kind, rel, chunk),
            send_sem=send_sem.at[number],
            recv_sem=recv_sem.at[number],
            device_id=place.across(link),
            device_id_type=MESH,
        )

    def arrival_of(number):
        kind, rel, chunk = plan.keys[number]
        return pltpu.make_async_remote_copy(
            src_ref=target(kind, rel, chunk),
            dst_ref=target(kind, rel, chunk),
            send_sem=send_sem.at[number],
            recv_sem=recv_sem.at[number],
            device_id=place.across(plan.sends[number][0]),
            device_id_type=MESH,
        )

    for number in plan.first:
        copy_of(number).start()
    local = [
        pltpu.make_async_copy(x_ref, x_all.at[place.dp], local_sem.at[0]),
        pltpu.make_async_copy(w_ref.at[0], w_all.at[0, place.tensor], local_sem.at[1]),
        pltpu.make_async_copy(w_ref.at[1], w_all.at[1, place.tensor], local_sem.at[2]),
        pltpu.make_async_copy(e_ref, e_all, local_sem.at[3]),
        pltpu.make_async_copy(q_ref, o_all.at[0], local_sem.at[4]),
        pltpu.make_async_copy(k_ref, o_all.at[1], local_sem.at[5]),
    ]
    for copy in local:
        copy.start()
    for copy in local:
        copy.wait()

    tile = 256
    tiles = e_all.shape[0] // tile

    def add_raw(rel, fresh, half):
        at = place.dp_at(rel)
        columns = pl.ds(pl.multiple_of(at * slab, 128), slab)

        def body(number, _):
            rows = pl.ds(pl.multiple_of(number * tile, tile), tile)
            part = lax.dot_general(
                x_all[at], e_all[rows, columns], LAST, preferred_element_type=jnp.float32
            )
            if fresh:
                raw_ref[:, rows] = part
            else:
                raw_ref[:, rows] += part
            return 0

        lax.fori_loop(half * tiles // 2, (half + 1) * tiles // 2, body, 0)

    pair = 2 * w_all.shape[2]

    def add_inner(rel, matrix, fresh):
        chip = place.tensor_at((rel[0], rel[1], 0)) // 2
        columns = pl.ds(pl.multiple_of(chip * pair, 128), pair)
        slabs = w_all[matrix, pl.ds(chip * 2, 2)].reshape(pair, w_all.shape[3])
        part = jnp.dot(o_all[matrix, :, columns], slabs, preferred_element_type=jnp.float32)
        if fresh:
            total[matrix] = part
        else:
            total[matrix] += part

    landed = {("X", (0, 0), chunk) for chunk in range(len(cuts))}
    landed |= {("W", (0, 0, 0), matrix) for matrix in range(2)}
    waiting = []
    for rel in [(flip, shift) for flip in (0, 1) for shift in range(4)]:
        needs = {("X", rel, chunk) for chunk in range(len(cuts))}
        waiting += [(needs, ("raw", rel, half)) for half in range(2)]
    for matrix in range(2):
        for flip in (0, 1):
            for shift in range(4):
                needs = {("W", (flip, shift, core), matrix) for core in (0, 1)}
                waiting.append((needs, ("inner", (flip, shift), matrix)))
    done = set()

    def work(limit):
        for item in list(waiting):
            if limit == 0:
                return
            needs, (what, rel, which) = item
            if needs <= landed:
                waiting.remove(item)
                fresh = (what, which) not in done
                done.add((what, which))
                if what == "raw":
                    add_raw(rel, fresh, which)
                else:
                    add_inner(rel, which, fresh)
                limit -= 1

    work(1)
    for number in plan.order:
        arrival_of(number).wait_recv()
        for following in plan.after.get(number, []):
            copy_of(following).start()
        landed.add(plan.keys[number])
        work(1)
    work(-1)
    assert not waiting
    inner_ref[...] = total[...].astype(inner_ref.dtype)
    for number in range(len(plan.sends)):
        copy_of(number).wait_send()


def gather_and_grow(old_embed, expand_in, query_out, key_out, old_query, old_key):
    vocab_rows, slab = old_embed.shape
    in_slab, out_slab = old_query.shape
    head_cols = query_out.shape[0]
    turned = jnp.stack([old_query.T, old_key.T])
    cuts, plan = plan_first(vocab_rows, slab, out_slab, in_slab)
    count = len(plan.sends)
    anywhere = pl.BlockSpec(memory_space=pl.ANY)
    inside = pl.BlockSpec(memory_space=pltpu.VMEM)
    return pl.pallas_call(
        lambda *refs: first_kernel(plan, cuts, *refs),
        out_shape=(
            jax.ShapeDtypeStruct((vocab_rows, expand_in.shape[0]), jnp.float32),
            jax.ShapeDtypeStruct((2, head_cols, in_slab), jnp.bfloat16),
        ),
        in_specs=[anywhere] * 5,
        out_specs=(inside, inside),
        scratch_shapes=[
            pltpu.VMEM((N_DP, vocab_rows, slab), jnp.bfloat16),
            pltpu.VMEM((2, N_TENSOR, out_slab, in_slab), jnp.bfloat16),
            pltpu.VMEM(expand_in.shape, jnp.bfloat16),
            pltpu.VMEM((2,) + query_out.shape, jnp.bfloat16),
            pltpu.VMEM((2, head_cols, in_slab), jnp.float32),
            pltpu.SemaphoreType.DMA((count,)),
            pltpu.SemaphoreType.DMA((count,)),
            pltpu.SemaphoreType.DMA((6,)),
        ],
        compiler_params=pltpu.CompilerParams(
            collective_id=1, has_side_effects=True, vmem_limit_bytes=VMEM_LIMIT
        ),
        name="gather_and_grow",
    )(old_embed, turned, expand_in, query_out, key_out)


class Flow:
    def __init__(self):
        self.sends = {}
        self.tasks = []

    def send(self, name, link, megabytes, source, target, to):
        assert name not in self.sends
        self.sends[name] = (link, megabytes, source, target, to)
        return name

    def task(self, needs, cost, run, sends=(), rank=5, after=(), name=None):
        self.tasks.append((frozenset(needs), cost, run, tuple(sends), rank, frozenset(after), name))

    def arrange(self, rates):
        free, landing, done, order = {}, {}, set(), []
        left = list(range(len(self.tasks)))
        now = 0.0
        while left:
            ready = []
            for number in left:
                needs, _, _, _, rank, after, _ = self.tasks[number]
                if after <= done and all(landing.get(need, 1e9) <= now for need in needs):
                    ready.append((rank, number))
            if not ready:
                later = [
                    max(landing.get(need, 1e9) for need in self.tasks[number][0])
                    for number in left
                    if self.tasks[number][5] <= done and self.tasks[number][0]
                ]
                assert later and min(later) < 1e8
                now = min(later)
                continue
            number = min(ready)[1]
            left.remove(number)
            order.append(number)
            _, cost, _, sends, _, _, name = self.tasks[number]
            now += cost
            if name is not None:
                done.add(name)
            for send in sends:
                link, megabytes = self.sends[send][:2]
                free[link] = max(free.get(link, 0.0), now) + megabytes / rates[link]
                landing[send] = free[link] + 1.5
        self.length = now
        return order

    def emit(self, order, send_sem, recv_sem):
        number_of = {name: number for number, name in enumerate(self.sends)}

        def copy_of(name):
            _, _, source, target, to = self.sends[name]
            return pltpu.make_async_remote_copy(
                src_ref=source(),
                dst_ref=target(),
                send_sem=send_sem.at[number_of[name]],
                recv_sem=recv_sem.at[number_of[name]],
                device_id=to(),
                device_id_type=MESH,
            )

        arrived, started = set(), []
        for number in order:
            needs, _, run, sends, _, _, _ = self.tasks[number]
            for need in sorted(needs - arrived, key=str):
                copy_of(need).wait_recv()
                arrived.add(need)
            if run is not None:
                run()
            for send in sends:
                copy_of(send).start()
                started.append(send)
        assert arrived == set(self.sends) and sorted(started, key=str) == sorted(self.sends, key=str)
        for name in self.sends:
            copy_of(name).wait_send()


LINK_RATES = {
    "y+": 0.0465, "y-": 0.0465, "z": 0.0465, "x+": 0.0465, "x-": 0.0465, "h": 0.0465, "c": 0.3, "far": 0.03,
}
DP_PEERS = ((1, 2), (0, 2), (1, 1), (1, 3), (1, 0), (0, 1), (0, 3))
PEER_LINKS = {(1, 2): "far", (0, 2): "far", (1, 1): "y+", (1, 3): "y-", (1, 0): "z", (0, 1): "y+", (0, 3): "y-"}
INNER_MODES = ((True, "y+"), (True, "y-"), (True, "y+"), (False, "y-"))


def second_kernel(
    sizes, raw_ref, x_ref, tokens_ref, inner_ref, e_ref,
    ge_ref, gq_ref, gk_ref, both_ref,
    raw_all, x_all, e_all, inner_all, grown_sum, lanes, squares, squares_in, ge_pad,
    masked, core_in, left_in, right_in, left_block, right_block, half_in, hidden,
    part_out, part_in, own_part, send_sem, recv_sem, local_sem,
):
    place = Place()
    vocab_rows, new_cols = raw_ref.shape
    head_cols, slab = inner_ref.shape[1:]
    token_rows = tokens_ref.shape[0]
    grown = (gq_ref, gk_ref)
    old_width, new_width = sizes
    per_seq = both_ref.shape[0]

    barrier = pltpu.get_barrier_semaphore()
    friends = [place.across(link) for link in ("x+", "x-", "h", "c")]
    friends += [(place.dp_at(rel), place.tensor) for rel in DP_PEERS]
    for friend in friends:
        pl.semaphore_signal(barrier, inc=1, device_id=friend, device_id_type=MESH)
    local = [
        pltpu.make_async_copy(raw_ref, raw_all, local_sem.at[0]),
        pltpu.make_async_copy(x_ref, x_all, local_sem.at[1]),
        pltpu.make_async_copy(inner_ref, inner_all.at[place.dp], local_sem.at[2]),
        pltpu.make_async_copy(e_ref, e_all, local_sem.at[3]),
    ]
    for copy in local:
        copy.start()
    pl.semaphore_wait(barrier, len(friends))

    flow = Flow()

    half = head_cols // 2
    sends = []
    for chunk, (z_first, extra) in enumerate(INNER_MODES):
        sends += gather_dp("I", chunk, z_first, extra)
    brought_by = {
        ("I", seen_by_receiver(link, rel), chunk): (link, rel, chunk) for link, _, rel, chunk in sends
    }

    def inner_view(ref, chunk):
        return ref.at[chunk // 2, pl.ds((chunk % 2) * half, half), :]

    first, after = [], {}
    for link, kind, rel, chunk in sends:
        def source(rel=rel, chunk=chunk):
            if not any(rel):
                return inner_view(inner_ref, chunk)
            return inner_view(inner_all.at[place.dp_at(rel)], chunk)

        def target(rel=rel, chunk=chunk):
            return inner_view(inner_all.at[place.dp_at(rel)], chunk)

        name = ("I", link, rel, chunk)
        flow.send(name, link, half * slab * 2e-6, source, target, lambda link=link: place.across(link))
        cause = brought_by.get((kind, rel, chunk))
        if cause is None:
            first.append(name)
        else:
            after.setdefault(("I",) + cause, []).append(name)
    flow.task((), 0.1, None, first, rank=0)
    for link, _, rel, chunk in sends:
        name = ("I", link, rel, chunk)
        flow.task((name,), 0.02, None, after.get(name, ()), rank=0)

    tile = 256
    e_rows = e_all.shape[0]
    seen = set()

    def add_grown(rel, matrix):
        at = place.dp_at(rel)
        columns = pl.ds(pl.multiple_of(at * slab, 128), slab)
        fresh = matrix not in seen
        seen.add(matrix)

        def body(number, _):
            rows = pl.ds(pl.multiple_of(number * tile, tile), tile)
            part = lax.dot_general(
                e_all[rows, columns], inner_all[at, matrix], LAST, preferred_element_type=jnp.float32
            )
            if fresh:
                grown_sum[matrix, rows, :] = part
            else:
                grown_sum[matrix, rows, :] += part
            return 0

        lax.fori_loop(0, e_rows // tile, body, 0)

    for rel in [(flip, shift) for flip in (0, 1) for shift in (0, 1, 3, 2)]:
        for matrix in range(2):
            needs = []
            if any(rel):
                for chunk in (2 * matrix, 2 * matrix + 1):
                    needs.append(("I",) + brought_by[("I", rel, chunk)])
            flow.task(
                needs, 0.8, lambda rel=rel, matrix=matrix: add_grown(rel, matrix),
                rank=6, name=("grown", rel, matrix), after=(("loaded",),),
            )

    def lane_sums(values_ref):
        rows, columns = values_ref.shape
        sums = None
        for start in range(0, columns, 128):
            part = jnp.square(values_ref[:, start:start + 128].astype(jnp.float32))
            sums = part if sums is None else sums + part
        lanes[pl.ds(lanes.shape[0] - 32, 32), :] = jnp.zeros((32, 128), jnp.float32)
        lanes[pl.ds(0, rows), :] = sums
        return jnp.sum(lanes[...].T, axis=0, keepdims=True)

    def load_and_square():
        for copy in local:
            copy.wait()
        row = lax.broadcasted_iota(jnp.int32, squares.shape, 0)
        new_row = jnp.broadcast_to(lane_sums(raw_all), squares.shape)
        old_row = jnp.broadcast_to(lane_sums(x_all), squares.shape)
        squares[...] = jnp.where(row == 0, new_row, jnp.where(row == 1, old_row, 0.0))

    square_sends = []
    for number, rel in enumerate(DP_PEERS):
        square_sends.append(
            flow.send(
                ("S", number), "far", 0.03, lambda: squares, lambda number=number: squares_in.at[number],
                lambda rel=rel: (place.dp_at(rel), place.tensor),
            )
        )
    flow.task((), 4.0, load_and_square, square_sends, rank=1, name=("loaded",))

    def rescale():
        total = squares[...]
        for number in range(len(DP_PEERS)):
            total = total + squares_in[number]
        factor = jnp.sqrt(
            (total[1:2] / old_width + EMBED_EPSILON) / (total[0:1] / new_width + EMBED_EPSILON)
        )
        column = jnp.broadcast_to(factor, (128, factor.shape[1])).T[:vocab_rows]
        ge_pad[pl.ds(ge_pad.shape[0] - 32, 32), :] = jnp.zeros((32, new_cols), jnp.bfloat16)
        for start in range(0, new_cols, 128):
            scaled = (raw_all[:, start:start + 128] * column).astype(jnp.bfloat16)
            ge_pad[pl.ds(0, vocab_rows), start:start + 128] = scaled
            ge_ref[:, start:start + 128] = scaled

    flow.task(square_sends, 2.5, rescale, rank=1, name=("scaled",), after=(("loaded",),))

    core_rows, chip_rows, own_rows = token_rows // 2, token_rows // 8, token_rows // 16
    mine = place.core * core_rows
    theirs = (1 - place.core) * core_rows
    middle = new_cols // 2

    def rows_of(core, shift):
        start = (1 - place.core if core else place.core) * core_rows + ((place.x + shift + 4) % 4) * chip_rows
        return pl.ds(pl.multiple_of(start, chip_rows), chip_rows)

    def small_rows(flip):
        z_hi = 1 - place.z_hi if flip else place.z_hi
        start = mine + place.x * chip_rows + z_hi * own_rows
        return pl.ds(pl.multiple_of(start, own_rows), own_rows)

    def choose(start):
        def body(number, _):
            rows = pl.ds(pl.multiple_of(start + number * tile, tile), tile)
            ids = tokens_ref[rows, :] - place.tensor * vocab_rows
            column = lax.broadcasted_iota(jnp.int32, (tile, ge_pad.shape[0]), 1)
            chosen = jnp.where(ids == column, 1.0, 0.0).astype(jnp.bfloat16)
            masked[rows, :] = jnp.dot(
                chosen, ge_pad[...], preferred_element_type=jnp.float32
            ).astype(jnp.bfloat16)
            return 0

        lax.fori_loop(0, core_rows // tile, body, 0)

    core_mb = core_rows * new_cols * 2e-6
    to = lambda link: (lambda: place.across(link))
    whole = lambda start, size: pl.ds(pl.multiple_of(start, size), size)
    flow.send("c1", "c", core_mb, lambda: masked.at[whole(theirs, core_rows), :], lambda: core_in, to("c"))
    flow.task((), 1.5, lambda: choose(theirs), ("c1",), rank=1, name=("theirs",), after=(("scaled",),))
    flow.task((), 1.5, lambda: choose(mine), rank=1, name=("mine",), after=(("theirs",),))

    def add_core():
        rows = whole(mine, core_rows)
        masked[rows, :] += core_in[...]

    block_mb = core_mb / 4
    left_part, right_part = pl.ds(0, middle), pl.ds(middle, middle)
    flow.send("r+", "x+", block_mb / 2, lambda: masked.at[rows_of(0, 2), left_part], lambda: left_in, to("x+"))
    flow.send("r-", "x-", block_mb / 2, lambda: masked.at[rows_of(0, 2), right_part], lambda: right_in, to("x-"))
    flow.task(("c1",), 0.7, add_core, ("r+", "r-"), rank=1, name=("core",), after=(("mine",),))

    def add_left():
        masked[rows_of(0, 1), left_part] += left_in[...]

    def add_right():
        masked[rows_of(0, 3), right_part] += right_in[...]

    flow.send("b+", "x+", block_mb, lambda: masked.at[rows_of(0, 1), :], lambda: left_block, to("x+"))
    flow.send("b-", "x-", block_mb, lambda: masked.at[rows_of(0, 3), :], lambda: right_block, to("x-"))
    flow.task(("r+",), 0.1, add_left, ("b+",), rank=1, after=(("core",),))
    flow.task(("r-",), 0.1, add_right, ("b-",), rank=1, after=(("core",),))

    def add_blocks():
        masked[rows_of(0, 0), :] += left_block[...] + right_block[...]

    flow.send("h1", "h", block_mb / 2, lambda: masked.at[small_rows(1), :], lambda: half_in, to("h"))
    flow.task(("b+", "b-"), 0.2, add_blocks, ("h1",), rank=1, name=("blocks",), after=(("core",),))

    def add_half():
        hidden[small_rows(0), :] = masked[small_rows(0), :] + half_in[...]

    flow.send("h2", "h", block_mb / 2, lambda: hidden.at[small_rows(0), :], lambda: hidden.at[small_rows(0), :], to("h"))
    flow.task(("h1",), 0.1, add_half, ("h2",), rank=1, name=("half",), after=(("blocks",),))

    def same(name, link, megabytes, view):
        return flow.send(name, link, megabytes, lambda: hidden.at[view()], lambda: hidden.at[view()], to(link))

    every = pl.ds(0, new_cols)
    same("a+", "x+", block_mb, lambda: (rows_of(0, 0), every))
    same("a-", "x-", block_mb, lambda: (rows_of(0, 0), every))
    same("f+", "x+", block_mb / 2, lambda: (rows_of(0, 3), left_part))
    same("f-", "x-", block_mb / 2, lambda: (rows_of(0, 1), right_part))
    for shift in range(4):
        same(("c", shift), "c", block_mb, lambda shift=shift: (rows_of(0, shift), every))
    flow.task(("h2",), 0.02, None, ("a+", "a-", ("c", 0)), rank=0, after=(("half",),))
    flow.task(("a+",), 0.02, None, ("f+", ("c", 3)), rank=0)
    flow.task(("a-",), 0.02, None, ("f-", ("c", 1)), rank=0)
    flow.task(("f+", "f-"), 0.02, None, (("c", 2),), rank=0)

    def finish_grown():
        for matrix in range(2):
            grown[matrix][...] = grown_sum[matrix].astype(jnp.bfloat16)

    flow.task(
        (), 1.0, finish_grown, rank=7, name=("grown",),
        after=[("grown", (flip, shift), matrix) for flip in (0, 1) for shift in range(4) for matrix in (0, 1)],
    )

    def partials(rel):
        rows = pl.ds(pl.multiple_of(place.dp_at(rel) * per_seq, per_seq), per_seq)
        block = hidden[rows, :]
        values = [jnp.dot(block, grown[matrix][...], preferred_element_type=jnp.float32) for matrix in range(2)]
        sums = None
        for start in range(0, new_cols, 128):
            part = jnp.square(block[:, start:start + 128].astype(jnp.float32))
            sums = part if sums is None else sums + part
        return values + [sums]

    def put_partials(number, rel):
        start = 0
        for value in partials(rel):
            part_out[number, :, start:start + value.shape[1]] = value.astype(jnp.bfloat16)
            start += value.shape[1]

    needs = ["h2", "a+", "a-", "f+", "f-"] + [("c", shift) for shift in range(4)]
    width = part_out.shape[2]
    names = []
    for number, rel in enumerate(DP_PEERS):
        name = flow.send(
            ("P", number), PEER_LINKS[rel], per_seq * width * 2e-6,
            lambda number=number: part_out.at[number], lambda number=number: part_in.at[number],
            lambda rel=rel: (place.dp_at(rel), place.tensor),
        )
        names.append(name)
        flow.task(
            needs, 0.5, lambda number=number, rel=rel: put_partials(number, rel), (name,),
            rank=8, after=(("grown",), ("half",)), name=name,
        )

    def keep_own():
        start = 0
        for value in partials((0, 0)):
            own_part[:, start:start + value.shape[1]] = value
            start += value.shape[1]

    flow.task(needs, 0.5, keep_own, rank=9, name=("own",), after=names)

    def add_up():
        total = own_part[...]
        for number in range(len(DP_PEERS)):
            total = total + part_in[number].astype(jnp.float32)
        square_sum = jnp.sum(total[:, 2 * head_cols:], axis=1, keepdims=True)
        both_ref[...] = total[:, :2 * head_cols] * lax.rsqrt(square_sum / new_width + TOKEN_EPSILON)

    flow.task(names, 1.0, add_up, rank=9, after=(("own",),))
    flow.emit(flow.arrange(LINK_RATES), send_sem, recv_sem)


def exchange_and_check(raw_rows, old_embed, token_ids, inner, expand_in):
    vocab_rows, new_cols = raw_rows.shape
    slab = old_embed.shape[1]
    head_cols = inner.shape[1]
    tokens = token_ids.shape[0]
    padded = -(-vocab_rows // 128) * 128
    per_seq = tokens // N_DP
    width = 2 * head_cols + 128
    anywhere = pl.BlockSpec(memory_space=pl.ANY)
    inside = pl.BlockSpec(memory_space=pltpu.VMEM)
    bf16, f32 = jnp.bfloat16, jnp.float32
    count = 7 * len(INNER_MODES) + 7 + 1 + 4 + 2 + 4 + 4 + 7
    sizes = (expand_in.shape[1], D_NEW)
    return pl.pallas_call(
        lambda *refs: second_kernel(sizes, *refs),
        out_shape=(
            jax.ShapeDtypeStruct((vocab_rows, new_cols), bf16),
            jax.ShapeDtypeStruct((new_cols, head_cols), bf16),
            jax.ShapeDtypeStruct((new_cols, head_cols), bf16),
            jax.ShapeDtypeStruct((per_seq, 2 * head_cols), f32),
        ),
        in_specs=[anywhere, anywhere, inside, anywhere, anywhere],
        out_specs=(inside,) * 4,
        scratch_shapes=[
            pltpu.VMEM((vocab_rows, new_cols), f32),
            pltpu.VMEM((vocab_rows, slab), bf16),
            pltpu.VMEM(expand_in.shape, bf16),
            pltpu.VMEM((N_DP,) + inner.shape, bf16),
            pltpu.VMEM((2, new_cols, head_cols), f32),
            pltpu.VMEM((padded, 128), f32),
            pltpu.VMEM((8, padded), f32),
            pltpu.VMEM((7, 8, padded), f32),
            pltpu.VMEM((padded, new_cols), bf16),
            pltpu.VMEM((tokens, new_cols), bf16),
            pltpu.VMEM((tokens // 2, new_cols), bf16),
            pltpu.VMEM((tokens // 8, new_cols // 2), bf16),
            pltpu.VMEM((tokens // 8, new_cols // 2), bf16),
            pltpu.VMEM((tokens // 8, new_cols), bf16),
            pltpu.VMEM((tokens // 8, new_cols), bf16),
            pltpu.VMEM((tokens // 16, new_cols), bf16),
            pltpu.VMEM((tokens, new_cols), bf16),
            pltpu.VMEM((7, per_seq, width), bf16),
            pltpu.VMEM((7, per_seq, width), bf16),
            pltpu.VMEM((per_seq, width), f32),
            pltpu.SemaphoreType.DMA((count,)),
            pltpu.SemaphoreType.DMA((count,)),
            pltpu.SemaphoreType.DMA((4,)),
        ],
        compiler_params=pltpu.CompilerParams(
            collective_id=2, has_side_effects=True, vmem_limit_bytes=VMEM_LIMIT
        ),
        name="exchange_and_check",
    )(raw_rows, old_embed, token_ids.reshape(tokens, 1), inner, expand_in)


def rotate(values, head_count):
    row_count = values.shape[0]
    shaped = values.reshape(row_count, head_count, HEAD)
    half_size = HEAD // 2
    position = jnp.arange(row_count).astype(jnp.float32)
    frequency = jnp.exp(
        -math.log(10000.0) * jnp.arange(half_size).astype(jnp.float32) * (2.0 / HEAD)
    )
    angles = position[:, None] * frequency[None, :]
    cosine = jnp.cos(angles)[:, None, :]
    sine_table = jnp.sin(angles)[:, None, :]
    first_half = shaped[..., :half_size]
    second = shaped[..., half_size:]
    return jnp.concatenate(
        [first_half * cosine - second * sine_table, second * cosine + first_half * sine_table],
        axis=-1,
    )


def entropy_of(queries, key_proj, head_count):
    rotated_q = rotate(queries, head_count).astype(jnp.bfloat16)
    rotated_k = rotate(key_proj, head_count).astype(jnp.bfloat16)
    scores = jnp.einsum(
        "ihd,jhd->hij", rotated_q, rotated_k, preferred_element_type=jnp.float32
    ) * HEAD ** (-0.5)
    row_count = queries.shape[0]
    causal = jnp.arange(row_count)[:, None] >= jnp.arange(row_count)[None, :]
    weights = jnp.where(causal[None], jnp.exp(scores), 0.0)
    weight_sum = jnp.sum(weights, axis=-1)
    entropy = jnp.log(weight_sum) - jnp.sum(weights * scores, axis=-1) / weight_sum
    return entropy.T


def on_device(token_ids, old_embed, expand_in, query_out, key_out, old_query, old_key):
    head_cols = query_out.shape[0]
    raw_rows, inner = gather_and_grow(old_embed, expand_in, query_out, key_out, old_query, old_key)
    grown_embedding, grown_query, grown_key, both = exchange_and_check(
        raw_rows, old_embed, token_ids, inner, expand_in
    )
    attention_entropy = entropy_of(both[:, :head_cols], both[:, head_cols:], head_cols // HEAD)
    return (grown_embedding, grown_query, grown_key, attention_entropy)


def solution(mesh):
    placed = (
        P(),
        P("tensor", "dp"),
        P("dp", None),
        P("tensor", None),
        P("tensor", None),
        P("dp", "tensor"),
        P("dp", "tensor"),
    )
    return jax.shard_map(
        on_device,
        mesh=mesh,
        in_specs=placed,
        out_specs=(P("tensor", "dp"), P("dp", "tensor"), P("dp", "tensor"), P("dp", "tensor")),
        check_vma=False,
    )
```

```python
import heapq
import math

import jax
import jax.numpy as jnp
from jax import lax
from jax.experimental import pallas as pl
from jax.experimental.pallas import tpu as pltpu
from jax.sharding import PartitionSpec as P

D_NEW = 8192
HEAD = 128
N_DP = 8
N_TENSOR = 16

EMBED_EPSILON = 1e-06
TOKEN_EPSILON = 1e-05

MESH = pl.DeviceIdType.MESH
LAST = (((1,), (1,)), ((), ()))
VMEM_LIMIT = 67_000_000

STEP = {"y+": 1, "y-": -1, "x+": 1, "x-": -1}


class Place:
    def __init__(self):
        self.dp = lax.axis_index("dp")
        self.tensor = lax.axis_index("tensor")
        self.z_lo = self.dp // 4
        self.y = self.dp % 4
        self.x = self.tensor // 4
        self.z_hi = (self.tensor // 2) % 2
        self.core = self.tensor % 2

    def dp_at(self, rel):
        flip, shift = rel
        z_lo = 1 - self.z_lo if flip else self.z_lo
        return z_lo * 4 + (self.y + shift + 4) % 4

    def tensor_at(self, rel):
        flip, shift, core_flip = rel
        z_hi = 1 - self.z_hi if flip else self.z_hi
        core = 1 - self.core if core_flip else self.core
        return (((self.x + shift + 4) % 4) * 2 + z_hi) * 2 + core

    def across(self, link):
        if link in ("y+", "y-"):
            return (self.dp_at((0, STEP[link])), self.tensor)
        if link == "z":
            return (self.dp_at((1, 0)), self.tensor)
        if link in ("x+", "x-"):
            return (self.dp, self.tensor_at((0, STEP[link], 0)))
        if link == "h":
            return (self.dp, self.tensor_at((1, 0, 0)))
        return (self.dp, self.tensor_at((0, 0, 1)))


def seen_by_receiver(link, rel):
    if link in ("y+", "y-"):
        return (rel[0], (rel[1] - STEP[link]) % 4)
    if link == "z":
        return (1 - rel[0], rel[1])
    if link in ("x+", "x-"):
        return (rel[0], (rel[1] - STEP[link]) % 4, rel[2])
    if link == "h":
        return (1 - rel[0], rel[1], rel[2])
    return (rel[0], rel[1], 1 - rel[2])


def ring_tree(plus, minus, kind, rel, chunk, extra):
    near = (rel[0], (rel[1] - STEP[extra]) % 4) + tuple(rel[2:])
    return [(plus, kind, rel, chunk), (minus, kind, rel, chunk), (extra, kind, near, chunk)]


def gather_dp(kind, chunk, z_first, extra):
    other = "y-" if extra == "y+" else "y+"
    if z_first:
        sends = [("z", kind, (0, 0), chunk)]
        sends += ring_tree("y+", "y-", kind, (0, 0), chunk, extra)
        sends += ring_tree("y+", "y-", kind, (1, 0), chunk, other)
        return sends
    sends = ring_tree("y+", "y-", kind, (0, 0), chunk, extra)
    return sends + [("z", kind, (0, shift), chunk) for shift in (0, 1, 3, 2)]


def gather_tensor(kind, chunk, extra):
    other = "x-" if extra == "x+" else "x+"
    sends = [("h", kind, (0, 0, 0), chunk)]
    sends += ring_tree("x+", "x-", kind, (0, 0, 0), chunk, extra)
    sends += ring_tree("x+", "x-", kind, (1, 0, 0), chunk, other)
    sends += [("c", kind, (flip, shift, 0), chunk) for flip in (0, 1) for shift in (0, 1, 3, 2)]
    return sends


def row_cuts(rows, pieces):
    step = -(-rows // (16 * pieces)) * 16
    return [(start, min(step, rows - start)) for start in range(0, rows, step)]


class Flow:
    def __init__(self):
        self.sends = {}
        self.tasks = []
        self.left_already = set()

    def send(self, name, link, priority, megabytes, source, target, to):
        assert name not in self.sends
        self.sends[name] = (link, priority, megabytes, source, target, to)
        return name

    def task(self, needs, cost, run, sends=(), rank=5, after=(), name=None):
        self.tasks.append((frozenset(needs), cost, run, tuple(sends), rank, frozenset(after), name))

    def arrange(self):
        free, flying, queues = {}, {}, {}
        landed, done, order, heap = set(), set(), [], []
        left = list(range(len(self.tasks)))
        now, serial = 0.0, 0

        def pump(link):
            while queues.get(link) and flying.get(link, 0) < DEPTH.get(link, 1000):
                name = heapq.heappop(queues[link])[2]
                flying[link] = flying.get(link, 0) + 1
                free[link] = max(free.get(link, 0.0), now) + self.sends[name][2] / LINK_RATES[link]
                heapq.heappush(heap, (free[link] + 1.5, len(order), name))
                order.append(("start", name))

        while left or heap:
            if heap and heap[0][0] <= now:
                name = heapq.heappop(heap)[2]
                link = self.sends[name][0]
                landed.add(name)
                flying[link] -= 1
                order.append(("arrive", name))
                now += 0.03
                for number in list(left):
                    needs, cost, run, sends, rank, after, _ = self.tasks[number]
                    if rank == 0 and name in needs and needs <= landed and after <= done:
                        left.remove(number)
                        for send in sends:
                            serial += 1
                            put = (self.sends[send][1], serial, send)
                            heapq.heappush(queues.setdefault(self.sends[send][0], []), put)
                for other in sorted(queues):
                    pump(other)
                continue
            ready = []
            for number in left:
                needs, _, _, _, rank, after, _ = self.tasks[number]
                if after <= done and needs <= landed:
                    ready.append((rank, number))
            if not ready:
                assert heap
                now = max(now, heap[0][0])
                continue
            number = min(ready)[1]
            left.remove(number)
            order.append(("run", number))
            _, cost, _, sends, _, _, name = self.tasks[number]
            now += cost
            if name is not None:
                done.add(name)
            for send in sends:
                serial += 1
                put = (self.sends[send][1], serial, send)
                heapq.heappush(queues.setdefault(self.sends[send][0], []), put)
            for other in sorted(queues):
                pump(other)
        self.length = now
        assert not any(queues.values())
        return order

    def copy_of(self, name):
        _, _, _, source, target, to = self.sends[name]
        number = self.number_of[name]
        return pltpu.make_async_remote_copy(
            src_ref=source(),
            dst_ref=target(),
            send_sem=self.send_sem.at[number],
            recv_sem=self.recv_sem.at[number],
            device_id=to(),
            device_id_type=MESH,
        )

    def wait_left(self, names):
        for name in names:
            if name not in self.left_already:
                self.left_already.add(name)
                self.copy_of(name).wait_send()

    def emit(self, order, send_sem, recv_sem):
        self.number_of = {name: number for number, name in enumerate(self.sends)}
        self.send_sem, self.recv_sem = send_sem, recv_sem
        arrived, started = set(), set()
        for what, which in order:
            if what == "arrive":
                self.copy_of(which).wait_recv()
                arrived.add(which)
            elif what == "start":
                self.copy_of(which).start()
                started.add(which)
            elif self.tasks[which][2] is not None:
                self.tasks[which][2]()
        assert arrived == set(self.sends) and started == set(self.sends)
        self.wait_left(list(self.sends))


DEPTH = {"y+": 3, "y-": 3, "z": 3, "x+": 3, "x-": 3, "h": 3}
LINK_RATES = {
    "y+": 0.0465, "y-": 0.0465, "z": 0.0465, "x+": 0.0465, "x-": 0.0465, "h": 0.0465, "c": 0.3, "far": 0.03,
}
DP_PEERS = ((1, 2), (0, 2), (1, 1), (1, 3), (1, 0), (0, 1), (0, 3))
X_CUTS = 7
X_MODES = ((False, "y+"), (False, "y-"), (True, "y+"), (True, "y-"), (True, "y+"), (True, "y-"), (True, "y+"))
INNER_MODES = ((True, "y+"), (False, "y-"), (True, "y-"), (False, "y+"))
RELS = [(flip, shift) for flip in (0, 1) for shift in (0, 1, 3, 2)]
TILE = 256


def slot_of(rel):
    return rel[0] * 4 + rel[1] - 1


def aligned(start, size):
    return pl.ds(pl.multiple_of(start, size), size)


def whole_kernel(
    sizes, x_ref, w_ref, e_ref, q_ref, k_ref, tokens_ref,
    ge_ref, gq_ref, gk_ref, both_ref,
    x_pad, x_all, raw, w_all, e_all, o_all, total, inner_own, inner_all, grown_sum,
    lanes, squares, squares_in,
    masked, core_in, left_in, right_in, left_block, right_block, half_in, chosen_all, chosen_sum, hidden,
    q_out, q_in, k_out, k_in, own_part,
    send_sem, recv_sem, local_sem,
):
    place = Place()
    vocab_rows, slab = x_ref.shape
    new_cols, old_width = e_ref.shape
    new_width = sizes
    head_cols = q_ref.shape[0]
    token_rows = tokens_ref.shape[0]
    out_slab, in_slab = w_ref.shape[1:]
    grown = (gq_ref, gk_ref)
    per_seq = both_ref.shape[0]
    cuts = row_cuts(vocab_rows, X_CUTS)
    assert len(cuts) == X_CUTS

    barrier = pltpu.get_barrier_semaphore()
    friends = [place.across(link) for link in ("x+", "x-", "h", "c")]
    friends += [(place.dp_at(rel), place.tensor) for rel in DP_PEERS]
    for friend in friends:
        pl.semaphore_signal(barrier, inc=1, device_id=friend, device_id_type=MESH)
    local = [
        pltpu.make_async_copy(x_ref, x_pad.at[pl.ds(0, vocab_rows), :], local_sem.at[0]),
        pltpu.make_async_copy(w_ref.at[0], w_all.at[0, place.tensor], local_sem.at[1]),
        pltpu.make_async_copy(w_ref.at[1], w_all.at[1, place.tensor], local_sem.at[2]),
        pltpu.make_async_copy(q_ref, o_all.at[0], local_sem.at[3]),
        pltpu.make_async_copy(e_ref, e_all, local_sem.at[4]),
        pltpu.make_async_copy(k_ref, o_all.at[1], local_sem.at[5]),
    ]
    for copy in local:
        copy.start()
    pl.semaphore_wait(barrier, len(friends))

    flow = Flow()

    def gather(kind, sends, megabytes, priority, source, target, ready):
        brought = {}
        for link, _, rel, chunk in sends:
            brought[(seen_by_receiver(link, rel), chunk)] = (kind, link, rel, chunk)
        first, after = {}, {}
        for link, _, rel, chunk in sends:
            name = flow.send(
                (kind, link, rel, chunk), link, priority(link, chunk), megabytes(chunk),
                lambda rel=rel, chunk=chunk: source(rel, chunk),
                lambda link=link, rel=rel, chunk=chunk: target(seen_by_receiver(link, rel), rel, chunk),
                lambda link=link: place.across(link),
            )
            if (rel, chunk) in brought:
                after.setdefault(brought[(rel, chunk)], []).append(name)
            else:
                assert not any(rel)
                first.setdefault(ready(chunk), []).append(name)
        for cause, names in first.items():
            flow.task((), 0.05, None, names, rank=0.5, after=cause)
        for cause, names in after.items():
            flow.task((cause,), 0.0, None, names, rank=0)
        return brought

    sends = []
    for matrix in range(2):
        sends += gather_tensor("W", matrix, ("x+", "x-")[matrix])

    def w_source(rel, matrix):
        return w_ref.at[matrix] if not any(rel) else w_all.at[matrix, place.tensor_at(rel)]

    w_from = gather(
        "W", sends, lambda matrix: out_slab * in_slab * 2e-6, lambda link, matrix: 1 + matrix,
        w_source, lambda _, rel, matrix: w_all.at[matrix, place.tensor_at(rel)], lambda matrix: (),
    )

    sends = []
    for chunk, (z_first, extra) in enumerate(X_MODES):
        sends += gather_dp("X", chunk, z_first, extra)

    def x_source(rel, chunk):
        rows = pl.ds(*cuts[chunk])
        return x_ref.at[rows, :] if not any(rel) else x_all.at[slot_of(rel), rows, :]

    x_from = gather(
        "X", sends, lambda chunk: cuts[chunk][1] * slab * 2e-6,
        lambda link, chunk: 10 + (link == "z" and not X_MODES[chunk][0]),
        x_source, lambda there, rel, chunk: x_all.at[slot_of(there), pl.ds(*cuts[chunk]), :], lambda chunk: (),
    )

    pair = 2 * out_slab

    def add_inner(rel, matrix, fresh, last):
        chip = place.tensor_at((rel[0], rel[1], 0)) // 2
        slabs = w_all[matrix, pl.ds(chip * 2, 2)].reshape(pair, in_slab)
        part = jnp.dot(o_all[matrix, :, aligned(chip * pair, pair)], slabs, preferred_element_type=jnp.float32)
        if not fresh:
            part = part + total[matrix]
        if last:
            inner_own[matrix] = part.astype(jnp.bfloat16)
        else:
            total[matrix] = part

    counts = {}

    def counted(key, times, run):
        def go():
            counts[key] = counts.get(key, 0) + 1
            run(counts[key] == 1, counts[key] == times)

        return go

    flow.task((), 0.3, lambda: [local[number].wait() for number in (1, 2, 3, 5)], rank=2, name=("w",))
    for matrix in range(2):
        units = []
        for rel in RELS:
            needs = [w_from[(rel + (core,), matrix)] for core in (0, 1) if any(rel) or core]
            units.append(("inner", rel, matrix))
            run = counted(
                ("inner", matrix), len(RELS),
                lambda fresh, last, rel=rel, matrix=matrix: add_inner(rel, matrix, fresh, last),
            )
            flow.task(needs, 0.6, run, rank=2 + matrix, after=(("w",),), name=units[-1])
        flow.task((), 0.0, None, rank=2, after=units, name=("inner", matrix))

    tiles = new_cols // TILE

    def e_columns(rel):
        return pl.ds(pl.multiple_of(place.dp_at(rel) * slab, 128), slab)

    def add_raw(rel, half, fresh):
        columns = e_columns(rel)

        def body(number, _):
            rows = aligned(number * TILE, TILE)
            block = x_all[slot_of(rel)] if any(rel) else x_pad[pl.ds(0, vocab_rows), :]
            part = lax.dot_general(block, e_all[rows, columns], LAST, preferred_element_type=jnp.float32)
            if fresh:
                raw[:, rows] = part
            else:
                raw[:, rows] += part
            return 0

        lax.fori_loop(half * tiles // 2, (half + 1) * tiles // 2, body, 0)

    raw_units = []
    for rel in RELS:
        for half in range(2):
            needs = [x_from[(rel, chunk)] for chunk in range(X_CUTS)] if any(rel) else []
            run = counted(
                ("raw", half), len(RELS), lambda fresh, last, rel=rel, half=half: add_raw(rel, half, fresh)
            )
            raw_units.append(("raw", rel, half))
            flow.task(needs, 1.3, run, rank=6, after=(("e",),), name=raw_units[-1])

    core_rows, chip_rows, own_rows = token_rows // 2, token_rows // 8, token_rows // 16
    mine = place.core * core_rows
    theirs = (1 - place.core) * core_rows

    def rows_of(core, shift, part=None):
        start = (1 - place.core if core else place.core) * core_rows + ((place.x + shift + 4) % 4) * chip_rows
        if part is None:
            return aligned(start, chip_rows)
        return aligned(start + part * own_rows, own_rows)

    def small_rows(flip):
        z_hi = 1 - place.z_hi if flip else place.z_hi
        return aligned(mine + place.x * chip_rows + z_hi * own_rows, own_rows)

    def lane_sums(values_ref, rows):
        sums = None
        for start in range(0, values_ref.shape[1], 128):
            part = jnp.square(values_ref[pl.ds(0, rows), start:start + 128].astype(jnp.float32))
            sums = part if sums is None else sums + part
        return sums

    def row_sums(values_ref):
        lanes[pl.ds(lanes.shape[0] - 32, 32), :] = jnp.zeros((32, 128), jnp.float32)
        lanes[pl.ds(0, vocab_rows), :] = lane_sums(values_ref, vocab_rows)
        return jnp.broadcast_to(jnp.sum(lanes[...].T, axis=0, keepdims=True), squares.shape)

    def load_x():
        local[0].wait()
        end = pl.ds(x_pad.shape[0] - 32, 32)
        row = lax.broadcasted_iota(jnp.int32, (32, slab), 0) + (x_pad.shape[0] - 32)
        x_pad[end, :] = jnp.where(row < vocab_rows, x_pad[end, :].astype(jnp.float32), 0.0).astype(jnp.bfloat16)

    def choose(start):
        def body(number, _):
            rows = aligned(start + number * TILE, TILE)
            ids = tokens_ref[rows, :] - place.tensor * vocab_rows
            column = lax.broadcasted_iota(jnp.int32, (TILE, x_pad.shape[0]), 1)
            one = jnp.where((ids == column) & (column < vocab_rows), 1.0, 0.0).astype(jnp.bfloat16)
            masked[rows, :] = jnp.dot(one, x_pad[...], preferred_element_type=jnp.float32).astype(jnp.bfloat16)
            return 0

        lax.fori_loop(0, core_rows // TILE, body, 0)

    def to(link):
        return lambda: place.across(link)

    core_mb = core_rows * slab * 2e-6
    block_mb = core_mb / 4
    flow.send("c1", "c", 0, core_mb, lambda: masked.at[aligned(theirs, core_rows), :], lambda: core_in, to("c"))
    flow.task((), 1.0, load_x, rank=1, name=("x",))
    flow.task((), 1.2, lambda: choose(theirs), ("c1",), rank=1, name=("theirs",), after=(("x",),))
    flow.task((), 1.2, lambda: choose(mine), rank=1, name=("mine",), after=(("theirs",),))

    def add_core():
        rows = aligned(mine, core_rows)
        masked[rows, :] += core_in[...]

    flow.send("r+", "x+", 0, block_mb / 2, lambda: masked.at[rows_of(0, 2, 0), :], lambda: left_in, to("x+"))
    flow.send("r-", "x-", 0, block_mb / 2, lambda: masked.at[rows_of(0, 2, 1), :], lambda: right_in, to("x-"))
    flow.task(("c1",), 0.5, add_core, ("r+", "r-"), rank=1, name=("core",), after=(("mine",),))

    def add_left():
        masked[rows_of(0, 1, 0), :] += left_in[...]

    def add_right():
        masked[rows_of(0, 3, 1), :] += right_in[...]

    flow.send("b+", "x+", 0, block_mb, lambda: masked.at[rows_of(0, 1), :], lambda: left_block, to("x+"))
    flow.send("b-", "x-", 0, block_mb, lambda: masked.at[rows_of(0, 3), :], lambda: right_block, to("x-"))
    flow.task(("r+",), 0.1, add_left, ("b+",), rank=1, after=(("core",),))
    flow.task(("r-",), 0.1, add_right, ("b-",), rank=1, after=(("core",),))

    def add_blocks():
        masked[rows_of(0, 0), :] += left_block[...] + right_block[...]

    flow.send("h1", "h", 0, block_mb / 2, lambda: masked.at[small_rows(1), :], lambda: half_in, to("h"))
    flow.task(("b+", "b-"), 0.2, add_blocks, ("h1",), rank=1, name=("blocks",), after=(("core",),))

    def add_half():
        chosen_all[0] = masked[small_rows(0), :] + half_in[...]

    flow.task(("h1",), 0.1, add_half, rank=1, name=("chosen",), after=(("blocks",),))
    t_from = gather(
        "T", gather_dp("T", 0, True, "y+"), lambda chunk: own_rows * slab * 2e-6, lambda link, chunk: 0,
        lambda rel, chunk: chosen_all.at[slot_of(rel) + 1], lambda there, rel, chunk: chosen_all.at[slot_of(there) + 1],
        lambda chunk: (("chosen",),),
    )

    def grow_chosen(rel, fresh, last):
        at = slot_of(rel) + 1
        columns = e_columns(rel)

        def body(number, _):
            rows = aligned(number * TILE, TILE)
            part = lax.dot_general(
                chosen_all[at], e_all[rows, columns], LAST, preferred_element_type=jnp.float32
            )
            if fresh:
                chosen_sum[:, rows] = part
            else:
                chosen_sum[:, rows] += part
            return 0

        lax.fori_loop(0, tiles, body, 0)
        if last:
            old_squares = None
            for number in range(N_DP):
                for start in range(0, slab, 128):
                    part = jnp.square(chosen_all[number, :, start:start + 128].astype(jnp.float32))
                    old_squares = part if old_squares is None else old_squares + part
            hidden[small_rows(0), pl.ds(0, new_cols)] = chosen_sum[...].astype(jnp.bfloat16)
            hidden[small_rows(0), pl.ds(new_cols, 128)] = old_squares.astype(jnp.bfloat16)

    units = []
    flow.task((), 0.1, lambda: local[4].wait(), rank=4, name=("e",))
    for rel in RELS:
        needs = [t_from[(rel, 0)]] if any(rel) else []
        run = counted("chosen", len(RELS), lambda fresh, last, rel=rel: grow_chosen(rel, fresh, last))
        units.append(("chosen", rel))
        flow.task(needs, 0.9, run, rank=1.5, after=(("e",), ("chosen",)), name=units[-1])

    own_mb = own_rows * hidden.shape[1] * 2e-6

    def same(name, link, megabytes, rows):
        return flow.send(
            name, link, 0, megabytes, lambda: hidden.at[rows(), :], lambda: hidden.at[rows(), :], to(link)
        )

    same("h2", "h", own_mb, lambda: small_rows(0))
    same("a+", "x+", 2 * own_mb, lambda: rows_of(0, 0))
    same("a-", "x-", 2 * own_mb, lambda: rows_of(0, 0))
    same("f+", "x+", own_mb, lambda: rows_of(0, 3, 0))
    same("f-", "x-", own_mb, lambda: rows_of(0, 1, 1))
    for shift in range(4):
        same(("c", shift), "c", 2 * own_mb, lambda shift=shift: rows_of(0, shift))
    flow.task((), 0.0, None, ("h2",), rank=0.5, after=units, name=("hidden",))
    flow.task(("h2",), 0.02, None, ("a+", "a-", ("c", 0)), rank=0.5, after=(("hidden",),))
    flow.task(("a+",), 0.0, None, ("f+", ("c", 3)), rank=0)
    flow.task(("a-",), 0.0, None, ("f-", ("c", 1)), rank=0)
    flow.task(("f+", "f-"), 0.0, None, (("c", 2),), rank=0)

    half = head_cols // 2
    sends = []
    for chunk, (z_first, extra) in enumerate(INNER_MODES):
        sends += gather_dp("I", chunk, z_first, extra)

    def inner_view(ref, chunk):
        return ref.at[chunk // 2, pl.ds((chunk % 2) * half, half), :]

    def i_source(rel, chunk):
        return inner_view(inner_all.at[slot_of(rel)] if any(rel) else inner_own, chunk)

    i_from = gather(
        "I", sends, lambda chunk: half * in_slab * 2e-6, lambda link, chunk: 3 + chunk // 2,
        i_source, lambda there, rel, chunk: inner_view(inner_all.at[slot_of(there)], chunk),
        lambda chunk: (("inner", chunk // 2),),
    )

    def add_grown(rel, matrix, fresh, last):
        columns = e_columns(rel)

        def body(number, _):
            rows = aligned(number * TILE, TILE)
            block = inner_all[slot_of(rel), matrix] if any(rel) else inner_own[matrix]
            part = lax.dot_general(e_all[rows, columns], block, LAST, preferred_element_type=jnp.float32)
            if not fresh:
                part = part + grown_sum[matrix, rows, :]
            if last:
                grown[matrix][rows, :] = part.astype(jnp.bfloat16)
            else:
                grown_sum[matrix, rows, :] = part
            return 0

        lax.fori_loop(0, tiles, body, 0)

    for matrix in range(2):
        units = []
        for rel in RELS:
            needs = [i_from[(rel, chunk)] for chunk in (2 * matrix, 2 * matrix + 1)] if any(rel) else []
            run = counted(
                ("grown", matrix), len(RELS),
                lambda fresh, last, rel=rel, matrix=matrix: add_grown(rel, matrix, fresh, last),
            )
            units.append(("grown", rel, matrix))
            flow.task(needs, 0.9, run, rank=3, after=(("e",), ("inner", matrix)), name=units[-1])
        flow.task((), 0.0, None, rank=3, after=units, name=("grown", matrix))

    def square_rows():
        row = lax.broadcasted_iota(jnp.int32, squares.shape, 0)
        squares[...] = jnp.where(row == 1, row_sums(x_pad), 0.0)
        squares[...] = jnp.where(row == 0, row_sums(raw), squares[...])

    square_sends = [
        flow.send(
            ("S", number), "far", 0, 0.03, lambda: squares, lambda number=number: squares_in.at[number],
            lambda rel=rel: (place.dp_at(rel), place.tensor),
        )
        for number, rel in enumerate(DP_PEERS)
    ]
    flow.task((), 2.5, square_rows, square_sends, rank=4, after=raw_units, name=("squares",))
    ge_cuts = ((0, slab, slot_of((1, 2))), (slab, new_cols - slab, slot_of((0, 2))))

    def ge_copies():
        return [
            pltpu.make_async_copy(
                x_all.at[slot, :, pl.ds(0, size)], ge_ref.at[:, pl.ds(start, size)], local_sem.at[6 + number]
            )
            for number, (start, size, slot) in enumerate(ge_cuts)
        ]

    def rescale():
        flow.wait_left([name for name in flow.sends if name[0] == "X"])
        sums = squares[...]
        for number in range(len(DP_PEERS)):
            sums = sums + squares_in[number]
        factor = jnp.sqrt((sums[1:2] / old_width + EMBED_EPSILON) / (sums[0:1] / new_width + EMBED_EPSILON))
        column = jnp.broadcast_to(factor, (128, factor.shape[1])).T[:vocab_rows]
        for start, size, slot in ge_cuts:
            for at in range(0, size, 128):
                scaled = raw[:, start + at:start + at + 128] * column
                x_all[slot, :, at:at + 128] = scaled.astype(jnp.bfloat16)
        for copy in ge_copies():
            copy.start()

    flow.task(square_sends, 2.5, rescale, rank=5, name=("scaled",), after=(("squares",),))

    def seq_rows(rel):
        return aligned(place.dp_at(rel) * per_seq, per_seq)

    def partial(rel, matrix):
        block = hidden[seq_rows(rel), pl.ds(0, new_cols)]
        return jnp.dot(block, grown[matrix][...], preferred_element_type=jnp.float32)

    def lane_squares_of(rel):
        sums = None
        for start in range(0, new_cols, 128):
            part = jnp.square(hidden[seq_rows(rel), start:start + 128].astype(jnp.float32))
            sums = part if sums is None else sums + part
        return sums

    def put_query(number, rel):
        q_out[number, :, :head_cols] = partial(rel, 0).astype(jnp.bfloat16)
        q_out[number, :, head_cols:] = lane_squares_of(rel).astype(jnp.bfloat16)

    def put_key(number, rel):
        k_out[number] = partial(rel, 1).astype(jnp.bfloat16)

    gathered = ["h2", "a+", "a-", "f+", "f-"] + [("c", shift) for shift in range(4)]
    arrivals = []
    for matrix, (put, out, into) in enumerate(((put_query, q_out, q_in), (put_key, k_out, k_in))):
        for number, rel in enumerate(DP_PEERS):
            name = flow.send(
                ("P", matrix, number), "far", 0, 0.1,
                lambda out=out, number=number: out.at[number], lambda into=into, number=number: into.at[number],
                lambda rel=rel: (place.dp_at(rel), place.tensor),
            )
            arrivals.append(name)
            flow.task(
                gathered, 0.4, lambda put=put, number=number, rel=rel: put(number, rel), (name,),
                rank=2.5, after=(("grown", matrix), ("hidden",)),
            )

    def keep_own(matrix):
        own_part[:, matrix * head_cols:(matrix + 1) * head_cols] = partial((0, 0), matrix)
        if matrix == 0:
            own_part[:, 2 * head_cols:] = lane_squares_of((0, 0))

    for matrix in range(2):
        flow.task(
            gathered, 0.4, lambda matrix=matrix: keep_own(matrix), rank=3.5,
            after=(("grown", matrix), ("hidden",)), name=("own", matrix),
        )

    def add_up():
        queries = own_part[:, :head_cols]
        keys = own_part[:, head_cols:2 * head_cols]
        square_lanes = own_part[:, 2 * head_cols:]
        for number in range(len(DP_PEERS)):
            queries = queries + q_in[number, :, :head_cols].astype(jnp.float32)
            square_lanes = square_lanes + q_in[number, :, head_cols:].astype(jnp.float32)
            keys = keys + k_in[number].astype(jnp.float32)
        raw_ms = jnp.sum(square_lanes, axis=1, keepdims=True) / new_width
        old_lanes = hidden[seq_rows((0, 0)), pl.ds(new_cols, 128)].astype(jnp.float32)
        old_ms = jnp.sum(old_lanes, axis=1, keepdims=True) / old_width
        factor = jnp.sqrt((old_ms + EMBED_EPSILON) / (raw_ms + EMBED_EPSILON))
        scale = factor * lax.rsqrt(factor * factor * raw_ms + TOKEN_EPSILON)
        both_ref[:, :head_cols] = queries * scale
        both_ref[:, head_cols:] = keys * scale

    flow.task(arrivals, 1.0, add_up, rank=9, after=(("own", 0), ("own", 1)))
    order = flow.arrange()
    flow.emit(order, send_sem, recv_sem)
    for copy in ge_copies():
        copy.wait()


def grow_and_check(token_ids, old_embed, expand_in, query_out, key_out, old_query, old_key):
    vocab_rows, slab = old_embed.shape
    in_slab, out_slab = old_query.shape
    new_cols = expand_in.shape[0]
    head_cols = query_out.shape[0]
    tokens = token_ids.shape[0]
    padded = -(-vocab_rows // 128) * 128
    per_seq = tokens // N_DP
    turned = jnp.stack([old_query.T, old_key.T])
    anywhere = pl.BlockSpec(memory_space=pl.ANY)
    inside = pl.BlockSpec(memory_space=pltpu.VMEM)
    bf16, f32 = jnp.bfloat16, jnp.float32
    count = (2 * 15) + 7 * X_CUTS + 7 * len(INNER_MODES) + 7 + 1 + 4 + 1 + 9 + 7 + 14
    return pl.pallas_call(
        lambda *refs: whole_kernel(D_NEW, *refs),
        out_shape=(
            jax.ShapeDtypeStruct((vocab_rows, new_cols), bf16),
            jax.ShapeDtypeStruct((new_cols, head_cols), bf16),
            jax.ShapeDtypeStruct((new_cols, head_cols), bf16),
            jax.ShapeDtypeStruct((per_seq, 2 * head_cols), f32),
        ),
        in_specs=[anywhere] * 5 + [inside],
        out_specs=(anywhere, inside, inside, inside),
        scratch_shapes=[
            pltpu.VMEM((padded, slab), bf16),
            pltpu.VMEM((N_DP - 1, vocab_rows, slab), bf16),
            pltpu.VMEM((vocab_rows, new_cols), f32),
            pltpu.VMEM((2, N_TENSOR, out_slab, in_slab), bf16),
            pltpu.VMEM(expand_in.shape, bf16),
            pltpu.VMEM((2,) + query_out.shape, bf16),
            pltpu.VMEM((2, head_cols, in_slab), f32),
            pltpu.VMEM((2, head_cols, in_slab), bf16),
            pltpu.VMEM((N_DP - 1, 2, head_cols, in_slab), bf16),
            pltpu.VMEM((2, new_cols, head_cols), f32),
            pltpu.VMEM((padded, 128), f32),
            pltpu.VMEM((8, padded), f32),
            pltpu.VMEM((7, 8, padded), f32),
            pltpu.VMEM((tokens, slab), bf16),
            pltpu.VMEM((tokens // 2, slab), bf16),
            pltpu.VMEM((tokens // 16, slab), bf16),
            pltpu.VMEM((tokens // 16, slab), bf16),
            pltpu.VMEM((tokens // 8, slab), bf16),
            pltpu.VMEM((tokens // 8, slab), bf16),
            pltpu.VMEM((tokens // 16, slab), bf16),
            pltpu.VMEM((N_DP, tokens // 16, slab), bf16),
            pltpu.VMEM((tokens // 16, new_cols), f32),
            pltpu.VMEM((tokens, new_cols + 128), bf16),
            pltpu.VMEM((7, per_seq, head_cols + 128), bf16),
            pltpu.VMEM((7, per_seq, head_cols + 128), bf16),
            pltpu.VMEM((7, per_seq, head_cols), bf16),
            pltpu.VMEM((7, per_seq, head_cols), bf16),
            pltpu.VMEM((per_seq, 2 * head_cols + 128), f32),
            pltpu.SemaphoreType.DMA((count,)),
            pltpu.SemaphoreType.DMA((count,)),
            pltpu.SemaphoreType.DMA((8,)),
        ],
        compiler_params=pltpu.CompilerParams(
            collective_id=1, has_side_effects=True, vmem_limit_bytes=VMEM_LIMIT
        ),
        name="grow_and_check",
    )(old_embed, turned, expand_in, query_out, key_out, token_ids.reshape(tokens, 1))


def rotate(values, head_count):
    row_count = values.shape[0]
    shaped = values.reshape(row_count, head_count, HEAD)
    half_size = HEAD // 2
    position = jnp.arange(row_count).astype(jnp.float32)
    frequency = jnp.exp(
        -math.log(10000.0) * jnp.arange(half_size).astype(jnp.float32) * (2.0 / HEAD)
    )
    angles = position[:, None] * frequency[None, :]
    cosine = jnp.cos(angles)[:, None, :]
    sine_table = jnp.sin(angles)[:, None, :]
    first_half = shaped[..., :half_size]
    second = shaped[..., half_size:]
    return jnp.concatenate(
        [first_half * cosine - second * sine_table, second * cosine + first_half * sine_table],
        axis=-1,
    )


def entropy_of(queries, key_proj, head_count):
    rotated_q = rotate(queries, head_count).astype(jnp.bfloat16)
    rotated_k = rotate(key_proj, head_count).astype(jnp.bfloat16)
    scores = jnp.einsum(
        "ihd,jhd->hij", rotated_q, rotated_k, preferred_element_type=jnp.float32
    ) * HEAD ** (-0.5)
    row_count = queries.shape[0]
    causal = jnp.arange(row_count)[:, None] >= jnp.arange(row_count)[None, :]
    weights = jnp.where(causal[None], jnp.exp(scores), 0.0)
    weight_sum = jnp.sum(weights, axis=-1)
    entropy = jnp.log(weight_sum) - jnp.sum(weights * scores, axis=-1) / weight_sum
    return entropy.T


def on_device(token_ids, old_embed, expand_in, query_out, key_out, old_query, old_key):
    head_cols = query_out.shape[0]
    grown_embedding, grown_query, grown_key, both = grow_and_check(
        token_ids, old_embed, expand_in, query_out, key_out, old_query, old_key
    )
    attention_entropy = entropy_of(both[:, :head_cols], both[:, head_cols:], head_cols // HEAD)
    return (grown_embedding, grown_query, grown_key, attention_entropy)


def solution(mesh):
    placed = (
        P(),
        P("tensor", "dp"),
        P("dp", None),
        P("tensor", None),
        P("tensor", None),
        P("dp", "tensor"),
        P("dp", "tensor"),
    )
    return jax.shard_map(
        on_device,
        mesh=mesh,
        in_specs=placed,
        out_specs=(P("tensor", "dp"), P("dp", "tensor"), P("dp", "tensor"), P("dp", "tensor")),
        check_vma=False,
    )
```

```python
import heapq
import math

import jax
import jax.numpy as jnp
from jax import lax
from jax.experimental import pallas as pl
from jax.experimental.pallas import tpu as pltpu
from jax.sharding import PartitionSpec as P

D_NEW = 8192
HEAD = 128
N_DP = 8
N_TENSOR = 16

EMBED_EPSILON = 1e-06
TOKEN_EPSILON = 1e-05

MESH = pl.DeviceIdType.MESH
LAST = (((1,), (1,)), ((), ()))
VMEM_LIMIT = 67_000_000

STEP = {"y+": 1, "y-": -1, "x+": 1, "x-": -1}


class Place:
    def __init__(self):
        self.dp = lax.axis_index("dp")
        self.tensor = lax.axis_index("tensor")
        self.z_lo = self.dp // 4
        self.y = self.dp % 4
        self.x = self.tensor // 4
        self.z_hi = (self.tensor // 2) % 2
        self.core = self.tensor % 2

    def dp_at(self, rel):
        flip, shift = rel
        z_lo = 1 - self.z_lo if flip else self.z_lo
        return z_lo * 4 + (self.y + shift + 4) % 4

    def tensor_at(self, rel):
        flip, shift, core_flip = rel
        z_hi = 1 - self.z_hi if flip else self.z_hi
        core = 1 - self.core if core_flip else self.core
        return (((self.x + shift + 4) % 4) * 2 + z_hi) * 2 + core

    def across(self, link):
        if link in ("y+", "y-"):
            return (self.dp_at((0, STEP[link])), self.tensor)
        if link == "z":
            return (self.dp_at((1, 0)), self.tensor)
        if link in ("x+", "x-"):
            return (self.dp, self.tensor_at((0, STEP[link], 0)))
        if link == "h":
            return (self.dp, self.tensor_at((1, 0, 0)))
        return (self.dp, self.tensor_at((0, 0, 1)))


def seen_by_receiver(link, rel):
    if link in ("y+", "y-"):
        return (rel[0], (rel[1] - STEP[link]) % 4)
    if link == "z":
        return (1 - rel[0], rel[1])
    if link in ("x+", "x-"):
        return (rel[0], (rel[1] - STEP[link]) % 4, rel[2])
    if link == "h":
        return (1 - rel[0], rel[1], rel[2])
    return (rel[0], rel[1], 1 - rel[2])


def ring_tree(plus, minus, kind, rel, chunk, extra):
    near = (rel[0], (rel[1] - STEP[extra]) % 4) + tuple(rel[2:])
    return [(plus, kind, rel, chunk), (minus, kind, rel, chunk), (extra, kind, near, chunk)]


def gather_dp(kind, chunk, z_first, extra):
    other = "y-" if extra == "y+" else "y+"
    if z_first:
        sends = [("z", kind, (0, 0), chunk)]
        sends += ring_tree("y+", "y-", kind, (0, 0), chunk, extra)
        sends += ring_tree("y+", "y-", kind, (1, 0), chunk, other)
        return sends
    sends = ring_tree("y+", "y-", kind, (0, 0), chunk, extra)
    return sends + [("z", kind, (0, shift), chunk) for shift in (0, 1, 3, 2)]


def gather_tensor(kind, chunk, extra):
    other = "x-" if extra == "x+" else "x+"
    sends = [("h", kind, (0, 0, 0), chunk)]
    sends += ring_tree("x+", "x-", kind, (0, 0, 0), chunk, extra)
    sends += ring_tree("x+", "x-", kind, (1, 0, 0), chunk, other)
    sends += [("c", kind, (flip, shift, 0), chunk) for flip in (0, 1) for shift in (0, 1, 3, 2)]
    return sends


def row_cuts(rows, pieces):
    step = -(-rows // (16 * pieces)) * 16
    return [(start, min(step, rows - start)) for start in range(0, rows, step)]


class Flow:
    def __init__(self):
        self.sends = {}
        self.tasks = []
        self.left_already = set()

    def send(self, name, link, priority, megabytes, source, target, to, over=()):
        assert name not in self.sends
        self.sends[name] = (link, priority, megabytes, source, target, to, over)
        return name

    def task(self, needs, cost, run, sends=(), rank=5, after=(), name=None):
        self.tasks.append((frozenset(needs), cost, run, tuple(sends), rank, frozenset(after), name))

    def arrange(self):
        free, flying, queues = {}, {}, {}
        landed, done, order, heap = set(), set(), [], []
        left = list(range(len(self.tasks)))
        now, serial = 0.0, 0

        def pump(link):
            while queues.get(link) and flying.get(link, 0) < DEPTH.get(link, 1000):
                name = heapq.heappop(queues[link])[2]
                flying[link] = flying.get(link, 0) + 1
                over = self.sends[name][6] + (("z",) if link == "h" else ())
                for each in (link,) + over:
                    free[each] = max(free.get(each, 0.0), now) + self.sends[name][2] / LINK_RATES[each]
                there = max(free[each] for each in (link,) + over)
                heapq.heappush(heap, (there + LATENCY.get(link, HOP), len(order), name))
                order.append(("start", name))

        while left or heap:
            if heap and heap[0][0] <= now:
                name = heapq.heappop(heap)[2]
                link = self.sends[name][0]
                landed.add(name)
                flying[link] -= 1
                order.append(("arrive", name))
                now += 0.03
                for number in list(left):
                    needs, cost, run, sends, rank, after, _ = self.tasks[number]
                    if rank == 0 and name in needs and needs <= landed and after <= done:
                        left.remove(number)
                        for send in sends:
                            serial += 1
                            put = (self.sends[send][1], serial, send)
                            heapq.heappush(queues.setdefault(self.sends[send][0], []), put)
                for other in sorted(queues):
                    pump(other)
                continue
            ready = []
            for number in left:
                needs, _, _, _, rank, after, _ = self.tasks[number]
                if after <= done and needs <= landed:
                    ready.append((rank, number))
            if not ready:
                assert heap
                now = max(now, heap[0][0])
                continue
            number = min(ready)[1]
            left.remove(number)
            order.append(("run", number))
            _, cost, _, sends, _, _, name = self.tasks[number]
            now += cost
            if name is not None:
                done.add(name)
            for send in sends:
                serial += 1
                put = (self.sends[send][1], serial, send)
                heapq.heappush(queues.setdefault(self.sends[send][0], []), put)
            for other in sorted(queues):
                pump(other)
        self.length = now
        assert not any(queues.values())
        return order

    def copy_of(self, name):
        _, _, _, source, target, to, _ = self.sends[name]
        number = self.number_of[name]
        return pltpu.make_async_remote_copy(
            src_ref=source(),
            dst_ref=target(),
            send_sem=self.send_sem.at[number],
            recv_sem=self.recv_sem.at[number],
            device_id=to(),
            device_id_type=MESH,
        )

    def wait_left(self, names):
        for name in names:
            if name not in self.left_already:
                self.left_already.add(name)
                self.copy_of(name).wait_send()

    def emit(self, order, send_sem, recv_sem):
        self.number_of = {name: number for number, name in enumerate(self.sends)}
        self.send_sem, self.recv_sem = send_sem, recv_sem
        arrived, started = set(), set()
        for what, which in order:
            if what == "arrive":
                self.copy_of(which).wait_recv()
                arrived.add(which)
            elif what == "start":
                self.copy_of(which).start()
                started.add(which)
            elif self.tasks[which][2] is not None:
                self.tasks[which][2]()
        assert arrived == set(self.sends) and started == set(self.sends)
        self.wait_left(list(self.sends))


DEPTH = {"y+": 3, "y-": 3, "z": 3, "x+": 2, "x-": 2, "h": 2}
LINK_RATES = {
    "y+": 0.0455, "y-": 0.0455, "z": 0.0455, "x+": 0.0455, "x-": 0.0455, "h": 0.0455, "c": 0.12, "far": 0.5, "s": 0.2,
}
HOP = 2.5
LATENCY = {"h": 3.5}
PEER_OVER = {
    (1, 2): ("z", "y+"), (0, 2): ("y+", "y-"), (1, 1): ("z", "y+"), (1, 3): ("z", "y-"),
    (1, 0): ("z",), (0, 1): ("y+",), (0, 3): ("y-",),
}
DP_PEERS = ((1, 2), (0, 2), (1, 1), (1, 3), (1, 0), (0, 1), (0, 3))
W_PARTS = 2
X_CUTS = 7
X_MODES = ((False, "y+"), (False, "y-"), (True, "y+"), (True, "y-"), (True, "y+"), (True, "y-"), (True, "y+"))
INNER_MODES = ((True, "y+"), (False, "y-"), (True, "y-"), (False, "y+"))
RELS = [(flip, shift) for flip in (0, 1) for shift in (0, 1, 3, 2)]
TILE = 256


def slot_of(rel):
    return rel[0] * 4 + rel[1] - 1


def aligned(start, size):
    return pl.ds(pl.multiple_of(start, size), size)


def whole_kernel(
    sizes, x_ref, w_ref, e_ref, q_ref, k_ref, tokens_ref,
    ge_ref, gq_ref, gk_ref, both_ref,
    x_pad, x_all, raw, w_all, e_all, o_all, total, inner_own, inner_all, grown_sum,
    lanes, squares, squares_in,
    masked, core_in, left_in, right_in, left_block, right_block, half_in, chosen_all, chosen_sum, hidden,
    q_out, q_in, k_out, k_in, own_part,
    send_sem, recv_sem, local_sem,
):
    place = Place()
    vocab_rows, slab = x_ref.shape
    new_cols, old_width = e_ref.shape
    new_width = sizes
    head_cols = q_ref.shape[0]
    token_rows = tokens_ref.shape[1]
    out_slab, in_slab = w_ref.shape[1:]
    grown = (gq_ref, gk_ref)
    per_seq = both_ref.shape[0]
    cuts = row_cuts(vocab_rows, X_CUTS)
    assert len(cuts) == X_CUTS

    barrier = pltpu.get_barrier_semaphore()
    friends = [place.across(link) for link in ("x+", "x-", "h", "c")]
    friends += [(place.dp_at(rel), place.tensor) for rel in DP_PEERS]
    for friend in friends:
        pl.semaphore_signal(barrier, inc=1, device_id=friend, device_id_type=MESH)
    local = [
        pltpu.make_async_copy(x_ref, x_pad.at[pl.ds(0, vocab_rows), :], local_sem.at[0]),
        pltpu.make_async_copy(w_ref.at[0], w_all.at[0, place.tensor], local_sem.at[1]),
        pltpu.make_async_copy(w_ref.at[1], w_all.at[1, place.tensor], local_sem.at[2]),
        pltpu.make_async_copy(q_ref, o_all.at[0], local_sem.at[3]),
        pltpu.make_async_copy(e_ref, e_all, local_sem.at[4]),
        pltpu.make_async_copy(k_ref, o_all.at[1], local_sem.at[5]),
    ]
    for copy in local:
        copy.start()
    pl.semaphore_wait(barrier, len(friends))

    flow = Flow()

    def gather(kind, sends, megabytes, priority, source, target, ready):
        brought = {}
        for link, _, rel, chunk in sends:
            brought[(seen_by_receiver(link, rel), chunk)] = (kind, link, rel, chunk)
        first, after = {}, {}
        for link, _, rel, chunk in sends:
            name = flow.send(
                (kind, link, rel, chunk), link, priority(link, chunk), megabytes(chunk),
                lambda rel=rel, chunk=chunk: source(rel, chunk),
                lambda link=link, rel=rel, chunk=chunk: target(seen_by_receiver(link, rel), rel, chunk),
                lambda link=link: place.across(link),
            )
            if (rel, chunk) in brought:
                after.setdefault(brought[(rel, chunk)], []).append(name)
            else:
                assert not any(rel)
                first.setdefault(ready(chunk), []).append(name)
        for cause, names in first.items():
            flow.task((), 0.05, None, names, rank=0.5, after=cause)
        for cause, names in after.items():
            flow.task((cause,), 0.0, None, names, rank=0)
        return brought

    sends = []
    for chunk in range(2 * W_PARTS):
        sends += gather_tensor("W", chunk, ("x+", "x-")[chunk % 2])
    w_rows = out_slab // W_PARTS

    def w_view(ref, chunk):
        return ref.at[pl.ds((chunk % W_PARTS) * w_rows, w_rows), :]

    def w_target(rel, chunk):
        return w_view(w_all.at[chunk // W_PARTS, place.tensor_at(rel)], chunk)

    w_from = gather(
        "W", sends, lambda chunk: w_rows * in_slab * 2e-6, lambda link, chunk: 1 + chunk // W_PARTS,
        lambda rel, chunk: w_target(rel, chunk) if any(rel) else w_view(w_ref.at[chunk // W_PARTS], chunk),
        lambda _, rel, chunk: w_target(rel, chunk), lambda chunk: (),
    )

    sends = []
    for chunk, (z_first, extra) in enumerate(X_MODES):
        sends += gather_dp("X", chunk, z_first, extra)

    def x_source(rel, chunk):
        rows = pl.ds(*cuts[chunk])
        return x_ref.at[rows, :] if not any(rel) else x_all.at[slot_of(rel), rows, :]

    x_from = gather(
        "X", sends, lambda chunk: cuts[chunk][1] * slab * 2e-6,
        lambda link, chunk: 10 + (link == "z" and not X_MODES[chunk][0]),
        x_source, lambda there, rel, chunk: x_all.at[slot_of(there), pl.ds(*cuts[chunk]), :], lambda chunk: (),
    )

    pair = 2 * out_slab

    def add_inner(rel, matrix, fresh, last):
        chip = place.tensor_at((rel[0], rel[1], 0)) // 2
        slabs = w_all[matrix, pl.ds(chip * 2, 2)].reshape(pair, in_slab)
        part = jnp.dot(o_all[matrix, :, aligned(chip * pair, pair)], slabs, preferred_element_type=jnp.float32)
        if not fresh:
            part = part + total[matrix]
        if last:
            inner_own[matrix] = part.astype(jnp.bfloat16)
        else:
            total[matrix] = part

    counts = {}

    def counted(key, times, run):
        def go():
            counts[key] = counts.get(key, 0) + 1
            run(counts[key] == 1, counts[key] == times)

        return go

    flow.task((), 0.3, lambda: [local[number].wait() for number in (1, 2, 3, 5)], rank=2, name=("w",))
    for matrix in range(2):
        units = []
        for rel in RELS:
            needs = [
                w_from[(rel + (core,), matrix * W_PARTS + part)]
                for core in (0, 1) for part in range(W_PARTS) if any(rel) or core
            ]
            units.append(("inner", rel, matrix))
            run = counted(
                ("inner", matrix), len(RELS),
                lambda fresh, last, rel=rel, matrix=matrix: add_inner(rel, matrix, fresh, last),
            )
            flow.task(needs, 0.6, run, rank=2 + matrix, after=(("w",),), name=units[-1])
        flow.task((), 0.0, None, rank=2, after=units, name=("inner", matrix))

    tiles = new_cols // TILE

    def e_columns(rel):
        return pl.ds(pl.multiple_of(place.dp_at(rel) * slab, 128), slab)

    def add_raw(rel, half, fresh):
        columns = e_columns(rel)

        def body(number, _):
            rows = aligned(number * TILE, TILE)
            block = x_all[slot_of(rel)] if any(rel) else x_pad[pl.ds(0, vocab_rows), :]
            part = lax.dot_general(block, e_all[rows, columns], LAST, preferred_element_type=jnp.float32)
            if fresh:
                raw[:, rows] = part
            else:
                raw[:, rows] += part
            return 0

        lax.fori_loop(half * tiles // 2, (half + 1) * tiles // 2, body, 0)

    raw_units = []
    for rel in RELS:
        for half in range(2):
            needs = [x_from[(rel, chunk)] for chunk in range(X_CUTS)] if any(rel) else []
            run = counted(
                ("raw", half), len(RELS), lambda fresh, last, rel=rel, half=half: add_raw(rel, half, fresh)
            )
            raw_units.append(("raw", rel, half))
            flow.task(needs, 1.3, run, rank=6, after=(("e",),), name=raw_units[-1])

    core_rows, chip_rows, own_rows = token_rows // 2, token_rows // 8, token_rows // 16
    mine = place.core * core_rows
    theirs = (1 - place.core) * core_rows

    def rows_of(core, shift, part=None):
        start = (1 - place.core if core else place.core) * core_rows + ((place.x + shift + 4) % 4) * chip_rows
        if part is None:
            return aligned(start, chip_rows)
        return aligned(start + part * own_rows, own_rows)

    def small_rows(flip):
        z_hi = 1 - place.z_hi if flip else place.z_hi
        return aligned(mine + place.x * chip_rows + z_hi * own_rows, own_rows)

    def lane_sums(values_ref, rows):
        sums = None
        for start in range(0, values_ref.shape[1], 128):
            part = jnp.square(values_ref[pl.ds(0, rows), start:start + 128].astype(jnp.float32))
            sums = part if sums is None else sums + part
        return sums

    def row_sums(values_ref):
        lanes[pl.ds(lanes.shape[0] - 32, 32), :] = jnp.zeros((32, 128), jnp.float32)
        lanes[pl.ds(0, vocab_rows), :] = lane_sums(values_ref, vocab_rows)
        return jnp.broadcast_to(jnp.sum(lanes[...].T, axis=0, keepdims=True), squares.shape)

    def load_x():
        local[0].wait()
        end = pl.ds(x_pad.shape[0] - 32, 32)
        row = lax.broadcasted_iota(jnp.int32, (32, slab), 0) + (x_pad.shape[0] - 32)
        x_pad[end, :] = jnp.where(row < vocab_rows, x_pad[end, :].astype(jnp.float32), 0.0).astype(jnp.bfloat16)

    def choose(start):
        def body(number, _):
            rows = aligned(start + number * TILE, TILE)
            row = jnp.broadcast_to(tokens_ref[:, rows].astype(jnp.float32), (128, TILE))
            ids = row.T[:, :1].astype(jnp.int32) - place.tensor * vocab_rows
            column = lax.broadcasted_iota(jnp.int32, (TILE, x_pad.shape[0]), 1)
            one = jnp.where((ids == column) & (column < vocab_rows), 1.0, 0.0).astype(jnp.bfloat16)
            masked[rows, :] = jnp.dot(one, x_pad[...], preferred_element_type=jnp.float32).astype(jnp.bfloat16)
            return 0

        lax.fori_loop(0, core_rows // TILE, body, 0)

    def to(link):
        return lambda: place.across(link)

    core_mb = core_rows * slab * 2e-6
    block_mb = core_mb / 4
    flow.send("c1", "c", 0, core_mb, lambda: masked.at[aligned(theirs, core_rows), :], lambda: core_in, to("c"))
    flow.task((), 1.0, load_x, rank=1, name=("x",))
    flow.task((), 1.2, lambda: choose(theirs), ("c1",), rank=1, name=("theirs",), after=(("x",),))
    flow.task((), 1.2, lambda: choose(mine), rank=1, name=("mine",), after=(("theirs",),))

    def add_core():
        rows = aligned(mine, core_rows)
        masked[rows, :] += core_in[...]

    flow.send("r+", "x+", 0, block_mb / 2, lambda: masked.at[rows_of(0, 2, 0), :], lambda: left_in, to("x+"))
    flow.send("r-", "x-", 0, block_mb / 2, lambda: masked.at[rows_of(0, 2, 1), :], lambda: right_in, to("x-"))
    flow.task(("c1",), 0.5, add_core, ("r+", "r-"), rank=1, name=("core",), after=(("mine",),))

    def add_left():
        masked[rows_of(0, 1, 0), :] += left_in[...]

    def add_right():
        masked[rows_of(0, 3, 1), :] += right_in[...]

    flow.send("b+", "x+", 0, block_mb, lambda: masked.at[rows_of(0, 1), :], lambda: left_block, to("x+"))
    flow.send("b-", "x-", 0, block_mb, lambda: masked.at[rows_of(0, 3), :], lambda: right_block, to("x-"))
    flow.task(("r+",), 0.1, add_left, ("b+",), rank=1, after=(("core",),))
    flow.task(("r-",), 0.1, add_right, ("b-",), rank=1, after=(("core",),))

    def add_blocks():
        masked[rows_of(0, 0), :] += left_block[...] + right_block[...]

    flow.send("h1", "h", 0, block_mb / 2, lambda: masked.at[small_rows(1), :], lambda: half_in, to("h"))
    flow.task(("b+", "b-"), 0.2, add_blocks, ("h1",), rank=1, name=("blocks",), after=(("core",),))

    def add_half():
        chosen_all[0] = masked[small_rows(0), :] + half_in[...]

    flow.task(("h1",), 0.1, add_half, rank=1, name=("chosen",), after=(("blocks",),))
    t_from = gather(
        "T", gather_dp("T", 0, True, "y+"), lambda chunk: own_rows * slab * 2e-6, lambda link, chunk: 0,
        lambda rel, chunk: chosen_all.at[slot_of(rel) + 1], lambda there, rel, chunk: chosen_all.at[slot_of(there) + 1],
        lambda chunk: (("chosen",),),
    )

    def grow_chosen(rel, fresh, last):
        at = slot_of(rel) + 1
        columns = e_columns(rel)

        def body(number, _):
            rows = aligned(number * TILE, TILE)
            part = lax.dot_general(
                chosen_all[at], e_all[rows, columns], LAST, preferred_element_type=jnp.float32
            )
            if fresh:
                chosen_sum[:, rows] = part
            else:
                chosen_sum[:, rows] += part
            return 0

        lax.fori_loop(0, tiles, body, 0)
        if last:
            old_squares = None
            for number in range(N_DP):
                for start in range(0, slab, 128):
                    part = jnp.square(chosen_all[number, :, start:start + 128].astype(jnp.float32))
                    old_squares = part if old_squares is None else old_squares + part
            hidden[small_rows(0), pl.ds(0, new_cols)] = chosen_sum[...].astype(jnp.bfloat16)
            hidden[small_rows(0), pl.ds(new_cols, 128)] = old_squares.astype(jnp.bfloat16)

    units = []
    flow.task((), 0.1, lambda: local[4].wait(), rank=4, name=("e",))
    for rel in RELS:
        needs = [t_from[(rel, 0)]] if any(rel) else []
        run = counted("chosen", len(RELS), lambda fresh, last, rel=rel: grow_chosen(rel, fresh, last))
        units.append(("chosen", rel))
        flow.task(needs, 0.9, run, rank=1.5, after=(("e",), ("chosen",)), name=units[-1])

    own_mb = own_rows * hidden.shape[1] * 2e-6

    def same(name, link, megabytes, rows):
        return flow.send(
            name, link, 0, megabytes, lambda: hidden.at[rows(), :], lambda: hidden.at[rows(), :], to(link)
        )

    same("h2", "h", own_mb, lambda: small_rows(0))
    same("a+", "x+", 2 * own_mb, lambda: rows_of(0, 0))
    same("a-", "x-", 2 * own_mb, lambda: rows_of(0, 0))
    same("f+", "x+", own_mb, lambda: rows_of(0, 3, 0))
    same("f-", "x-", own_mb, lambda: rows_of(0, 1, 1))
    for shift in range(4):
        same(("c", shift), "c", 2 * own_mb, lambda shift=shift: rows_of(0, shift))
    flow.task((), 0.0, None, ("h2",), rank=0.5, after=units, name=("hidden",))
    flow.task(("h2",), 0.02, None, ("a+", "a-", ("c", 0)), rank=0.5, after=(("hidden",),))
    flow.task(("a+",), 0.0, None, ("f+", ("c", 3)), rank=0)
    flow.task(("a-",), 0.0, None, ("f-", ("c", 1)), rank=0)
    flow.task(("f+", "f-"), 0.0, None, (("c", 2),), rank=0)

    half = head_cols // 2
    sends = []
    for chunk, (z_first, extra) in enumerate(INNER_MODES):
        sends += gather_dp("I", chunk, z_first, extra)

    def inner_view(ref, chunk):
        return ref.at[chunk // 2, pl.ds((chunk % 2) * half, half), :]

    def i_source(rel, chunk):
        return inner_view(inner_all.at[slot_of(rel)] if any(rel) else inner_own, chunk)

    i_from = gather(
        "I", sends, lambda chunk: half * in_slab * 2e-6, lambda link, chunk: 3 + chunk // 2,
        i_source, lambda there, rel, chunk: inner_view(inner_all.at[slot_of(there)], chunk),
        lambda chunk: (("inner", chunk // 2),),
    )

    def add_grown(rel, matrix, fresh, last):
        columns = e_columns(rel)

        def body(number, _):
            rows = aligned(number * TILE, TILE)
            block = inner_all[slot_of(rel), matrix] if any(rel) else inner_own[matrix]
            part = lax.dot_general(e_all[rows, columns], block, LAST, preferred_element_type=jnp.float32)
            if not fresh:
                part = part + grown_sum[matrix, rows, :]
            if last:
                grown[matrix][rows, :] = part.astype(jnp.bfloat16)
            else:
                grown_sum[matrix, rows, :] = part
            return 0

        lax.fori_loop(0, tiles, body, 0)

    for matrix in range(2):
        units = []
        for rel in RELS:
            needs = [i_from[(rel, chunk)] for chunk in (2 * matrix, 2 * matrix + 1)] if any(rel) else []
            run = counted(
                ("grown", matrix), len(RELS),
                lambda fresh, last, rel=rel, matrix=matrix: add_grown(rel, matrix, fresh, last),
            )
            units.append(("grown", rel, matrix))
            flow.task(needs, 0.9, run, rank=3, after=(("e",), ("inner", matrix)), name=units[-1])
        flow.task((), 0.0, None, rank=3, after=units, name=("grown", matrix))

    def square_rows():
        row = lax.broadcasted_iota(jnp.int32, squares.shape, 0)
        squares[...] = jnp.where(row == 1, row_sums(x_pad), 0.0)
        squares[...] = jnp.where(row == 0, row_sums(raw), squares[...])

    square_sends = [
        flow.send(
            ("S", number), "s", 0, 0.03, lambda: squares, lambda number=number: squares_in.at[number],
            lambda rel=rel: (place.dp_at(rel), place.tensor),
        )
        for number, rel in enumerate(DP_PEERS)
    ]
    flow.task((), 2.5, square_rows, square_sends, rank=4, after=raw_units, name=("squares",))
    ge_cuts = ((0, slab, slot_of((1, 2))), (slab, new_cols - slab, slot_of((0, 2))))

    def ge_copies():
        return [
            pltpu.make_async_copy(
                x_all.at[slot, :, pl.ds(0, size)], ge_ref.at[:, pl.ds(start, size)], local_sem.at[6 + number]
            )
            for number, (start, size, slot) in enumerate(ge_cuts)
        ]

    def rescale():
        flow.wait_left([name for name in flow.sends if name[0] == "X"])
        sums = squares[...]
        for number in range(len(DP_PEERS)):
            sums = sums + squares_in[number]
        factor = jnp.sqrt((sums[1:2] / old_width + EMBED_EPSILON) / (sums[0:1] / new_width + EMBED_EPSILON))
        column = jnp.broadcast_to(factor, (128, factor.shape[1])).T[:vocab_rows]
        for start, size, slot in ge_cuts:
            for at in range(0, size, 128):
                scaled = raw[:, start + at:start + at + 128] * column
                x_all[slot, :, at:at + 128] = scaled.astype(jnp.bfloat16)
        for copy in ge_copies():
            copy.start()

    flow.task(square_sends, 2.5, rescale, rank=5, name=("scaled",), after=(("squares",),))

    def seq_rows(rel):
        return aligned(place.dp_at(rel) * per_seq, per_seq)

    def partial(rel, matrix):
        block = hidden[seq_rows(rel), pl.ds(0, new_cols)]
        return jnp.dot(block, grown[matrix][...], preferred_element_type=jnp.float32)

    def lane_squares_of(rel):
        sums = None
        for start in range(0, new_cols, 128):
            part = jnp.square(hidden[seq_rows(rel), start:start + 128].astype(jnp.float32))
            sums = part if sums is None else sums + part
        return sums

    def put_query(number, rel):
        q_out[number, :, :head_cols] = partial(rel, 0).astype(jnp.bfloat16)
        q_out[number, :, head_cols:] = lane_squares_of(rel).astype(jnp.bfloat16)

    def put_key(number, rel):
        k_out[number] = partial(rel, 1).astype(jnp.bfloat16)

    gathered = ["h2", "a+", "a-", "f+", "f-"] + [("c", shift) for shift in range(4)]
    arrivals = []
    for matrix, (put, out, into) in enumerate(((put_query, q_out, q_in), (put_key, k_out, k_in))):
        for number, rel in enumerate(DP_PEERS):
            name = flow.send(
                ("P", matrix, number), "far", 0, per_seq * out.shape[2] * 2e-6,
                lambda out=out, number=number: out.at[number], lambda into=into, number=number: into.at[number],
                lambda rel=rel: (place.dp_at(rel), place.tensor), PEER_OVER[rel],
            )
            arrivals.append(name)
            flow.task(
                gathered, 0.4, lambda put=put, number=number, rel=rel: put(number, rel), (name,),
                rank=2.5, after=(("grown", matrix), ("hidden",)),
            )

    def keep_own(matrix):
        own_part[:, matrix * head_cols:(matrix + 1) * head_cols] = partial((0, 0), matrix)
        if matrix == 0:
            own_part[:, 2 * head_cols:] = lane_squares_of((0, 0))

    for matrix in range(2):
        flow.task(
            gathered, 0.4, lambda matrix=matrix: keep_own(matrix), rank=3.5,
            after=(("grown", matrix), ("hidden",)), name=("own", matrix),
        )

    def add_up():
        queries = own_part[:, :head_cols]
        keys = own_part[:, head_cols:2 * head_cols]
        square_lanes = own_part[:, 2 * head_cols:]
        for number in range(len(DP_PEERS)):
            queries = queries + q_in[number, :, :head_cols].astype(jnp.float32)
            square_lanes = square_lanes + q_in[number, :, head_cols:].astype(jnp.float32)
            keys = keys + k_in[number].astype(jnp.float32)
        raw_ms = jnp.sum(square_lanes, axis=1, keepdims=True) / new_width
        old_lanes = hidden[seq_rows((0, 0)), pl.ds(new_cols, 128)].astype(jnp.float32)
        old_ms = jnp.sum(old_lanes, axis=1, keepdims=True) / old_width
        factor = jnp.sqrt((old_ms + EMBED_EPSILON) / (raw_ms + EMBED_EPSILON))
        scale = factor * lax.rsqrt(factor * factor * raw_ms + TOKEN_EPSILON)
        both_ref[:, :head_cols] = queries * scale
        both_ref[:, head_cols:] = keys * scale

    flow.task(arrivals, 1.0, add_up, rank=9, after=(("own", 0), ("own", 1)))
    order = flow.arrange()
    flow.emit(order, send_sem, recv_sem)
    for copy in ge_copies():
        copy.wait()


def grow_and_check(token_ids, old_embed, expand_in, query_out, key_out, old_query, old_key):
    vocab_rows, slab = old_embed.shape
    in_slab, out_slab = old_query.shape
    new_cols = expand_in.shape[0]
    head_cols = query_out.shape[0]
    tokens = token_ids.shape[0]
    padded = -(-vocab_rows // 128) * 128
    per_seq = tokens // N_DP
    turned = jnp.stack([old_query.T, old_key.T])
    anywhere = pl.BlockSpec(memory_space=pl.ANY)
    inside = pl.BlockSpec(memory_space=pltpu.VMEM)
    bf16, f32 = jnp.bfloat16, jnp.float32
    count = (2 * W_PARTS * 15) + 7 * X_CUTS + 7 * len(INNER_MODES) + 7 + 1 + 4 + 1 + 9 + 7 + 14
    return pl.pallas_call(
        lambda *refs: whole_kernel(D_NEW, *refs),
        out_shape=(
            jax.ShapeDtypeStruct((vocab_rows, new_cols), bf16),
            jax.ShapeDtypeStruct((new_cols, head_cols), bf16),
            jax.ShapeDtypeStruct((new_cols, head_cols), bf16),
            jax.ShapeDtypeStruct((per_seq, 2 * head_cols), f32),
        ),
        in_specs=[anywhere] * 5 + [inside],
        out_specs=(anywhere, inside, inside, inside),
        scratch_shapes=[
            pltpu.VMEM((padded, slab), bf16),
            pltpu.VMEM((N_DP - 1, vocab_rows, slab), bf16),
            pltpu.VMEM((vocab_rows, new_cols), f32),
            pltpu.VMEM((2, N_TENSOR, out_slab, in_slab), bf16),
            pltpu.VMEM(expand_in.shape, bf16),
            pltpu.VMEM((2,) + query_out.shape, bf16),
            pltpu.VMEM((2, head_cols, in_slab), f32),
            pltpu.VMEM((2, head_cols, in_slab), bf16),
            pltpu.VMEM((N_DP - 1, 2, head_cols, in_slab), bf16),
            pltpu.VMEM((2, new_cols, head_cols), f32),
            pltpu.VMEM((padded, 128), f32),
            pltpu.VMEM((8, padded), f32),
            pltpu.VMEM((7, 8, padded), f32),
            pltpu.VMEM((tokens, slab), bf16),
            pltpu.VMEM((tokens // 2, slab), bf16),
            pltpu.VMEM((tokens // 16, slab), bf16),
            pltpu.VMEM((tokens // 16, slab), bf16),
            pltpu.VMEM((tokens // 8, slab), bf16),
            pltpu.VMEM((tokens // 8, slab), bf16),
            pltpu.VMEM((tokens // 16, slab), bf16),
            pltpu.VMEM((N_DP, tokens // 16, slab), bf16),
            pltpu.VMEM((tokens // 16, new_cols), f32),
            pltpu.VMEM((tokens, new_cols + 128), bf16),
            pltpu.VMEM((7, per_seq, head_cols + 128), bf16),
            pltpu.VMEM((7, per_seq, head_cols + 128), bf16),
            pltpu.VMEM((7, per_seq, head_cols), bf16),
            pltpu.VMEM((7, per_seq, head_cols), bf16),
            pltpu.VMEM((per_seq, 2 * head_cols + 128), f32),
            pltpu.SemaphoreType.DMA((count,)),
            pltpu.SemaphoreType.DMA((count,)),
            pltpu.SemaphoreType.DMA((8,)),
        ],
        compiler_params=pltpu.CompilerParams(
            collective_id=1, has_side_effects=True, vmem_limit_bytes=VMEM_LIMIT
        ),
        name="grow_and_check",
    )(old_embed, turned, expand_in, query_out, key_out, token_ids.reshape(1, tokens))


def rotate(values, head_count):
    row_count = values.shape[0]
    shaped = values.reshape(row_count, head_count, HEAD)
    half_size = HEAD // 2
    position = jnp.arange(row_count).astype(jnp.float32)
    frequency = jnp.exp(
        -math.log(10000.0) * jnp.arange(half_size).astype(jnp.float32) * (2.0 / HEAD)
    )
    angles = position[:, None] * frequency[None, :]
    cosine = jnp.cos(angles)[:, None, :]
    sine_table = jnp.sin(angles)[:, None, :]
    first_half = shaped[..., :half_size]
    second = shaped[..., half_size:]
    return jnp.concatenate(
        [first_half * cosine - second * sine_table, second * cosine + first_half * sine_table],
        axis=-1,
    )


def entropy_of(queries, key_proj, head_count):
    rotated_q = rotate(queries, head_count).astype(jnp.bfloat16)
    rotated_k = rotate(key_proj, head_count).astype(jnp.bfloat16)
    scores = jnp.einsum(
        "ihd,jhd->hij", rotated_q, rotated_k, preferred_element_type=jnp.float32
    ) * HEAD ** (-0.5)
    row_count = queries.shape[0]
    causal = jnp.arange(row_count)[:, None] >= jnp.arange(row_count)[None, :]
    weights = jnp.where(causal[None], jnp.exp(scores), 0.0)
    weight_sum = jnp.sum(weights, axis=-1)
    entropy = jnp.log(weight_sum) - jnp.sum(weights * scores, axis=-1) / weight_sum
    return entropy.T


def on_device(token_ids, old_embed, expand_in, query_out, key_out, old_query, old_key):
    head_cols = query_out.shape[0]
    grown_embedding, grown_query, grown_key, both = grow_and_check(
        token_ids, old_embed, expand_in, query_out, key_out, old_query, old_key
    )
    attention_entropy = entropy_of(both[:, :head_cols], both[:, head_cols:], head_cols // HEAD)
    return (grown_embedding, grown_query, grown_key, attention_entropy)


def solution(mesh):
    placed = (
        P(),
        P("tensor", "dp"),
        P("dp", None),
        P("tensor", None),
        P("tensor", None),
        P("dp", "tensor"),
        P("dp", "tensor"),
    )
    return jax.shard_map(
        on_device,
        mesh=mesh,
        in_specs=placed,
        out_specs=(P("tensor", "dp"), P("dp", "tensor"), P("dp", "tensor"), P("dp", "tensor")),
        check_vma=False,
    )
```

```python
import heapq
import math

import jax
import jax.numpy as jnp
from jax import lax
from jax.experimental import pallas as pl
from jax.experimental.pallas import tpu as pltpu
from jax.sharding import PartitionSpec as P

D_NEW = 8192
HEAD = 128
N_DP = 8
N_TENSOR = 16

EMBED_EPSILON = 1e-06
TOKEN_EPSILON = 1e-05

MESH = pl.DeviceIdType.MESH
LAST = (((1,), (1,)), ((), ()))
VMEM_LIMIT = 67_000_000

STEP = {"y+": 1, "y-": -1, "x+": 1, "x-": -1}


class Place:
    def __init__(self):
        self.dp = lax.axis_index("dp")
        self.tensor = lax.axis_index("tensor")
        self.z_lo = self.dp // 4
        self.y = self.dp % 4
        self.x = self.tensor // 4
        self.z_hi = (self.tensor // 2) % 2
        self.core = self.tensor % 2

    def dp_at(self, rel):
        flip, shift = rel
        z_lo = 1 - self.z_lo if flip else self.z_lo
        return z_lo * 4 + (self.y + shift + 4) % 4

    def tensor_at(self, rel):
        flip, shift, core_flip = rel
        z_hi = 1 - self.z_hi if flip else self.z_hi
        core = 1 - self.core if core_flip else self.core
        return (((self.x + shift + 4) % 4) * 2 + z_hi) * 2 + core

    def across(self, link):
        if link in ("y+", "y-"):
            return (self.dp_at((0, STEP[link])), self.tensor)
        if link == "z":
            return (self.dp_at((1, 0)), self.tensor)
        if link in ("x+", "x-"):
            return (self.dp, self.tensor_at((0, STEP[link], 0)))
        if link == "h":
            return (self.dp, self.tensor_at((1, 0, 0)))
        return (self.dp, self.tensor_at((0, 0, 1)))


def seen_by_receiver(link, rel):
    if link in ("y+", "y-"):
        return (rel[0], (rel[1] - STEP[link]) % 4)
    if link == "z":
        return (1 - rel[0], rel[1])
    if link in ("x+", "x-"):
        return (rel[0], (rel[1] - STEP[link]) % 4, rel[2])
    if link == "h":
        return (1 - rel[0], rel[1], rel[2])
    return (rel[0], rel[1], 1 - rel[2])


def ring_tree(plus, minus, kind, rel, chunk, extra):
    near = (rel[0], (rel[1] - STEP[extra]) % 4) + tuple(rel[2:])
    return [(plus, kind, rel, chunk), (minus, kind, rel, chunk), (extra, kind, near, chunk)]


def gather_dp(kind, chunk, z_first, extra):
    other = "y-" if extra == "y+" else "y+"
    if z_first:
        sends = [("z", kind, (0, 0), chunk)]
        sends += ring_tree("y+", "y-", kind, (0, 0), chunk, extra)
        sends += ring_tree("y+", "y-", kind, (1, 0), chunk, other)
        return sends
    sends = ring_tree("y+", "y-", kind, (0, 0), chunk, extra)
    return sends + [("z", kind, (0, shift), chunk) for shift in (0, 1, 3, 2)]


def gather_tensor(kind, chunk, extra):
    other = "x-" if extra == "x+" else "x+"
    sends = [("h", kind, (0, 0, 0), chunk)]
    sends += ring_tree("x+", "x-", kind, (0, 0, 0), chunk, extra)
    sends += ring_tree("x+", "x-", kind, (1, 0, 0), chunk, other)
    sends += [("c", kind, (flip, shift, 0), chunk) for flip in (0, 1) for shift in (0, 1, 3, 2)]
    return sends


def row_cuts(rows, pieces):
    step = -(-rows // (16 * pieces)) * 16
    return [(start, min(step, rows - start)) for start in range(0, rows, step)]


class Flow:
    def __init__(self):
        self.sends = {}
        self.tasks = []
        self.left_already = set()

    def send(self, name, link, priority, megabytes, source, target, to, over=()):
        assert name not in self.sends
        self.sends[name] = (link, priority, megabytes, source, target, to, over)
        return name

    def task(self, needs, cost, run, sends=(), rank=5, after=(), name=None):
        self.tasks.append((frozenset(needs), cost, run, tuple(sends), rank, frozenset(after), name))

    def arrange(self):
        free, flying, queues = {}, {}, {}
        landed, done, order, heap = set(), set(), [], []
        left = list(range(len(self.tasks)))
        now, serial = 0.0, 0

        def pump(link):
            while queues.get(link) and flying.get(link, 0) < DEPTH.get(link, 1000):
                name = heapq.heappop(queues[link])[2]
                flying[link] = flying.get(link, 0) + 1
                over = self.sends[name][6] + (("z",) if link == "h" else ())
                for each in (link,) + over:
                    free[each] = max(free.get(each, 0.0), now) + self.sends[name][2] / LINK_RATES[each]
                there = max(free[each] for each in (link,) + over)
                heapq.heappush(heap, (there + LATENCY.get(link, HOP), len(order), name))
                order.append(("start", name))

        while left or heap:
            if heap and heap[0][0] <= now:
                name = heapq.heappop(heap)[2]
                link = self.sends[name][0]
                landed.add(name)
                flying[link] -= 1
                order.append(("arrive", name))
                now += 0.03
                for number in list(left):
                    needs, cost, run, sends, rank, after, _ = self.tasks[number]
                    if rank == 0 and name in needs and needs <= landed and after <= done:
                        left.remove(number)
                        for send in sends:
                            serial += 1
                            put = (self.sends[send][1], serial, send)
                            heapq.heappush(queues.setdefault(self.sends[send][0], []), put)
                for other in sorted(queues):
                    pump(other)
                continue
            ready = []
            for number in left:
                needs, _, _, _, rank, after, _ = self.tasks[number]
                if after <= done and needs <= landed:
                    ready.append((rank, number))
            if not ready:
                assert heap
                now = max(now, heap[0][0])
                continue
            number = min(ready)[1]
            left.remove(number)
            order.append(("run", number))
            _, cost, _, sends, _, _, name = self.tasks[number]
            now += cost
            if name is not None:
                done.add(name)
            for send in sends:
                serial += 1
                put = (self.sends[send][1], serial, send)
                heapq.heappush(queues.setdefault(self.sends[send][0], []), put)
            for other in sorted(queues):
                pump(other)
        self.length = now
        assert not any(queues.values())
        return order

    def copy_of(self, name):
        _, _, _, source, target, to, _ = self.sends[name]
        number = self.number_of[name]
        return pltpu.make_async_remote_copy(
            src_ref=source(),
            dst_ref=target(),
            send_sem=self.send_sem.at[number],
            recv_sem=self.recv_sem.at[number],
            device_id=to(),
            device_id_type=MESH,
        )

    def wait_left(self, names):
        for name in names:
            if name not in self.left_already:
                self.left_already.add(name)
                self.copy_of(name).wait_send()

    def emit(self, order, send_sem, recv_sem):
        self.number_of = {name: number for number, name in enumerate(self.sends)}
        self.send_sem, self.recv_sem = send_sem, recv_sem
        arrived, started = set(), set()
        needed = {send: needs for needs, _, _, sends, _, _, _ in self.tasks for send in sends}

        def wait_for(names):
            for name in sorted(names - arrived, key=str):
                self.copy_of(name).wait_recv()
                arrived.add(name)

        for what, which in order:
            if what == "start":
                wait_for(needed[which])
                self.copy_of(which).start()
                started.add(which)
            elif what == "run":
                wait_for(self.tasks[which][0])
                if self.tasks[which][2] is not None:
                    self.tasks[which][2]()
        wait_for(set(self.sends))
        assert arrived == set(self.sends) and started == set(self.sends)
        self.wait_left(list(self.sends))


DEPTH = {"y+": 3, "y-": 3, "z": 3, "x+": 2, "x-": 2, "h": 2}
LINK_RATES = {
    "y+": 0.0455, "y-": 0.0455, "z": 0.0455, "x+": 0.0455, "x-": 0.0455, "h": 0.0455, "c": 0.12, "far": 0.5, "s": 0.2,
}
HOP = 2.5
LATENCY = {"h": 3.5}
PEER_OVER = {
    (1, 2): ("z", "y+"), (0, 2): ("y+", "y-"), (1, 1): ("z", "y+"), (1, 3): ("z", "y-"),
    (1, 0): ("z",), (0, 1): ("y+",), (0, 3): ("y-",),
}
DP_PEERS = ((1, 2), (0, 2), (1, 1), (1, 3), (1, 0), (0, 1), (0, 3))
W_PARTS = 2
X_CUTS = 7
X_MODES = ((False, "y+"), (False, "y-"), (True, "y+"), (True, "y-"), (True, "y+"), (True, "y-"), (True, "y+"))
INNER_MODES = ((True, "y+"), (False, "y-"), (True, "y-"), (False, "y+"))
RELS = [(flip, shift) for flip in (0, 1) for shift in (0, 1, 3, 2)]
TILE = 256


def slot_of(rel):
    return rel[0] * 4 + rel[1] - 1


def aligned(start, size):
    return pl.ds(pl.multiple_of(start, size), size)


def whole_kernel(
    sizes, x_ref, w_ref, e_ref, q_ref, k_ref, tokens_ref,
    ge_ref, gq_ref, gk_ref, both_ref,
    x_pad, x_all, raw, w_all, e_all, o_all, total, inner_own, inner_all, grown_sum,
    lanes, squares, squares_in,
    masked, core_in, left_in, right_in, left_block, right_block, half_in, chosen_all, chosen_sum, hidden,
    q_out, q_in, k_out, k_in, own_part, chunk_squares, chunk_in,
    send_sem, recv_sem, local_sem,
):
    place = Place()
    vocab_rows, slab = x_ref.shape
    new_cols, old_width = e_ref.shape
    new_width = sizes
    head_cols = q_ref.shape[0]
    token_rows = tokens_ref.shape[1]
    out_slab, in_slab = w_ref.shape[1:]
    grown = (gq_ref, gk_ref)
    per_seq = both_ref.shape[0]
    cuts = row_cuts(vocab_rows, X_CUTS)
    assert len(cuts) == X_CUTS

    barrier = pltpu.get_barrier_semaphore()
    friends = [place.across(link) for link in ("x+", "x-", "h", "c")]
    friends += [(place.dp_at(rel), place.tensor) for rel in DP_PEERS]
    for friend in friends:
        pl.semaphore_signal(barrier, inc=1, device_id=friend, device_id_type=MESH)
    local = [
        pltpu.make_async_copy(x_ref, x_pad.at[pl.ds(0, vocab_rows), :], local_sem.at[0]),
        pltpu.make_async_copy(w_ref.at[0], w_all.at[0, place.tensor], local_sem.at[1]),
        pltpu.make_async_copy(w_ref.at[1], w_all.at[1, place.tensor], local_sem.at[2]),
        pltpu.make_async_copy(q_ref, o_all.at[0], local_sem.at[3]),
        pltpu.make_async_copy(e_ref, e_all, local_sem.at[4]),
        pltpu.make_async_copy(k_ref, o_all.at[1], local_sem.at[5]),
    ]
    for copy in local:
        copy.start()
    pl.semaphore_wait(barrier, len(friends))

    flow = Flow()

    def gather(kind, sends, megabytes, priority, source, target, ready):
        brought = {}
        for link, _, rel, chunk in sends:
            brought[(seen_by_receiver(link, rel), chunk)] = (kind, link, rel, chunk)
        first, after = {}, {}
        for link, _, rel, chunk in sends:
            name = flow.send(
                (kind, link, rel, chunk), link, priority(link, chunk), megabytes(chunk),
                lambda rel=rel, chunk=chunk: source(rel, chunk),
                lambda link=link, rel=rel, chunk=chunk: target(seen_by_receiver(link, rel), rel, chunk),
                lambda link=link: place.across(link),
            )
            if (rel, chunk) in brought:
                after.setdefault(brought[(rel, chunk)], []).append(name)
            else:
                assert not any(rel)
                first.setdefault(ready(chunk), []).append(name)
        for cause, names in first.items():
            flow.task((), 0.05, None, names, rank=0.5, after=cause)
        for cause, names in after.items():
            flow.task((cause,), 0.0, None, names, rank=0)
        return brought

    sends = []
    for chunk in range(2 * W_PARTS):
        sends += gather_tensor("W", chunk, ("x+", "x-")[chunk % 2])
    w_rows = out_slab // W_PARTS

    def w_view(ref, chunk):
        return ref.at[pl.ds((chunk % W_PARTS) * w_rows, w_rows), :]

    def w_target(rel, chunk):
        return w_view(w_all.at[chunk // W_PARTS, place.tensor_at(rel)], chunk)

    w_from = gather(
        "W", sends, lambda chunk: w_rows * in_slab * 2e-6, lambda link, chunk: 1 + chunk // W_PARTS,
        lambda rel, chunk: w_target(rel, chunk) if any(rel) else w_view(w_ref.at[chunk // W_PARTS], chunk),
        lambda _, rel, chunk: w_target(rel, chunk), lambda chunk: (),
    )

    sends = []
    for chunk, (z_first, extra) in enumerate(X_MODES):
        sends += gather_dp("X", chunk, z_first, extra)

    def x_source(rel, chunk):
        rows = pl.ds(*cuts[chunk])
        return x_ref.at[rows, :] if not any(rel) else x_all.at[slot_of(rel), rows, :]

    x_from = gather(
        "X", sends, lambda chunk: cuts[chunk][1] * slab * 2e-6,
        lambda link, chunk: 10 + (link == "z" and not X_MODES[chunk][0]),
        x_source, lambda there, rel, chunk: x_all.at[slot_of(there), pl.ds(*cuts[chunk]), :], lambda chunk: (),
    )

    pair = 2 * out_slab

    def add_inner(rel, matrix, fresh, last):
        chip = place.tensor_at((rel[0], rel[1], 0)) // 2
        slabs = w_all[matrix, pl.ds(chip * 2, 2)].reshape(pair, in_slab)
        part = jnp.dot(o_all[matrix, :, aligned(chip * pair, pair)], slabs, preferred_element_type=jnp.float32)
        if not fresh:
            part = part + total[matrix]
        if last:
            inner_own[matrix] = part.astype(jnp.bfloat16)
        else:
            total[matrix] = part

    counts = {}

    def counted(key, times, run):
        def go():
            counts[key] = counts.get(key, 0) + 1
            run(counts[key] == 1, counts[key] == times)

        return go

    flow.task((), 0.3, lambda: [local[number].wait() for number in (1, 2, 3, 5)], rank=2, name=("w",))
    for matrix in range(2):
        units = []
        for rel in RELS:
            needs = [
                w_from[(rel + (core,), matrix * W_PARTS + part)]
                for core in (0, 1) for part in range(W_PARTS) if any(rel) or core
            ]
            units.append(("inner", rel, matrix))
            run = counted(
                ("inner", matrix), len(RELS),
                lambda fresh, last, rel=rel, matrix=matrix: add_inner(rel, matrix, fresh, last),
            )
            flow.task(needs, 0.6, run, rank=2 + matrix, after=(("w",),), name=units[-1])
        flow.task((), 0.0, None, rank=2, after=units, name=("inner", matrix))

    tiles = new_cols // TILE

    def e_columns(rel):
        return pl.ds(pl.multiple_of(place.dp_at(rel) * slab, 128), slab)

    def add_raw(rel, half, fresh):
        columns = e_columns(rel)

        def body(number, _):
            rows = aligned(number * TILE, TILE)
            block = x_all[slot_of(rel)] if any(rel) else x_pad[pl.ds(0, vocab_rows), :]
            part = lax.dot_general(block, e_all[rows, columns], LAST, preferred_element_type=jnp.float32)
            if fresh:
                raw[:, rows] = part
            else:
                raw[:, rows] += part
            return 0

        lax.fori_loop(half * tiles // 2, (half + 1) * tiles // 2, body, 0)

    raw_units = []
    for rel in RELS:
        for half in range(2):
            needs = [x_from[(rel, chunk)] for chunk in range(X_CUTS)] if any(rel) else []
            run = counted(
                ("raw", half), len(RELS), lambda fresh, last, rel=rel, half=half: add_raw(rel, half, fresh)
            )
            raw_units.append(("raw", rel, half))
            flow.task(needs, 1.3, run, rank=6, after=(("e",),), name=raw_units[-1])

    core_rows, chip_rows, own_rows = token_rows // 2, token_rows // 8, token_rows // 16
    mine = place.core * core_rows
    theirs = (1 - place.core) * core_rows

    def rows_of(core, shift, part=None):
        start = (1 - place.core if core else place.core) * core_rows + ((place.x + shift + 4) % 4) * chip_rows
        if part is None:
            return aligned(start, chip_rows)
        return aligned(start + part * own_rows, own_rows)

    def small_rows(flip):
        z_hi = 1 - place.z_hi if flip else place.z_hi
        return aligned(mine + place.x * chip_rows + z_hi * own_rows, own_rows)

    def lane_sums(values_ref, rows):
        sums = None
        for start in range(0, values_ref.shape[1], 128):
            part = jnp.square(values_ref[pl.ds(0, rows), start:start + 128].astype(jnp.float32))
            sums = part if sums is None else sums + part
        return sums

    def row_sums(values_ref):
        lanes[pl.ds(lanes.shape[0] - 32, 32), :] = jnp.zeros((32, 128), jnp.float32)
        lanes[pl.ds(0, vocab_rows), :] = lane_sums(values_ref, vocab_rows)
        return jnp.broadcast_to(jnp.sum(lanes[...].T, axis=0, keepdims=True), squares.shape)

    def load_x():
        local[0].wait()
        end = pl.ds(x_pad.shape[0] - 32, 32)
        row = lax.broadcasted_iota(jnp.int32, (32, slab), 0) + (x_pad.shape[0] - 32)
        x_pad[end, :] = jnp.where(row < vocab_rows, x_pad[end, :].astype(jnp.float32), 0.0).astype(jnp.bfloat16)

    def choose(start):
        def body(number, _):
            rows = aligned(start + number * TILE, TILE)
            row = jnp.broadcast_to(tokens_ref[:, rows].astype(jnp.float32), (128, TILE))
            ids = row.T[:, :1].astype(jnp.int32) - place.tensor * vocab_rows
            column = lax.broadcasted_iota(jnp.int32, (TILE, x_pad.shape[0]), 1)
            one = jnp.where((ids == column) & (column < vocab_rows), 1.0, 0.0).astype(jnp.bfloat16)
            masked[rows, :] = jnp.dot(one, x_pad[...], preferred_element_type=jnp.float32).astype(jnp.bfloat16)
            return 0

        lax.fori_loop(0, core_rows // TILE, body, 0)

    def to(link):
        return lambda: place.across(link)

    core_mb = core_rows * slab * 2e-6
    block_mb = core_mb / 4
    flow.send("c1", "c", 0, core_mb, lambda: masked.at[aligned(theirs, core_rows), :], lambda: core_in, to("c"))
    flow.task((), 1.0, load_x, rank=1, name=("x",))
    flow.task((), 1.2, lambda: choose(theirs), ("c1",), rank=1, name=("theirs",), after=(("x",),))
    flow.task((), 1.2, lambda: choose(mine), rank=1, name=("mine",), after=(("theirs",),))

    def add_core():
        rows = aligned(mine, core_rows)
        masked[rows, :] += core_in[...]

    flow.send("r+", "x+", 0, block_mb / 2, lambda: masked.at[rows_of(0, 2, 0), :], lambda: left_in, to("x+"))
    flow.send("r-", "x-", 0, block_mb / 2, lambda: masked.at[rows_of(0, 2, 1), :], lambda: right_in, to("x-"))
    flow.task(("c1",), 0.5, add_core, ("r+", "r-"), rank=1, name=("core",), after=(("mine",),))

    def add_left():
        masked[rows_of(0, 1, 0), :] += left_in[...]

    def add_right():
        masked[rows_of(0, 3, 1), :] += right_in[...]

    flow.send("b+", "x+", 0, block_mb, lambda: masked.at[rows_of(0, 1), :], lambda: left_block, to("x+"))
    flow.send("b-", "x-", 0, block_mb, lambda: masked.at[rows_of(0, 3), :], lambda: right_block, to("x-"))
    flow.task(("r+",), 0.1, add_left, ("b+",), rank=1, after=(("core",),))
    flow.task(("r-",), 0.1, add_right, ("b-",), rank=1, after=(("core",),))

    def add_blocks():
        masked[rows_of(0, 0), :] += left_block[...] + right_block[...]

    flow.send("h1", "h", 0, block_mb / 2, lambda: masked.at[small_rows(1), :], lambda: half_in, to("h"))
    flow.task(("b+", "b-"), 0.2, add_blocks, ("h1",), rank=1, name=("blocks",), after=(("core",),))

    def add_half():
        chosen_all[0] = masked[small_rows(0), :] + half_in[...]

    flow.task(("h1",), 0.1, add_half, rank=1, name=("chosen",), after=(("blocks",),))
    t_from = gather(
        "T", gather_dp("T", 0, True, "y+"), lambda chunk: own_rows * slab * 2e-6, lambda link, chunk: 0,
        lambda rel, chunk: chosen_all.at[slot_of(rel) + 1], lambda there, rel, chunk: chosen_all.at[slot_of(there) + 1],
        lambda chunk: (("chosen",),),
    )

    def grow_chosen(rel, fresh, last):
        at = slot_of(rel) + 1
        columns = e_columns(rel)

        def body(number, _):
            rows = aligned(number * TILE, TILE)
            part = lax.dot_general(
                chosen_all[at], e_all[rows, columns], LAST, preferred_element_type=jnp.float32
            )
            if fresh:
                chosen_sum[:, rows] = part
            else:
                chosen_sum[:, rows] += part
            return 0

        lax.fori_loop(0, tiles, body, 0)
        if last:
            sums = None
            for start in range(0, new_cols, 128):
                part = jnp.square(chosen_sum[:, start:start + 128])
                sums = part if sums is None else sums + part
            lanes[pl.ds(0, own_rows), :] = sums
            lanes[pl.ds(own_rows, 128 - own_rows), :] = jnp.zeros((128 - own_rows, 128), jnp.float32)
            row = jnp.sum(lanes[pl.ds(0, 128), :].T, axis=0, keepdims=True)
            chunk_squares[...] = jnp.broadcast_to(row, chunk_squares.shape)

    def scale_chosen():
        row = chunk_squares[...]
        for number in range(len(DP_PEERS)):
            row = row + chunk_in[number]
        raw_ms = jnp.broadcast_to(row[:1], (128, 128)).T[:own_rows, :1] / new_width
        old_squares = None
        for number in range(N_DP):
            for start in range(0, slab, 128):
                part = jnp.square(chosen_all[number, :, start:start + 128].astype(jnp.float32))
                old_squares = part if old_squares is None else old_squares + part
        old_ms = jnp.sum(old_squares, axis=1, keepdims=True) / old_width
        factor = jnp.sqrt((old_ms + EMBED_EPSILON) / (raw_ms + EMBED_EPSILON))
        scale = factor * lax.rsqrt(factor * factor * raw_ms + TOKEN_EPSILON)
        hidden[small_rows(0), :] = (chosen_sum[...] * scale).astype(jnp.bfloat16)

    chunk_sends = [
        flow.send(
            ("Q", number), "s", 0, 0.004, lambda: chunk_squares, lambda number=number: chunk_in.at[number],
            lambda rel=rel: (place.dp_at(rel), place.tensor),
        )
        for number, rel in enumerate(DP_PEERS)
    ]

    units = []
    flow.task((), 0.1, lambda: local[4].wait(), rank=4, name=("e",))
    for rel in RELS:
        needs = [t_from[(rel, 0)]] if any(rel) else []
        run = counted("chosen", len(RELS), lambda fresh, last, rel=rel: grow_chosen(rel, fresh, last))
        units.append(("chosen", rel))
        flow.task(needs, 0.9, run, rank=1.5, after=(("e",), ("chosen",)), name=units[-1])

    own_mb = own_rows * hidden.shape[1] * 2e-6

    def same(name, link, megabytes, rows):
        return flow.send(
            name, link, 0, megabytes, lambda: hidden.at[rows(), :], lambda: hidden.at[rows(), :], to(link)
        )

    same("h2", "h", own_mb, lambda: small_rows(0))
    same("a+", "x+", 2 * own_mb, lambda: rows_of(0, 0))
    same("a-", "x-", 2 * own_mb, lambda: rows_of(0, 0))
    same("f+", "x+", own_mb, lambda: rows_of(0, 3, 0))
    same("f-", "x-", own_mb, lambda: rows_of(0, 1, 1))
    for shift in range(4):
        same(("c", shift), "c", 2 * own_mb, lambda shift=shift: rows_of(0, shift))
    flow.task((), 0.0, None, chunk_sends, rank=0.5, after=units, name=("chunk",))
    flow.task(chunk_sends, 0.5, scale_chosen, ("h2",), rank=0.5, after=(("chunk",),), name=("hidden",))
    flow.task(("h2",), 0.02, None, ("a+", "a-", ("c", 0)), rank=0.5, after=(("hidden",),))
    flow.task(("a+",), 0.0, None, ("f+", ("c", 3)), rank=0)
    flow.task(("a-",), 0.0, None, ("f-", ("c", 1)), rank=0)
    flow.task(("f+", "f-"), 0.0, None, (("c", 2),), rank=0)

    half = head_cols // 2
    sends = []
    for chunk, (z_first, extra) in enumerate(INNER_MODES):
        sends += gather_dp("I", chunk, z_first, extra)

    def inner_view(ref, chunk):
        return ref.at[chunk // 2, pl.ds((chunk % 2) * half, half), :]

    def i_source(rel, chunk):
        return inner_view(inner_all.at[slot_of(rel)] if any(rel) else inner_own, chunk)

    i_from = gather(
        "I", sends, lambda chunk: half * in_slab * 2e-6, lambda link, chunk: 3 + chunk // 2,
        i_source, lambda there, rel, chunk: inner_view(inner_all.at[slot_of(there)], chunk),
        lambda chunk: (("inner", chunk // 2),),
    )

    def add_grown(rel, matrix, fresh, last):
        columns = e_columns(rel)

        def body(number, _):
            rows = aligned(number * TILE, TILE)
            block = inner_all[slot_of(rel), matrix] if any(rel) else inner_own[matrix]
            part = lax.dot_general(e_all[rows, columns], block, LAST, preferred_element_type=jnp.float32)
            if not fresh:
                part = part + grown_sum[matrix, rows, :]
            if last:
                grown[matrix][rows, :] = part.astype(jnp.bfloat16)
            else:
                grown_sum[matrix, rows, :] = part
            return 0

        lax.fori_loop(0, tiles, body, 0)

    for matrix in range(2):
        units = []
        for rel in RELS:
            needs = [i_from[(rel, chunk)] for chunk in (2 * matrix, 2 * matrix + 1)] if any(rel) else []
            run = counted(
                ("grown", matrix), len(RELS),
                lambda fresh, last, rel=rel, matrix=matrix: add_grown(rel, matrix, fresh, last),
            )
            units.append(("grown", rel, matrix))
            flow.task(needs, 0.9, run, rank=3, after=(("e",), ("inner", matrix)), name=units[-1])
        flow.task((), 0.0, None, rank=3, after=units, name=("grown", matrix))

    def square_rows():
        row = lax.broadcasted_iota(jnp.int32, squares.shape, 0)
        squares[...] = jnp.where(row == 1, row_sums(x_pad), 0.0)
        squares[...] = jnp.where(row == 0, row_sums(raw), squares[...])

    square_sends = [
        flow.send(
            ("S", number), "s", 0, 0.03, lambda: squares, lambda number=number: squares_in.at[number],
            lambda rel=rel: (place.dp_at(rel), place.tensor),
        )
        for number, rel in enumerate(DP_PEERS)
    ]
    flow.task((), 2.5, square_rows, square_sends, rank=4, after=raw_units, name=("squares",))
    ge_cuts = ((0, slab, slot_of((1, 2))), (slab, new_cols - slab, slot_of((0, 2))))

    def ge_copies():
        return [
            pltpu.make_async_copy(
                x_all.at[slot, :, pl.ds(0, size)], ge_ref.at[:, pl.ds(start, size)], local_sem.at[6 + number]
            )
            for number, (start, size, slot) in enumerate(ge_cuts)
        ]

    def rescale():
        flow.wait_left([name for name in flow.sends if name[0] == "X"])
        sums = squares[...]
        for number in range(len(DP_PEERS)):
            sums = sums + squares_in[number]
        factor = jnp.sqrt((sums[1:2] / old_width + EMBED_EPSILON) / (sums[0:1] / new_width + EMBED_EPSILON))
        column = jnp.broadcast_to(factor, (128, factor.shape[1])).T[:vocab_rows]
        for start, size, slot in ge_cuts:
            for at in range(0, size, 128):
                scaled = raw[:, start + at:start + at + 128] * column
                x_all[slot, :, at:at + 128] = scaled.astype(jnp.bfloat16)
        for copy in ge_copies():
            copy.start()

    flow.task(square_sends, 2.5, rescale, rank=5, name=("scaled",), after=(("squares",),))

    def seq_rows(rel):
        return aligned(place.dp_at(rel) * per_seq, per_seq)

    def partial(rel, matrix):
        block = hidden[seq_rows(rel), :]
        return jnp.dot(block, grown[matrix][...], preferred_element_type=jnp.float32)

    def put_query(number, rel):
        q_out[number] = partial(rel, 0).astype(jnp.bfloat16)

    def put_key(number, rel):
        k_out[number] = partial(rel, 1).astype(jnp.bfloat16)

    gathered = ["h2", "a+", "a-", "f+", "f-"] + [("c", shift) for shift in range(4)]
    arrivals = []
    for matrix, (put, out, into) in enumerate(((put_query, q_out, q_in), (put_key, k_out, k_in))):
        for number, rel in enumerate(DP_PEERS):
            name = flow.send(
                ("P", matrix, number), "far", 0, per_seq * out.shape[2] * 2e-6,
                lambda out=out, number=number: out.at[number], lambda into=into, number=number: into.at[number],
                lambda rel=rel: (place.dp_at(rel), place.tensor), PEER_OVER[rel],
            )
            arrivals.append(name)
            flow.task(
                gathered, 0.4, lambda put=put, number=number, rel=rel: put(number, rel), (name,),
                rank=2.5, after=(("grown", matrix), ("hidden",)),
            )

    def keep_own(matrix):
        own_part[:, matrix * head_cols:(matrix + 1) * head_cols] = partial((0, 0), matrix)

    for matrix in range(2):
        flow.task(
            gathered, 0.4, lambda matrix=matrix: keep_own(matrix), rank=3.5,
            after=(("grown", matrix), ("hidden",)), name=("own", matrix),
        )

    def add_up():
        for matrix, into in enumerate((q_in, k_in)):
            columns = pl.ds(matrix * head_cols, head_cols)
            sums = own_part[:, columns]
            for number in range(len(DP_PEERS)):
                sums = sums + into[number].astype(jnp.float32)
            both_ref[:, columns] = sums

    flow.task(arrivals, 1.0, add_up, rank=9, after=(("own", 0), ("own", 1)))
    order = flow.arrange()
    flow.emit(order, send_sem, recv_sem)
    for copy in ge_copies():
        copy.wait()


def grow_and_check(token_ids, old_embed, expand_in, query_out, key_out, old_query, old_key):
    vocab_rows, slab = old_embed.shape
    in_slab, out_slab = old_query.shape
    new_cols = expand_in.shape[0]
    head_cols = query_out.shape[0]
    tokens = token_ids.shape[0]
    padded = -(-vocab_rows // 128) * 128
    per_seq = tokens // N_DP
    turned = jnp.stack([old_query.T, old_key.T])
    anywhere = pl.BlockSpec(memory_space=pl.ANY)
    inside = pl.BlockSpec(memory_space=pltpu.VMEM)
    bf16, f32 = jnp.bfloat16, jnp.float32
    count = (2 * W_PARTS * 15) + 7 * X_CUTS + 7 * len(INNER_MODES) + 7 + 1 + 4 + 1 + 9 + 7 + 14 + 7
    return pl.pallas_call(
        lambda *refs: whole_kernel(D_NEW, *refs),
        out_shape=(
            jax.ShapeDtypeStruct((vocab_rows, new_cols), bf16),
            jax.ShapeDtypeStruct((new_cols, head_cols), bf16),
            jax.ShapeDtypeStruct((new_cols, head_cols), bf16),
            jax.ShapeDtypeStruct((per_seq, 2 * head_cols), f32),
        ),
        in_specs=[anywhere] * 5 + [inside],
        out_specs=(anywhere, inside, inside, inside),
        scratch_shapes=[
            pltpu.VMEM((padded, slab), bf16),
            pltpu.VMEM((N_DP - 1, vocab_rows, slab), bf16),
            pltpu.VMEM((vocab_rows, new_cols), f32),
            pltpu.VMEM((2, N_TENSOR, out_slab, in_slab), bf16),
            pltpu.VMEM(expand_in.shape, bf16),
            pltpu.VMEM((2,) + query_out.shape, bf16),
            pltpu.VMEM((2, head_cols, in_slab), f32),
            pltpu.VMEM((2, head_cols, in_slab), bf16),
            pltpu.VMEM((N_DP - 1, 2, head_cols, in_slab), bf16),
            pltpu.VMEM((2, new_cols, head_cols), f32),
            pltpu.VMEM((padded, 128), f32),
            pltpu.VMEM((8, padded), f32),
            pltpu.VMEM((7, 8, padded), f32),
            pltpu.VMEM((tokens, slab), bf16),
            pltpu.VMEM((tokens // 2, slab), bf16),
            pltpu.VMEM((tokens // 16, slab), bf16),
            pltpu.VMEM((tokens // 16, slab), bf16),
            pltpu.VMEM((tokens // 8, slab), bf16),
            pltpu.VMEM((tokens // 8, slab), bf16),
            pltpu.VMEM((tokens // 16, slab), bf16),
            pltpu.VMEM((N_DP, tokens // 16, slab), bf16),
            pltpu.VMEM((tokens // 16, new_cols), f32),
            pltpu.VMEM((tokens, new_cols), bf16),
            pltpu.VMEM((7, per_seq, head_cols), bf16),
            pltpu.VMEM((7, per_seq, head_cols), bf16),
            pltpu.VMEM((7, per_seq, head_cols), bf16),
            pltpu.VMEM((7, per_seq, head_cols), bf16),
            pltpu.VMEM((per_seq, 2 * head_cols), f32),
            pltpu.VMEM((8, 128), f32),
            pltpu.VMEM((7, 8, 128), f32),
            pltpu.SemaphoreType.DMA((count,)),
            pltpu.SemaphoreType.DMA((count,)),
            pltpu.SemaphoreType.DMA((8,)),
        ],
        compiler_params=pltpu.CompilerParams(
            collective_id=1, has_side_effects=True, vmem_limit_bytes=VMEM_LIMIT
        ),
        name="grow_and_check",
    )(old_embed, turned, expand_in, query_out, key_out, token_ids.reshape(1, tokens))


def rotate(values, head_count):
    row_count = values.shape[0]
    shaped = values.reshape(row_count, head_count, HEAD)
    half_size = HEAD // 2
    position = jnp.arange(row_count).astype(jnp.float32)
    frequency = jnp.exp(
        -math.log(10000.0) * jnp.arange(half_size).astype(jnp.float32) * (2.0 / HEAD)
    )
    angles = position[:, None] * frequency[None, :]
    cosine = jnp.cos(angles)[:, None, :]
    sine_table = jnp.sin(angles)[:, None, :]
    first_half = shaped[..., :half_size]
    second = shaped[..., half_size:]
    return jnp.concatenate(
        [first_half * cosine - second * sine_table, second * cosine + first_half * sine_table],
        axis=-1,
    )


def entropy_of(queries, key_proj, head_count):
    rotated_q = rotate(queries, head_count).astype(jnp.bfloat16)
    rotated_k = rotate(key_proj, head_count).astype(jnp.bfloat16)
    scores = jnp.einsum(
        "ihd,jhd->hij", rotated_q, rotated_k, preferred_element_type=jnp.float32
    ) * HEAD ** (-0.5)
    row_count = queries.shape[0]
    causal = jnp.arange(row_count)[:, None] >= jnp.arange(row_count)[None, :]
    weights = jnp.where(causal[None], jnp.exp(scores), 0.0)
    weight_sum = jnp.sum(weights, axis=-1)
    entropy = jnp.log(weight_sum) - jnp.sum(weights * scores, axis=-1) / weight_sum
    return entropy.T


def on_device(token_ids, old_embed, expand_in, query_out, key_out, old_query, old_key):
    head_cols = query_out.shape[0]
    grown_embedding, grown_query, grown_key, both = grow_and_check(
        token_ids, old_embed, expand_in, query_out, key_out, old_query, old_key
    )
    attention_entropy = entropy_of(both[:, :head_cols], both[:, head_cols:], head_cols // HEAD)
    return (grown_embedding, grown_query, grown_key, attention_entropy)


def solution(mesh):
    placed = (
        P(),
        P("tensor", "dp"),
        P("dp", None),
        P("tensor", None),
        P("tensor", None),
        P("dp", "tensor"),
        P("dp", "tensor"),
    )
    return jax.shard_map(
        on_device,
        mesh=mesh,
        in_specs=placed,
        out_specs=(P("tensor", "dp"), P("dp", "tensor"), P("dp", "tensor"), P("dp", "tensor")),
        check_vma=False,
    )
```

```python
import heapq
import math

import jax
import jax.numpy as jnp
from jax import lax
from jax.experimental import pallas as pl
from jax.experimental.pallas import tpu as pltpu
from jax.sharding import PartitionSpec as P

D_NEW = 8192
HEAD = 128
N_DP = 8
N_TENSOR = 16

EMBED_EPSILON = 1e-06
TOKEN_EPSILON = 1e-05

MESH = pl.DeviceIdType.MESH
LAST = (((1,), (1,)), ((), ()))
VMEM_LIMIT = 67_000_000

STEP = {"y+": 1, "y-": -1, "x+": 1, "x-": -1}


class Place:
    def __init__(self):
        self.dp = lax.axis_index("dp")
        self.tensor = lax.axis_index("tensor")
        self.z_lo = self.dp // 4
        self.y = self.dp % 4
        self.x = self.tensor // 4
        self.z_hi = (self.tensor // 2) % 2
        self.core = self.tensor % 2

    def dp_at(self, rel):
        flip, shift = rel
        z_lo = 1 - self.z_lo if flip else self.z_lo
        return z_lo * 4 + (self.y + shift + 4) % 4

    def tensor_at(self, rel):
        flip, shift, core_flip = rel
        z_hi = 1 - self.z_hi if flip else self.z_hi
        core = 1 - self.core if core_flip else self.core
        return (((self.x + shift + 4) % 4) * 2 + z_hi) * 2 + core

    def across(self, link):
        if link in ("y+", "y-"):
            return (self.dp_at((0, STEP[link])), self.tensor)
        if link == "z":
            return (self.dp_at((1, 0)), self.tensor)
        if link in ("x+", "x-"):
            return (self.dp, self.tensor_at((0, STEP[link], 0)))
        if link == "h":
            return (self.dp, self.tensor_at((1, 0, 0)))
        return (self.dp, self.tensor_at((0, 0, 1)))


def seen_by_receiver(link, rel):
    if link in ("y+", "y-"):
        return (rel[0], (rel[1] - STEP[link]) % 4)
    if link == "z":
        return (1 - rel[0], rel[1])
    if link in ("x+", "x-"):
        return (rel[0], (rel[1] - STEP[link]) % 4, rel[2])
    if link == "h":
        return (1 - rel[0], rel[1], rel[2])
    return (rel[0], rel[1], 1 - rel[2])


def ring_tree(plus, minus, kind, rel, chunk, extra):
    near = (rel[0], (rel[1] - STEP[extra]) % 4) + tuple(rel[2:])
    return [(plus, kind, rel, chunk), (minus, kind, rel, chunk), (extra, kind, near, chunk)]


def gather_dp(kind, chunk, z_first, extra):
    other = "y-" if extra == "y+" else "y+"
    if z_first:
        sends = [("z", kind, (0, 0), chunk)]
        sends += ring_tree("y+", "y-", kind, (0, 0), chunk, extra)
        sends += ring_tree("y+", "y-", kind, (1, 0), chunk, other)
        return sends
    sends = ring_tree("y+", "y-", kind, (0, 0), chunk, extra)
    return sends + [("z", kind, (0, shift), chunk) for shift in (0, 1, 3, 2)]


def gather_tensor(kind, chunk, extra):
    other = "x-" if extra == "x+" else "x+"
    sends = [("h", kind, (0, 0, 0), chunk)]
    sends += ring_tree("x+", "x-", kind, (0, 0, 0), chunk, extra)
    sends += ring_tree("x+", "x-", kind, (1, 0, 0), chunk, other)
    sends += [("c", kind, (flip, shift, 0), chunk) for flip in (0, 1) for shift in (0, 1, 3, 2)]
    return sends


def row_cuts(rows, pieces):
    step = -(-rows // (16 * pieces)) * 16
    return [(start, min(step, rows - start)) for start in range(0, rows, step)]


class Flow:
    def __init__(self):
        self.sends = {}
        self.tasks = []
        self.left_already = set()

    def send(self, name, link, priority, megabytes, source, target, to, over=()):
        assert name not in self.sends
        self.sends[name] = (link, priority, megabytes, source, target, to, over)
        return name

    def task(self, needs, cost, run, sends=(), rank=5, after=(), name=None):
        self.tasks.append((frozenset(needs), cost, run, tuple(sends), rank, frozenset(after), name))

    def arrange(self):
        free, flying, queues = {}, {}, {}
        landed, done, order, heap = set(), set(), [], []
        left = list(range(len(self.tasks)))
        now, serial = 0.0, 0

        def pump(link):
            while queues.get(link) and flying.get(link, 0) < DEPTH.get(link, 1000):
                name = heapq.heappop(queues[link])[2]
                flying[link] = flying.get(link, 0) + 1
                over = self.sends[name][6] + (("z",) if link == "h" else ())
                for each in (link,) + over:
                    free[each] = max(free.get(each, 0.0), now) + self.sends[name][2] / LINK_RATES[each]
                there = max(free[each] for each in (link,) + over)
                heapq.heappush(heap, (there + LATENCY.get(link, HOP), len(order), name))
                order.append(("start", name))

        while left or heap:
            if heap and heap[0][0] <= now:
                name = heapq.heappop(heap)[2]
                link = self.sends[name][0]
                landed.add(name)
                flying[link] -= 1
                order.append(("arrive", name))
                now += 0.03
                for number in list(left):
                    needs, cost, run, sends, rank, after, _ = self.tasks[number]
                    if rank == 0 and name in needs and needs <= landed and after <= done:
                        left.remove(number)
                        for send in sends:
                            serial += 1
                            put = (self.sends[send][1], serial, send)
                            heapq.heappush(queues.setdefault(self.sends[send][0], []), put)
                for other in sorted(queues):
                    pump(other)
                continue
            ready = []
            for number in left:
                needs, _, _, _, rank, after, _ = self.tasks[number]
                if after <= done and needs <= landed:
                    ready.append((rank, number))
            if not ready:
                assert heap
                now = max(now, heap[0][0])
                continue
            number = min(ready)[1]
            left.remove(number)
            order.append(("run", number))
            _, cost, _, sends, _, _, name = self.tasks[number]
            now += cost
            if name is not None:
                done.add(name)
            for send in sends:
                serial += 1
                put = (self.sends[send][1], serial, send)
                heapq.heappush(queues.setdefault(self.sends[send][0], []), put)
            for other in sorted(queues):
                pump(other)
        self.length = now
        assert not any(queues.values())
        return order

    def copy_of(self, name):
        _, _, _, source, target, to, _ = self.sends[name]
        number = self.number_of[name]
        return pltpu.make_async_remote_copy(
            src_ref=source(),
            dst_ref=target(),
            send_sem=self.send_sem.at[number],
            recv_sem=self.recv_sem.at[number],
            device_id=to(),
            device_id_type=MESH,
        )

    def wait_left(self, names):
        for name in names:
            if name not in self.left_already:
                self.left_already.add(name)
                self.copy_of(name).wait_send()

    def emit(self, order, send_sem, recv_sem):
        self.number_of = {name: number for number, name in enumerate(self.sends)}
        self.send_sem, self.recv_sem = send_sem, recv_sem
        arrived, started = set(), set()
        needed = {send: needs for needs, _, _, sends, _, _, _ in self.tasks for send in sends}

        def wait_for(names):
            for name in sorted(names - arrived, key=str):
                self.copy_of(name).wait_recv()
                arrived.add(name)

        for what, which in order:
            if what == "start":
                wait_for(needed[which])
                self.copy_of(which).start()
                started.add(which)
            elif what == "run":
                wait_for(self.tasks[which][0])
                if self.tasks[which][2] is not None:
                    self.tasks[which][2]()
        wait_for(set(self.sends))
        assert arrived == set(self.sends) and started == set(self.sends)
        self.wait_left(list(self.sends))


DEPTH = {"y+": 3, "y-": 3, "z": 3, "x+": 2, "x-": 2, "h": 2}
LINK_RATES = {
    "y+": 0.0455, "y-": 0.0455, "z": 0.0455, "x+": 0.0455, "x-": 0.0455, "h": 0.0455, "c": 0.12, "far": 0.5, "s": 0.2,
}
HOP = 2.5
LATENCY = {"h": 3.5}
PEER_OVER = {
    (1, 2): ("z", "y+"), (0, 2): ("y+", "y-"), (1, 1): ("z", "y+"), (1, 3): ("z", "y-"),
    (1, 0): ("z",), (0, 1): ("y+",), (0, 3): ("y-",),
}
DP_PEERS = ((1, 2), (0, 2), (1, 1), (1, 3), (1, 0), (0, 1), (0, 3))
W_PARTS = 2
X_CUTS = 7
X_MODES = ((False, "y+"), (False, "y-"), (True, "y+"), (True, "y-"), (True, "y+"), (True, "y-"), (True, "y+"))
INNER_MODES = ((True, "y+"), (False, "y-"), (True, "y-"), (False, "y+"))
RELS = [(flip, shift) for flip in (0, 1) for shift in (0, 1, 3, 2)]
TILE = 256


def slot_of(rel):
    return rel[0] * 4 + rel[1] - 1


def aligned(start, size):
    return pl.ds(pl.multiple_of(start, size), size)


def whole_kernel(
    sizes, x_ref, wq_ref, wk_ref, e_ref, q_ref, k_ref, tokens_ref,
    ge_ref, gq_ref, gk_ref, queries_ref, keys_ref,
    x_pad, x_all, raw, w_all, e_all, o_all, total, inner_own, inner_all, grown_sum,
    lanes, squares, squares_in,
    masked, core_in, left_in, right_in, left_block, right_block, half_in, chosen_all, chosen_sum, hidden,
    q_out, q_in, k_out, k_in, own_part, chunk_squares, chunk_in,
    send_sem, recv_sem, local_sem,
):
    place = Place()
    vocab_rows, slab = x_ref.shape
    new_cols, old_width = e_ref.shape
    new_width = sizes
    head_cols = q_ref.shape[0]
    token_rows = tokens_ref.shape[1]
    turned = (wq_ref, wk_ref)
    out_slab, in_slab = wq_ref.shape
    grown = (gq_ref, gk_ref)
    per_seq = queries_ref.shape[0]
    cuts = row_cuts(vocab_rows, X_CUTS)
    assert len(cuts) == X_CUTS

    barrier = pltpu.get_barrier_semaphore()
    friends = [place.across(link) for link in ("x+", "x-", "h", "c")]
    friends += [(place.dp_at(rel), place.tensor) for rel in DP_PEERS]
    for friend in friends:
        pl.semaphore_signal(barrier, inc=1, device_id=friend, device_id_type=MESH)
    local = [
        pltpu.make_async_copy(x_ref, x_pad.at[pl.ds(0, vocab_rows), :], local_sem.at[0]),
        pltpu.make_async_copy(wq_ref, w_all.at[0, place.tensor], local_sem.at[1]),
        pltpu.make_async_copy(wk_ref, w_all.at[1, place.tensor], local_sem.at[2]),
        pltpu.make_async_copy(q_ref, o_all.at[0], local_sem.at[3]),
        pltpu.make_async_copy(e_ref, e_all, local_sem.at[4]),
        pltpu.make_async_copy(k_ref, o_all.at[1], local_sem.at[5]),
    ]
    for copy in local:
        copy.start()
    pl.semaphore_wait(barrier, len(friends))

    flow = Flow()

    def gather(kind, sends, megabytes, priority, source, target, ready):
        brought = {}
        for link, _, rel, chunk in sends:
            brought[(seen_by_receiver(link, rel), chunk)] = (kind, link, rel, chunk)
        first, after = {}, {}
        for link, _, rel, chunk in sends:
            name = flow.send(
                (kind, link, rel, chunk), link, priority(link, chunk), megabytes(chunk),
                lambda rel=rel, chunk=chunk: source(rel, chunk),
                lambda link=link, rel=rel, chunk=chunk: target(seen_by_receiver(link, rel), rel, chunk),
                lambda link=link: place.across(link),
            )
            if (rel, chunk) in brought:
                after.setdefault(brought[(rel, chunk)], []).append(name)
            else:
                assert not any(rel)
                first.setdefault(ready(chunk), []).append(name)
        for cause, names in first.items():
            flow.task((), 0.05, None, names, rank=0.5, after=cause)
        for cause, names in after.items():
            flow.task((cause,), 0.0, None, names, rank=0)
        return brought

    sends = []
    for chunk in range(2 * W_PARTS):
        sends += gather_tensor("W", chunk, ("x+", "x-")[chunk % 2])
    w_rows = out_slab // W_PARTS

    def w_view(ref, chunk):
        return ref.at[pl.ds((chunk % W_PARTS) * w_rows, w_rows), :]

    def w_target(rel, chunk):
        return w_view(w_all.at[chunk // W_PARTS, place.tensor_at(rel)], chunk)

    w_from = gather(
        "W", sends, lambda chunk: w_rows * in_slab * 2e-6, lambda link, chunk: 1 + chunk // W_PARTS,
        lambda rel, chunk: w_target(rel, chunk) if any(rel) else w_view(turned[chunk // W_PARTS], chunk),
        lambda _, rel, chunk: w_target(rel, chunk), lambda chunk: (),
    )

    sends = []
    for chunk, (z_first, extra) in enumerate(X_MODES):
        sends += gather_dp("X", chunk, z_first, extra)

    def x_source(rel, chunk):
        rows = pl.ds(*cuts[chunk])
        return x_ref.at[rows, :] if not any(rel) else x_all.at[slot_of(rel), rows, :]

    x_from = gather(
        "X", sends, lambda chunk: cuts[chunk][1] * slab * 2e-6,
        lambda link, chunk: 10 + (link == "z" and not X_MODES[chunk][0]),
        x_source, lambda there, rel, chunk: x_all.at[slot_of(there), pl.ds(*cuts[chunk]), :], lambda chunk: (),
    )

    pair = 2 * out_slab

    def add_inner(rel, matrix, fresh, last):
        chip = place.tensor_at((rel[0], rel[1], 0)) // 2
        slabs = w_all[matrix, pl.ds(chip * 2, 2)].reshape(pair, in_slab)
        part = jnp.dot(o_all[matrix, :, aligned(chip * pair, pair)], slabs, preferred_element_type=jnp.float32)
        if not fresh:
            part = part + total[matrix]
        if last:
            inner_own[matrix] = part.astype(jnp.bfloat16)
        else:
            total[matrix] = part

    counts = {}

    def counted(key, times, run):
        def go():
            counts[key] = counts.get(key, 0) + 1
            run(counts[key] == 1, counts[key] == times)

        return go

    flow.task((), 0.3, lambda: [local[number].wait() for number in (1, 2, 3, 5)], rank=2, name=("w",))
    for matrix in range(2):
        units = []
        for rel in RELS:
            needs = [
                w_from[(rel + (core,), matrix * W_PARTS + part)]
                for core in (0, 1) for part in range(W_PARTS) if any(rel) or core
            ]
            units.append(("inner", rel, matrix))
            run = counted(
                ("inner", matrix), len(RELS),
                lambda fresh, last, rel=rel, matrix=matrix: add_inner(rel, matrix, fresh, last),
            )
            flow.task(needs, 0.6, run, rank=2 + matrix, after=(("w",),), name=units[-1])
        flow.task((), 0.0, None, rank=2, after=units, name=("inner", matrix))

    tiles = new_cols // TILE

    def e_columns(rel):
        return pl.ds(pl.multiple_of(place.dp_at(rel) * slab, 128), slab)

    def add_raw(rel, half, fresh):
        columns = e_columns(rel)

        def body(number, _):
            rows = aligned(number * TILE, TILE)
            block = x_all[slot_of(rel)] if any(rel) else x_pad[pl.ds(0, vocab_rows), :]
            part = lax.dot_general(block, e_all[rows, columns], LAST, preferred_element_type=jnp.float32)
            if fresh:
                raw[:, rows] = part
            else:
                raw[:, rows] += part
            return 0

        lax.fori_loop(half * tiles // 2, (half + 1) * tiles // 2, body, 0)

    raw_units = []
    for rel in RELS:
        for half in range(2):
            needs = [x_from[(rel, chunk)] for chunk in range(X_CUTS)] if any(rel) else []
            run = counted(
                ("raw", half), len(RELS), lambda fresh, last, rel=rel, half=half: add_raw(rel, half, fresh)
            )
            raw_units.append(("raw", rel, half))
            flow.task(needs, 1.3, run, rank=6, after=(("e",),), name=raw_units[-1])

    core_rows, chip_rows, own_rows = token_rows // 2, token_rows // 8, token_rows // 16
    mine = place.core * core_rows
    theirs = (1 - place.core) * core_rows

    def rows_of(core, shift, part=None):
        start = (1 - place.core if core else place.core) * core_rows + ((place.x + shift + 4) % 4) * chip_rows
        if part is None:
            return aligned(start, chip_rows)
        return aligned(start + part * own_rows, own_rows)

    def small_rows(flip):
        z_hi = 1 - place.z_hi if flip else place.z_hi
        return aligned(mine + place.x * chip_rows + z_hi * own_rows, own_rows)

    def lane_sums(values_ref, rows):
        sums = None
        for start in range(0, values_ref.shape[1], 128):
            part = jnp.square(values_ref[pl.ds(0, rows), start:start + 128].astype(jnp.float32))
            sums = part if sums is None else sums + part
        return sums

    def row_sums(values_ref):
        lanes[pl.ds(lanes.shape[0] - 32, 32), :] = jnp.zeros((32, 128), jnp.float32)
        lanes[pl.ds(0, vocab_rows), :] = lane_sums(values_ref, vocab_rows)
        return jnp.broadcast_to(jnp.sum(lanes[...].T, axis=0, keepdims=True), squares.shape)

    def load_x():
        local[0].wait()
        end = pl.ds(x_pad.shape[0] - 32, 32)
        row = lax.broadcasted_iota(jnp.int32, (32, slab), 0) + (x_pad.shape[0] - 32)
        x_pad[end, :] = jnp.where(row < vocab_rows, x_pad[end, :].astype(jnp.float32), 0.0).astype(jnp.bfloat16)

    def choose(start):
        def body(number, _):
            rows = aligned(start + number * TILE, TILE)
            row = jnp.broadcast_to(tokens_ref[:, rows].astype(jnp.float32), (128, TILE))
            ids = row.T[:, :1].astype(jnp.int32) - place.tensor * vocab_rows
            column = lax.broadcasted_iota(jnp.int32, (TILE, x_pad.shape[0]), 1)
            one = jnp.where((ids == column) & (column < vocab_rows), 1.0, 0.0).astype(jnp.bfloat16)
            masked[rows, :] = jnp.dot(one, x_pad[...], preferred_element_type=jnp.float32).astype(jnp.bfloat16)
            return 0

        lax.fori_loop(0, core_rows // TILE, body, 0)

    def to(link):
        return lambda: place.across(link)

    core_mb = core_rows * slab * 2e-6
    block_mb = core_mb / 4
    flow.send("c1", "c", 0, core_mb, lambda: masked.at[aligned(theirs, core_rows), :], lambda: core_in, to("c"))
    flow.task((), 1.0, load_x, rank=1, name=("x",))
    flow.task((), 1.2, lambda: choose(theirs), ("c1",), rank=1, name=("theirs",), after=(("x",),))
    flow.task((), 1.2, lambda: choose(mine), rank=1, name=("mine",), after=(("theirs",),))

    def add_core():
        rows = aligned(mine, core_rows)
        masked[rows, :] += core_in[...]

    flow.send("r+", "x+", 0, block_mb / 2, lambda: masked.at[rows_of(0, 2, 0), :], lambda: left_in, to("x+"))
    flow.send("r-", "x-", 0, block_mb / 2, lambda: masked.at[rows_of(0, 2, 1), :], lambda: right_in, to("x-"))
    flow.task(("c1",), 0.5, add_core, ("r+", "r-"), rank=1, name=("core",), after=(("mine",),))

    def add_left():
        masked[rows_of(0, 1, 0), :] += left_in[...]

    def add_right():
        masked[rows_of(0, 3, 1), :] += right_in[...]

    flow.send("b+", "x+", 0, block_mb, lambda: masked.at[rows_of(0, 1), :], lambda: left_block, to("x+"))
    flow.send("b-", "x-", 0, block_mb, lambda: masked.at[rows_of(0, 3), :], lambda: right_block, to("x-"))
    flow.task(("r+",), 0.1, add_left, ("b+",), rank=1, after=(("core",),))
    flow.task(("r-",), 0.1, add_right, ("b-",), rank=1, after=(("core",),))

    def add_blocks():
        masked[rows_of(0, 0), :] += left_block[...] + right_block[...]

    flow.send("h1", "h", 0, block_mb / 2, lambda: masked.at[small_rows(1), :], lambda: half_in, to("h"))
    flow.task(("b+", "b-"), 0.2, add_blocks, ("h1",), rank=1, name=("blocks",), after=(("core",),))

    def add_half():
        chosen_all[0] = masked[small_rows(0), :] + half_in[...]

    flow.task(("h1",), 0.1, add_half, rank=1, name=("chosen",), after=(("blocks",),))
    t_from = gather(
        "T", gather_dp("T", 0, True, "y+"), lambda chunk: own_rows * slab * 2e-6, lambda link, chunk: 0,
        lambda rel, chunk: chosen_all.at[slot_of(rel) + 1], lambda there, rel, chunk: chosen_all.at[slot_of(there) + 1],
        lambda chunk: (("chosen",),),
    )

    def grow_chosen(rel, fresh, last):
        at = slot_of(rel) + 1
        columns = e_columns(rel)

        def body(number, _):
            rows = aligned(number * TILE, TILE)
            part = lax.dot_general(
                chosen_all[at], e_all[rows, columns], LAST, preferred_element_type=jnp.float32
            )
            if fresh:
                chosen_sum[:, rows] = part
            else:
                chosen_sum[:, rows] += part
            return 0

        lax.fori_loop(0, tiles, body, 0)
        if last:
            sums = None
            for start in range(0, new_cols, 128):
                part = jnp.square(chosen_sum[:, start:start + 128])
                sums = part if sums is None else sums + part
            lanes[pl.ds(0, own_rows), :] = sums
            lanes[pl.ds(own_rows, 128 - own_rows), :] = jnp.zeros((128 - own_rows, 128), jnp.float32)
            row = jnp.sum(lanes[pl.ds(0, 128), :].T, axis=0, keepdims=True)
            chunk_squares[...] = jnp.broadcast_to(row, chunk_squares.shape)

    def scale_chosen():
        row = chunk_squares[...]
        for number in range(len(DP_PEERS)):
            row = row + chunk_in[number]
        raw_ms = jnp.broadcast_to(row[:1], (128, 128)).T[:own_rows, :1] / new_width
        old_squares = None
        for number in range(N_DP):
            for start in range(0, slab, 128):
                part = jnp.square(chosen_all[number, :, start:start + 128].astype(jnp.float32))
                old_squares = part if old_squares is None else old_squares + part
        old_ms = jnp.sum(old_squares, axis=1, keepdims=True) / old_width
        factor = jnp.sqrt((old_ms + EMBED_EPSILON) / (raw_ms + EMBED_EPSILON))
        scale = factor * lax.rsqrt(factor * factor * raw_ms + TOKEN_EPSILON)
        hidden[small_rows(0), :] = (chosen_sum[...] * scale).astype(jnp.bfloat16)

    chunk_sends = [
        flow.send(
            ("Q", number), "s", 0, 0.004, lambda: chunk_squares, lambda number=number: chunk_in.at[number],
            lambda rel=rel: (place.dp_at(rel), place.tensor),
        )
        for number, rel in enumerate(DP_PEERS)
    ]

    units = []
    flow.task((), 0.1, lambda: local[4].wait(), rank=4, name=("e",))
    for rel in RELS:
        needs = [t_from[(rel, 0)]] if any(rel) else []
        run = counted("chosen", len(RELS), lambda fresh, last, rel=rel: grow_chosen(rel, fresh, last))
        units.append(("chosen", rel))
        flow.task(needs, 0.9, run, rank=1.5, after=(("e",), ("chosen",)), name=units[-1])

    own_mb = own_rows * hidden.shape[1] * 2e-6

    def same(name, link, megabytes, rows):
        return flow.send(
            name, link, 0, megabytes, lambda: hidden.at[rows(), :], lambda: hidden.at[rows(), :], to(link)
        )

    same("h2", "h", own_mb, lambda: small_rows(0))
    same("a+", "x+", 2 * own_mb, lambda: rows_of(0, 0))
    same("a-", "x-", 2 * own_mb, lambda: rows_of(0, 0))
    same("f+", "x+", own_mb, lambda: rows_of(0, 3, 0))
    same("f-", "x-", own_mb, lambda: rows_of(0, 1, 1))
    for shift in range(4):
        same(("c", shift), "c", 2 * own_mb, lambda shift=shift: rows_of(0, shift))
    flow.task((), 0.0, None, chunk_sends, rank=0.5, after=units, name=("chunk",))
    flow.task(chunk_sends, 0.5, scale_chosen, ("h2",), rank=0.5, after=(("chunk",),), name=("hidden",))
    flow.task(("h2",), 0.02, None, ("a+", "a-", ("c", 0)), rank=0.5, after=(("hidden",),))
    flow.task(("a+",), 0.0, None, ("f+", ("c", 3)), rank=0)
    flow.task(("a-",), 0.0, None, ("f-", ("c", 1)), rank=0)
    flow.task(("f+", "f-"), 0.0, None, (("c", 2),), rank=0)

    half = head_cols // 2
    sends = []
    for chunk, (z_first, extra) in enumerate(INNER_MODES):
        sends += gather_dp("I", chunk, z_first, extra)

    def inner_view(ref, chunk):
        return ref.at[chunk // 2, pl.ds((chunk % 2) * half, half), :]

    def i_source(rel, chunk):
        return inner_view(inner_all.at[slot_of(rel)] if any(rel) else inner_own, chunk)

    i_from = gather(
        "I", sends, lambda chunk: half * in_slab * 2e-6, lambda link, chunk: 3 + chunk // 2,
        i_source, lambda there, rel, chunk: inner_view(inner_all.at[slot_of(there)], chunk),
        lambda chunk: (("inner", chunk // 2),),
    )

    def add_grown(rel, matrix, fresh, last):
        columns = e_columns(rel)

        def body(number, _):
            rows = aligned(number * TILE, TILE)
            block = inner_all[slot_of(rel), matrix] if any(rel) else inner_own[matrix]
            part = lax.dot_general(e_all[rows, columns], block, LAST, preferred_element_type=jnp.float32)
            if not fresh:
                part = part + grown_sum[matrix, rows, :]
            if last:
                grown[matrix][rows, :] = part.astype(jnp.bfloat16)
            else:
                grown_sum[matrix, rows, :] = part
            return 0

        lax.fori_loop(0, tiles, body, 0)

    for matrix in range(2):
        units = []
        for rel in RELS:
            needs = [i_from[(rel, chunk)] for chunk in (2 * matrix, 2 * matrix + 1)] if any(rel) else []
            run = counted(
                ("grown", matrix), len(RELS),
                lambda fresh, last, rel=rel, matrix=matrix: add_grown(rel, matrix, fresh, last),
            )
            units.append(("grown", rel, matrix))
            flow.task(needs, 0.9, run, rank=3, after=(("e",), ("inner", matrix)), name=units[-1])
        flow.task((), 0.0, None, rank=3, after=units, name=("grown", matrix))

    def square_rows():
        row = lax.broadcasted_iota(jnp.int32, squares.shape, 0)
        squares[...] = jnp.where(row == 1, row_sums(x_pad), 0.0)
        squares[...] = jnp.where(row == 0, row_sums(raw), squares[...])

    square_sends = [
        flow.send(
            ("S", number), "s", 0, 0.03, lambda: squares, lambda number=number: squares_in.at[number],
            lambda rel=rel: (place.dp_at(rel), place.tensor),
        )
        for number, rel in enumerate(DP_PEERS)
    ]
    flow.task((), 2.5, square_rows, square_sends, rank=4, after=raw_units, name=("squares",))
    ge_cuts = ((0, slab, slot_of((1, 2))), (slab, new_cols - slab, slot_of((0, 2))))

    def ge_copies():
        return [
            pltpu.make_async_copy(
                x_all.at[slot, :, pl.ds(0, size)], ge_ref.at[:, pl.ds(start, size)], local_sem.at[6 + number]
            )
            for number, (start, size, slot) in enumerate(ge_cuts)
        ]

    def rescale():
        flow.wait_left([name for name in flow.sends if name[0] == "X"])
        sums = squares[...]
        for number in range(len(DP_PEERS)):
            sums = sums + squares_in[number]
        factor = jnp.sqrt((sums[1:2] / old_width + EMBED_EPSILON) / (sums[0:1] / new_width + EMBED_EPSILON))
        column = jnp.broadcast_to(factor, (128, factor.shape[1])).T[:vocab_rows]
        for start, size, slot in ge_cuts:
            for at in range(0, size, 128):
                scaled = raw[:, start + at:start + at + 128] * column
                x_all[slot, :, at:at + 128] = scaled.astype(jnp.bfloat16)
        for copy in ge_copies():
            copy.start()

    flow.task(square_sends, 2.5, rescale, rank=5, name=("scaled",), after=(("squares",),))

    def seq_rows(rel):
        return aligned(place.dp_at(rel) * per_seq, per_seq)

    def partial(rel, matrix):
        block = hidden[seq_rows(rel), :]
        return jnp.dot(block, grown[matrix][...], preferred_element_type=jnp.float32)

    def put_query(number, rel):
        q_out[number] = partial(rel, 0).astype(jnp.bfloat16)

    def put_key(number, rel):
        k_out[number] = partial(rel, 1).astype(jnp.bfloat16)

    gathered = ["h2", "a+", "a-", "f+", "f-"] + [("c", shift) for shift in range(4)]
    arrivals = []
    for matrix, (put, out, into) in enumerate(((put_query, q_out, q_in), (put_key, k_out, k_in))):
        for number, rel in enumerate(DP_PEERS):
            name = flow.send(
                ("P", matrix, number), "far", 0, per_seq * out.shape[2] * 2e-6,
                lambda out=out, number=number: out.at[number], lambda into=into, number=number: into.at[number],
                lambda rel=rel: (place.dp_at(rel), place.tensor), PEER_OVER[rel],
            )
            arrivals.append(name)
            flow.task(
                gathered, 0.4, lambda put=put, number=number, rel=rel: put(number, rel), (name,),
                rank=2.5, after=(("grown", matrix), ("hidden",)),
            )

    def keep_own(matrix):
        own_part[:, matrix * head_cols:(matrix + 1) * head_cols] = partial((0, 0), matrix)

    for matrix in range(2):
        flow.task(
            gathered, 0.4, lambda matrix=matrix: keep_own(matrix), rank=3.5,
            after=(("grown", matrix), ("hidden",)), name=("own", matrix),
        )

    def add_up():
        for matrix, into in enumerate((q_in, k_in)):
            columns = pl.ds(matrix * head_cols, head_cols)
            sums = own_part[:, columns]
            for number in range(len(DP_PEERS)):
                sums = sums + into[number].astype(jnp.float32)
            (queries_ref, keys_ref)[matrix][...] = sums

    flow.task(arrivals, 1.0, add_up, rank=9, after=(("own", 0), ("own", 1)))
    order = flow.arrange()
    flow.emit(order, send_sem, recv_sem)
    for copy in ge_copies():
        copy.wait()


def grow_and_check(token_ids, old_embed, expand_in, query_out, key_out, old_query, old_key):
    vocab_rows, slab = old_embed.shape
    in_slab, out_slab = old_query.shape
    new_cols = expand_in.shape[0]
    head_cols = query_out.shape[0]
    tokens = token_ids.shape[0]
    padded = -(-vocab_rows // 128) * 128
    per_seq = tokens // N_DP
    anywhere = pl.BlockSpec(memory_space=pl.ANY)
    inside = pl.BlockSpec(memory_space=pltpu.VMEM)
    bf16, f32 = jnp.bfloat16, jnp.float32
    count = (2 * W_PARTS * 15) + 7 * X_CUTS + 7 * len(INNER_MODES) + 7 + 1 + 4 + 1 + 9 + 7 + 14 + 7
    return pl.pallas_call(
        lambda *refs: whole_kernel(D_NEW, *refs),
        out_shape=(
            jax.ShapeDtypeStruct((vocab_rows, new_cols), bf16),
            jax.ShapeDtypeStruct((new_cols, head_cols), bf16),
            jax.ShapeDtypeStruct((new_cols, head_cols), bf16),
            jax.ShapeDtypeStruct((per_seq, head_cols), f32),
            jax.ShapeDtypeStruct((per_seq, head_cols), f32),
        ),
        in_specs=[anywhere] * 6 + [inside],
        out_specs=(anywhere, inside, inside, inside, inside),
        scratch_shapes=[
            pltpu.VMEM((padded, slab), bf16),
            pltpu.VMEM((N_DP - 1, vocab_rows, slab), bf16),
            pltpu.VMEM((vocab_rows, new_cols), f32),
            pltpu.VMEM((2, N_TENSOR, out_slab, in_slab), bf16),
            pltpu.VMEM(expand_in.shape, bf16),
            pltpu.VMEM((2,) + query_out.shape, bf16),
            pltpu.VMEM((2, head_cols, in_slab), f32),
            pltpu.VMEM((2, head_cols, in_slab), bf16),
            pltpu.VMEM((N_DP - 1, 2, head_cols, in_slab), bf16),
            pltpu.VMEM((2, new_cols, head_cols), f32),
            pltpu.VMEM((padded, 128), f32),
            pltpu.VMEM((8, padded), f32),
            pltpu.VMEM((7, 8, padded), f32),
            pltpu.VMEM((tokens, slab), bf16),
            pltpu.VMEM((tokens // 2, slab), bf16),
            pltpu.VMEM((tokens // 16, slab), bf16),
            pltpu.VMEM((tokens // 16, slab), bf16),
            pltpu.VMEM((tokens // 8, slab), bf16),
            pltpu.VMEM((tokens // 8, slab), bf16),
            pltpu.VMEM((tokens // 16, slab), bf16),
            pltpu.VMEM((N_DP, tokens // 16, slab), bf16),
            pltpu.VMEM((tokens // 16, new_cols), f32),
            pltpu.VMEM((tokens, new_cols), bf16),
            pltpu.VMEM((7, per_seq, head_cols), bf16),
            pltpu.VMEM((7, per_seq, head_cols), bf16),
            pltpu.VMEM((7, per_seq, head_cols), bf16),
            pltpu.VMEM((7, per_seq, head_cols), bf16),
            pltpu.VMEM((per_seq, 2 * head_cols), f32),
            pltpu.VMEM((8, 128), f32),
            pltpu.VMEM((7, 8, 128), f32),
            pltpu.SemaphoreType.DMA((count,)),
            pltpu.SemaphoreType.DMA((count,)),
            pltpu.SemaphoreType.DMA((8,)),
        ],
        compiler_params=pltpu.CompilerParams(
            collective_id=1, has_side_effects=True, vmem_limit_bytes=VMEM_LIMIT
        ),
        name="grow_and_check",
    )(old_embed, old_query.T, old_key.T, expand_in, query_out, key_out, token_ids.reshape(1, tokens))


def rotate(values, head_count):
    row_count = values.shape[0]
    shaped = values.reshape(row_count, head_count, HEAD)
    half_size = HEAD // 2
    position = jnp.arange(row_count).astype(jnp.float32)
    frequency = jnp.exp(
        -math.log(10000.0) * jnp.arange(half_size).astype(jnp.float32) * (2.0 / HEAD)
    )
    angles = position[:, None] * frequency[None, :]
    cosine = jnp.cos(angles)[:, None, :]
    sine_table = jnp.sin(angles)[:, None, :]
    first_half = shaped[..., :half_size]
    second = shaped[..., half_size:]
    return jnp.concatenate(
        [first_half * cosine - second * sine_table, second * cosine + first_half * sine_table],
        axis=-1,
    )


def entropy_of(queries, key_proj, head_count):
    rotated_q = rotate(queries, head_count).astype(jnp.bfloat16)
    rotated_k = rotate(key_proj, head_count).astype(jnp.bfloat16)
    scores = jnp.einsum(
        "ihd,jhd->hij", rotated_q, rotated_k, preferred_element_type=jnp.float32
    ) * HEAD ** (-0.5)
    row_count = queries.shape[0]
    causal = jnp.arange(row_count)[:, None] >= jnp.arange(row_count)[None, :]
    weights = jnp.where(causal[None], jnp.exp(scores), 0.0)
    weight_sum = jnp.sum(weights, axis=-1)
    entropy = jnp.log(weight_sum) - jnp.sum(weights * scores, axis=-1) / weight_sum
    return entropy.T


def on_device(token_ids, old_embed, expand_in, query_out, key_out, old_query, old_key):
    head_cols = query_out.shape[0]
    grown_embedding, grown_query, grown_key, queries, keys = grow_and_check(
        token_ids, old_embed, expand_in, query_out, key_out, old_query, old_key
    )
    attention_entropy = entropy_of(queries, keys, head_cols // HEAD)
    return (grown_embedding, grown_query, grown_key, attention_entropy)


def solution(mesh):
    placed = (
        P(),
        P("tensor", "dp"),
        P("dp", None),
        P("tensor", None),
        P("tensor", None),
        P("dp", "tensor"),
        P("dp", "tensor"),
    )
    return jax.shard_map(
        on_device,
        mesh=mesh,
        in_specs=placed,
        out_specs=(P("tensor", "dp"), P("dp", "tensor"), P("dp", "tensor"), P("dp", "tensor")),
        check_vma=False,
    )
```

```python
import heapq
import math

import jax
import jax.numpy as jnp
from jax import lax
from jax.experimental import pallas as pl
from jax.experimental.pallas import tpu as pltpu
from jax.sharding import PartitionSpec as P

D_NEW = 8192
HEAD = 128
N_DP = 8
N_TENSOR = 16

EMBED_EPSILON = 1e-06
TOKEN_EPSILON = 1e-05

MESH = pl.DeviceIdType.MESH
LAST = (((1,), (1,)), ((), ()))
VMEM_LIMIT = 67_000_000

STEP = {"y+": 1, "y-": -1, "x+": 1, "x-": -1}


class Place:
    def __init__(self):
        self.dp = lax.axis_index("dp")
        self.tensor = lax.axis_index("tensor")
        self.z_lo = self.dp // 4
        self.y = self.dp % 4
        self.x = self.tensor // 4
        self.z_hi = (self.tensor // 2) % 2
        self.core = self.tensor % 2

    def dp_at(self, rel):
        flip, shift = rel
        z_lo = 1 - self.z_lo if flip else self.z_lo
        return z_lo * 4 + (self.y + shift + 4) % 4

    def tensor_at(self, rel):
        flip, shift, core_flip = rel
        z_hi = 1 - self.z_hi if flip else self.z_hi
        core = 1 - self.core if core_flip else self.core
        return (((self.x + shift + 4) % 4) * 2 + z_hi) * 2 + core

    def across(self, link):
        if link in ("y+", "y-"):
            return (self.dp_at((0, STEP[link])), self.tensor)
        if link == "z":
            return (self.dp_at((1, 0)), self.tensor)
        if link in ("x+", "x-"):
            return (self.dp, self.tensor_at((0, STEP[link], 0)))
        if link == "h":
            return (self.dp, self.tensor_at((1, 0, 0)))
        return (self.dp, self.tensor_at((0, 0, 1)))


def seen_by_receiver(link, rel):
    if link in ("y+", "y-"):
        return (rel[0], (rel[1] - STEP[link]) % 4)
    if link == "z":
        return (1 - rel[0], rel[1])
    if link in ("x+", "x-"):
        return (rel[0], (rel[1] - STEP[link]) % 4, rel[2])
    if link == "h":
        return (1 - rel[0], rel[1], rel[2])
    return (rel[0], rel[1], 1 - rel[2])


def ring_tree(plus, minus, kind, rel, chunk, extra):
    near = (rel[0], (rel[1] - STEP[extra]) % 4) + tuple(rel[2:])
    return [(plus, kind, rel, chunk), (minus, kind, rel, chunk), (extra, kind, near, chunk)]


def gather_dp(kind, chunk, z_first, extra):
    other = "y-" if extra == "y+" else "y+"
    if z_first:
        sends = [("z", kind, (0, 0), chunk)]
        sends += ring_tree("y+", "y-", kind, (0, 0), chunk, extra)
        sends += ring_tree("y+", "y-", kind, (1, 0), chunk, other)
        return sends
    sends = ring_tree("y+", "y-", kind, (0, 0), chunk, extra)
    return sends + [("z", kind, (0, shift), chunk) for shift in (0, 1, 3, 2)]


def gather_tensor(kind, chunk, extra):
    other = "x-" if extra == "x+" else "x+"
    sends = [("h", kind, (0, 0, 0), chunk)]
    sends += ring_tree("x+", "x-", kind, (0, 0, 0), chunk, extra)
    sends += ring_tree("x+", "x-", kind, (1, 0, 0), chunk, other)
    sends += [("c", kind, (flip, shift, 0), chunk) for flip in (0, 1) for shift in (0, 1, 3, 2)]
    return sends


def row_cuts(rows, pieces):
    step = -(-rows // (16 * pieces)) * 16
    return [(start, min(step, rows - start)) for start in range(0, rows, step)]


class Flow:
    def __init__(self):
        self.sends = {}
        self.tasks = []
        self.left_already = set()

    def send(self, name, link, priority, megabytes, source, target, to, over=()):
        assert name not in self.sends
        self.sends[name] = (link, priority, megabytes, source, target, to, over)
        return name

    def task(self, needs, cost, run, sends=(), rank=5, after=(), name=None):
        self.tasks.append((frozenset(needs), cost, run, tuple(sends), rank, frozenset(after), name))

    def arrange(self):
        free, flying, queues = {}, {}, {}
        landed, done, order, heap = set(), set(), [], []
        left = list(range(len(self.tasks)))
        now, serial = 0.0, 0

        def pump(link):
            while queues.get(link) and flying.get(link, 0) < DEPTH.get(link, 1000):
                name = heapq.heappop(queues[link])[2]
                flying[link] = flying.get(link, 0) + 1
                over = self.sends[name][6] + (("z",) if link == "h" else ())
                for each in (link,) + over:
                    free[each] = max(free.get(each, 0.0), now) + self.sends[name][2] / LINK_RATES[each]
                there = max(free[each] for each in (link,) + over)
                heapq.heappush(heap, (there + LATENCY.get(link, HOP), len(order), name))
                order.append(("start", name))

        while left or heap:
            if heap and heap[0][0] <= now:
                name = heapq.heappop(heap)[2]
                link = self.sends[name][0]
                landed.add(name)
                flying[link] -= 1
                order.append(("arrive", name))
                now += 0.03
                for number in list(left):
                    needs, cost, run, sends, rank, after, _ = self.tasks[number]
                    if rank == 0 and name in needs and needs <= landed and after <= done:
                        left.remove(number)
                        for send in sends:
                            serial += 1
                            put = (self.sends[send][1], serial, send)
                            heapq.heappush(queues.setdefault(self.sends[send][0], []), put)
                for other in sorted(queues):
                    pump(other)
                continue
            ready = []
            for number in left:
                needs, _, _, _, rank, after, _ = self.tasks[number]
                if after <= done and needs <= landed:
                    ready.append((rank, number))
            if not ready:
                assert heap
                now = max(now, heap[0][0])
                continue
            number = min(ready)[1]
            left.remove(number)
            order.append(("run", number))
            _, cost, _, sends, _, _, name = self.tasks[number]
            now += cost
            if name is not None:
                done.add(name)
            for send in sends:
                serial += 1
                put = (self.sends[send][1], serial, send)
                heapq.heappush(queues.setdefault(self.sends[send][0], []), put)
            for other in sorted(queues):
                pump(other)
        self.length = now
        assert not any(queues.values())
        return order

    def copy_of(self, name):
        _, _, _, source, target, to, _ = self.sends[name]
        number = self.number_of[name]
        return pltpu.make_async_remote_copy(
            src_ref=source(),
            dst_ref=target(),
            send_sem=self.send_sem.at[number],
            recv_sem=self.recv_sem.at[number],
            device_id=to(),
            device_id_type=MESH,
        )

    def wait_left(self, names):
        for name in names:
            if name not in self.left_already:
                self.left_already.add(name)
                self.copy_of(name).wait_send()

    def emit(self, order, send_sem, recv_sem):
        self.number_of = {name: number for number, name in enumerate(self.sends)}
        self.send_sem, self.recv_sem = send_sem, recv_sem
        arrived, started = set(), set()
        needed = {send: needs for needs, _, _, sends, _, _, _ in self.tasks for send in sends}

        def wait_for(names):
            for name in sorted(names - arrived, key=str):
                self.copy_of(name).wait_recv()
                arrived.add(name)

        for what, which in order:
            if what == "start":
                wait_for(needed[which])
                self.copy_of(which).start()
                started.add(which)
            elif what == "run":
                wait_for(self.tasks[which][0])
                if self.tasks[which][2] is not None:
                    self.tasks[which][2]()
        wait_for(set(self.sends))
        assert arrived == set(self.sends) and started == set(self.sends)
        self.wait_left(list(self.sends))


DEPTH = {"y+": 3, "y-": 3, "z": 3, "x+": 2, "x-": 2, "h": 2}
LINK_RATES = {
    "y+": 0.0455, "y-": 0.0455, "z": 0.0455, "x+": 0.0455, "x-": 0.0455, "h": 0.0455, "c": 0.12, "far": 0.5, "s": 0.2,
}
HOP = 2.7
LATENCY = {"h": 3.5}
PEER_OVER = {
    (1, 2): ("z", "y+"), (0, 2): ("y+", "y-"), (1, 1): ("z", "y+"), (1, 3): ("z", "y-"),
    (1, 0): ("z",), (0, 1): ("y+",), (0, 3): ("y-",),
}
DP_PEERS = ((1, 2), (0, 2), (1, 1), (1, 3), (1, 0), (0, 1), (0, 3))
W_PARTS = 2
X_CUTS = 7
X_MODES = ((False, "y+"), (False, "y-"), (True, "y+"), (True, "y-"), (True, "y+"), (True, "y-"), (True, "y+"))
INNER_MODES = ((True, "y+"), (False, "y-"), (True, "y-"), (False, "y+"))
RELS = [(flip, shift) for flip in (0, 1) for shift in (0, 1, 3, 2)]
TILE = 256


def slot_of(rel):
    return rel[0] * 4 + rel[1] - 1


def aligned(start, size):
    return pl.ds(pl.multiple_of(start, size), size)


def whole_kernel(
    sizes, x_ref, wq_ref, wk_ref, e_ref, q_ref, k_ref, tokens_ref,
    ge_ref, gq_ref, gk_ref, queries_ref, keys_ref,
    x_pad, x_all, raw, w_all, e_all, o_all, total, inner_own, inner_all, grown_sum,
    lanes, squares, squares_in,
    masked, core_in, left_in, right_in, left_block, right_block, half_in, chosen_all, chosen_sum, hidden,
    q_out, q_in, k_out, k_in, own_part, chunk_squares, chunk_in,
    send_sem, recv_sem, local_sem,
):
    place = Place()
    vocab_rows, slab = x_ref.shape
    new_cols, old_width = e_ref.shape
    new_width = sizes
    head_cols = q_ref.shape[0]
    token_rows = tokens_ref.shape[1]
    turned = (wq_ref, wk_ref)
    out_slab, in_slab = wq_ref.shape
    grown = (gq_ref, gk_ref)
    per_seq = queries_ref.shape[0]
    cuts = row_cuts(vocab_rows, X_CUTS)
    assert len(cuts) == X_CUTS

    barrier = pltpu.get_barrier_semaphore()
    friends = [place.across(link) for link in ("x+", "x-", "h", "c")]
    friends += [(place.dp_at(rel), place.tensor) for rel in DP_PEERS]
    for friend in friends:
        pl.semaphore_signal(barrier, inc=1, device_id=friend, device_id_type=MESH)
    local = [
        pltpu.make_async_copy(x_ref, x_pad.at[pl.ds(0, vocab_rows), :], local_sem.at[0]),
        pltpu.make_async_copy(wq_ref, w_all.at[0, place.tensor], local_sem.at[1]),
        pltpu.make_async_copy(wk_ref, w_all.at[1, place.tensor], local_sem.at[2]),
        pltpu.make_async_copy(q_ref, o_all.at[0], local_sem.at[3]),
        pltpu.make_async_copy(e_ref, e_all, local_sem.at[4]),
        pltpu.make_async_copy(k_ref, o_all.at[1], local_sem.at[5]),
    ]
    for copy in local:
        copy.start()
    pl.semaphore_wait(barrier, len(friends))

    flow = Flow()

    def gather(kind, sends, megabytes, priority, source, target, ready):
        brought = {}
        for link, _, rel, chunk in sends:
            brought[(seen_by_receiver(link, rel), chunk)] = (kind, link, rel, chunk)
        first, after = {}, {}
        for link, _, rel, chunk in sends:
            name = flow.send(
                (kind, link, rel, chunk), link, priority(link, chunk), megabytes(chunk),
                lambda rel=rel, chunk=chunk: source(rel, chunk),
                lambda link=link, rel=rel, chunk=chunk: target(seen_by_receiver(link, rel), rel, chunk),
                lambda link=link: place.across(link),
            )
            if (rel, chunk) in brought:
                after.setdefault(brought[(rel, chunk)], []).append(name)
            else:
                assert not any(rel)
                first.setdefault(ready(chunk), []).append(name)
        for cause, names in first.items():
            flow.task((), 0.05, None, names, rank=0.5, after=cause)
        for cause, names in after.items():
            flow.task((cause,), 0.0, None, names, rank=0)
        return brought

    sends = []
    for chunk in range(2 * W_PARTS):
        sends += gather_tensor("W", chunk, ("x+", "x-")[chunk % 2])
    w_rows = out_slab // W_PARTS

    def w_view(ref, chunk):
        return ref.at[pl.ds((chunk % W_PARTS) * w_rows, w_rows), :]

    def w_target(rel, chunk):
        return w_view(w_all.at[chunk // W_PARTS, place.tensor_at(rel)], chunk)

    w_from = gather(
        "W", sends, lambda chunk: w_rows * in_slab * 2e-6, lambda link, chunk: 1 + chunk // W_PARTS,
        lambda rel, chunk: w_target(rel, chunk) if any(rel) else w_view(turned[chunk // W_PARTS], chunk),
        lambda _, rel, chunk: w_target(rel, chunk), lambda chunk: (),
    )

    sends = []
    for chunk, (z_first, extra) in enumerate(X_MODES):
        sends += gather_dp("X", chunk, z_first, extra)

    def x_source(rel, chunk):
        rows = pl.ds(*cuts[chunk])
        return x_ref.at[rows, :] if not any(rel) else x_all.at[slot_of(rel), rows, :]

    x_from = gather(
        "X", sends, lambda chunk: cuts[chunk][1] * slab * 2e-6,
        lambda link, chunk: 10 + (link == "z" and not X_MODES[chunk][0]),
        x_source, lambda there, rel, chunk: x_all.at[slot_of(there), pl.ds(*cuts[chunk]), :], lambda chunk: (),
    )

    pair = 2 * out_slab

    def add_inner(rel, matrix, fresh, last):
        chip = place.tensor_at((rel[0], rel[1], 0)) // 2
        slabs = w_all[matrix, pl.ds(chip * 2, 2)].reshape(pair, in_slab)
        part = jnp.dot(o_all[matrix, :, aligned(chip * pair, pair)], slabs, preferred_element_type=jnp.float32)
        if not fresh:
            part = part + total[matrix]
        if last:
            inner_own[matrix] = part.astype(jnp.bfloat16)
        else:
            total[matrix] = part

    counts = {}

    def counted(key, times, run):
        def go():
            counts[key] = counts.get(key, 0) + 1
            run(counts[key] == 1, counts[key] == times)

        return go

    flow.task((), 0.3, lambda: [local[number].wait() for number in (1, 2, 3, 5)], rank=2, name=("w",))
    for matrix in range(2):
        units = []
        for rel in RELS:
            needs = [
                w_from[(rel + (core,), matrix * W_PARTS + part)]
                for core in (0, 1) for part in range(W_PARTS) if any(rel) or core
            ]
            units.append(("inner", rel, matrix))
            run = counted(
                ("inner", matrix), len(RELS),
                lambda fresh, last, rel=rel, matrix=matrix: add_inner(rel, matrix, fresh, last),
            )
            flow.task(needs, 0.6, run, rank=2 + matrix, after=(("w",),), name=units[-1])
        flow.task((), 0.0, None, rank=2, after=units, name=("inner", matrix))

    tiles = new_cols // TILE

    def e_columns(rel):
        return pl.ds(pl.multiple_of(place.dp_at(rel) * slab, 128), slab)

    def add_raw(rel, half, fresh):
        columns = e_columns(rel)

        def body(number, _):
            rows = aligned(number * TILE, TILE)
            block = x_all[slot_of(rel)] if any(rel) else x_pad[pl.ds(0, vocab_rows), :]
            part = lax.dot_general(block, e_all[rows, columns], LAST, preferred_element_type=jnp.float32)
            if fresh:
                raw[:, rows] = part
            else:
                raw[:, rows] += part
            return 0

        lax.fori_loop(half * tiles // 2, (half + 1) * tiles // 2, body, 0)

    raw_units = []
    for rel in RELS:
        for half in range(2):
            needs = [x_from[(rel, chunk)] for chunk in range(X_CUTS)] if any(rel) else []
            run = counted(
                ("raw", half), len(RELS), lambda fresh, last, rel=rel, half=half: add_raw(rel, half, fresh)
            )
            raw_units.append(("raw", rel, half))
            flow.task(needs, 1.3, run, rank=6, after=(("e",),), name=raw_units[-1])

    core_rows, chip_rows, own_rows = token_rows // 2, token_rows // 8, token_rows // 16
    mine = place.core * core_rows
    theirs = (1 - place.core) * core_rows

    def rows_of(core, shift, part=None):
        start = (1 - place.core if core else place.core) * core_rows + ((place.x + shift + 4) % 4) * chip_rows
        if part is None:
            return aligned(start, chip_rows)
        return aligned(start + part * own_rows, own_rows)

    def small_rows(flip):
        z_hi = 1 - place.z_hi if flip else place.z_hi
        return aligned(mine + place.x * chip_rows + z_hi * own_rows, own_rows)

    def lane_sums(values_ref, rows):
        sums = None
        for start in range(0, values_ref.shape[1], 128):
            part = jnp.square(values_ref[pl.ds(0, rows), start:start + 128].astype(jnp.float32))
            sums = part if sums is None else sums + part
        return sums

    def row_sums(values_ref):
        lanes[pl.ds(lanes.shape[0] - 32, 32), :] = jnp.zeros((32, 128), jnp.float32)
        lanes[pl.ds(0, vocab_rows), :] = lane_sums(values_ref, vocab_rows)
        return jnp.broadcast_to(jnp.sum(lanes[...].T, axis=0, keepdims=True), squares.shape)

    def load_x():
        local[0].wait()
        end = pl.ds(x_pad.shape[0] - 32, 32)
        row = lax.broadcasted_iota(jnp.int32, (32, slab), 0) + (x_pad.shape[0] - 32)
        x_pad[end, :] = jnp.where(row < vocab_rows, x_pad[end, :].astype(jnp.float32), 0.0).astype(jnp.bfloat16)

    def choose(start):
        def body(number, _):
            rows = aligned(start + number * TILE, TILE)
            row = jnp.broadcast_to(tokens_ref[:, rows].astype(jnp.float32), (128, TILE))
            ids = row.T[:, :1].astype(jnp.int32) - place.tensor * vocab_rows
            column = lax.broadcasted_iota(jnp.int32, (TILE, x_pad.shape[0]), 1)
            one = jnp.where((ids == column) & (column < vocab_rows), 1.0, 0.0).astype(jnp.bfloat16)
            masked[rows, :] = jnp.dot(one, x_pad[...], preferred_element_type=jnp.float32).astype(jnp.bfloat16)
            return 0

        lax.fori_loop(0, core_rows // TILE, body, 0)

    def to(link):
        return lambda: place.across(link)

    core_mb = core_rows * slab * 2e-6
    block_mb = core_mb / 4
    flow.send("c1", "c", 0, core_mb, lambda: masked.at[aligned(theirs, core_rows), :], lambda: core_in, to("c"))
    flow.task((), 1.0, load_x, rank=1, name=("x",))
    flow.task((), 1.2, lambda: choose(theirs), ("c1",), rank=1, name=("theirs",), after=(("x",),))
    flow.task((), 1.2, lambda: choose(mine), rank=1, name=("mine",), after=(("theirs",),))

    def add_core():
        rows = aligned(mine, core_rows)
        masked[rows, :] += core_in[...]

    flow.send("r+", "x+", 0, block_mb / 2, lambda: masked.at[rows_of(0, 2, 0), :], lambda: left_in, to("x+"))
    flow.send("r-", "x-", 0, block_mb / 2, lambda: masked.at[rows_of(0, 2, 1), :], lambda: right_in, to("x-"))
    flow.task(("c1",), 0.5, add_core, ("r+", "r-"), rank=1, name=("core",), after=(("mine",),))

    def add_left():
        masked[rows_of(0, 1, 0), :] += left_in[...]

    def add_right():
        masked[rows_of(0, 3, 1), :] += right_in[...]

    flow.send("b+", "x+", 0, block_mb, lambda: masked.at[rows_of(0, 1), :], lambda: left_block, to("x+"))
    flow.send("b-", "x-", 0, block_mb, lambda: masked.at[rows_of(0, 3), :], lambda: right_block, to("x-"))
    flow.task(("r+",), 0.1, add_left, ("b+",), rank=1, after=(("core",),))
    flow.task(("r-",), 0.1, add_right, ("b-",), rank=1, after=(("core",),))

    def add_blocks():
        masked[rows_of(0, 0), :] += left_block[...] + right_block[...]

    flow.send("h1", "h", 0, block_mb / 2, lambda: masked.at[small_rows(1), :], lambda: half_in, to("h"))
    flow.task(("b+", "b-"), 0.2, add_blocks, ("h1",), rank=1, name=("blocks",), after=(("core",),))

    def add_half():
        chosen_all[0] = masked[small_rows(0), :] + half_in[...]

    flow.task(("h1",), 0.1, add_half, rank=1, name=("chosen",), after=(("blocks",),))
    t_from = gather(
        "T", gather_dp("T", 0, True, "y+"), lambda chunk: own_rows * slab * 2e-6, lambda link, chunk: 0,
        lambda rel, chunk: chosen_all.at[slot_of(rel) + 1], lambda there, rel, chunk: chosen_all.at[slot_of(there) + 1],
        lambda chunk: (("chosen",),),
    )

    def grow_chosen(rel, fresh, last):
        at = slot_of(rel) + 1
        columns = e_columns(rel)

        def body(number, _):
            rows = aligned(number * TILE, TILE)
            part = lax.dot_general(
                chosen_all[at], e_all[rows, columns], LAST, preferred_element_type=jnp.float32
            )
            if fresh:
                chosen_sum[:, rows] = part
            else:
                chosen_sum[:, rows] += part
            return 0

        lax.fori_loop(0, tiles, body, 0)
        if last:
            sums = None
            for start in range(0, new_cols, 128):
                part = jnp.square(chosen_sum[:, start:start + 128])
                sums = part if sums is None else sums + part
            lanes[pl.ds(0, own_rows), :] = sums
            lanes[pl.ds(own_rows, 128 - own_rows), :] = jnp.zeros((128 - own_rows, 128), jnp.float32)
            row = jnp.sum(lanes[pl.ds(0, 128), :].T, axis=0, keepdims=True)
            chunk_squares[...] = jnp.broadcast_to(row, chunk_squares.shape)

    def scale_chosen():
        row = chunk_squares[...]
        for number in range(len(DP_PEERS)):
            row = row + chunk_in[number]
        raw_ms = jnp.broadcast_to(row[:1], (128, 128)).T[:own_rows, :1] / new_width
        old_squares = None
        for number in range(N_DP):
            for start in range(0, slab, 128):
                part = jnp.square(chosen_all[number, :, start:start + 128].astype(jnp.float32))
                old_squares = part if old_squares is None else old_squares + part
        old_ms = jnp.sum(old_squares, axis=1, keepdims=True) / old_width
        factor = jnp.sqrt((old_ms + EMBED_EPSILON) / (raw_ms + EMBED_EPSILON))
        scale = factor * lax.rsqrt(factor * factor * raw_ms + TOKEN_EPSILON)
        hidden[small_rows(0), :] = (chosen_sum[...] * scale).astype(jnp.bfloat16)

    chunk_sends = [
        flow.send(
            ("Q", number), "s", 0, 0.004, lambda: chunk_squares, lambda number=number: chunk_in.at[number],
            lambda rel=rel: (place.dp_at(rel), place.tensor),
        )
        for number, rel in enumerate(DP_PEERS)
    ]

    units = []
    flow.task((), 0.1, lambda: local[4].wait(), rank=4, name=("e",))
    for rel in RELS:
        needs = [t_from[(rel, 0)]] if any(rel) else []
        run = counted("chosen", len(RELS), lambda fresh, last, rel=rel: grow_chosen(rel, fresh, last))
        units.append(("chosen", rel))
        flow.task(needs, 0.9, run, rank=1.5, after=(("e",), ("chosen",)), name=units[-1])

    own_mb = own_rows * hidden.shape[1] * 2e-6

    def same(name, link, megabytes, rows):
        return flow.send(
            name, link, 0, megabytes, lambda: hidden.at[rows(), :], lambda: hidden.at[rows(), :], to(link)
        )

    same("h2", "h", own_mb, lambda: small_rows(0))
    same("a+", "x+", 2 * own_mb, lambda: rows_of(0, 0))
    same("a-", "x-", 2 * own_mb, lambda: rows_of(0, 0))
    same("f+", "x+", own_mb, lambda: rows_of(0, 3, 0))
    same("f-", "x-", own_mb, lambda: rows_of(0, 1, 1))
    for shift in range(4):
        same(("c", shift), "c", 2 * own_mb, lambda shift=shift: rows_of(0, shift))
    flow.task((), 0.0, None, chunk_sends, rank=0.5, after=units, name=("chunk",))
    flow.task(chunk_sends, 0.5, scale_chosen, ("h2",), rank=0.5, after=(("chunk",),), name=("hidden",))
    flow.task(("h2",), 0.02, None, ("a+", "a-", ("c", 0)), rank=0.5, after=(("hidden",),))
    flow.task(("a+",), 0.0, None, ("f+", ("c", 3)), rank=0)
    flow.task(("a-",), 0.0, None, ("f-", ("c", 1)), rank=0)
    flow.task(("f+", "f-"), 0.0, None, (("c", 2),), rank=0)

    half = head_cols // 2
    sends = []
    for chunk, (z_first, extra) in enumerate(INNER_MODES):
        sends += gather_dp("I", chunk, z_first, extra)

    def inner_view(ref, chunk):
        return ref.at[chunk // 2, pl.ds((chunk % 2) * half, half), :]

    def i_source(rel, chunk):
        return inner_view(inner_all.at[slot_of(rel)] if any(rel) else inner_own, chunk)

    i_from = gather(
        "I", sends, lambda chunk: half * in_slab * 2e-6, lambda link, chunk: 3 + chunk // 2,
        i_source, lambda there, rel, chunk: inner_view(inner_all.at[slot_of(there)], chunk),
        lambda chunk: (("inner", chunk // 2),),
    )

    def add_grown(rel, matrix, fresh, last):
        columns = e_columns(rel)

        def body(number, _):
            rows = aligned(number * TILE, TILE)
            block = inner_all[slot_of(rel), matrix] if any(rel) else inner_own[matrix]
            part = lax.dot_general(e_all[rows, columns], block, LAST, preferred_element_type=jnp.float32)
            if not fresh:
                part = part + grown_sum[matrix, rows, :]
            if last:
                grown[matrix][rows, :] = part.astype(jnp.bfloat16)
            else:
                grown_sum[matrix, rows, :] = part
            return 0

        lax.fori_loop(0, tiles, body, 0)

    for matrix in range(2):
        units = []
        for rel in RELS:
            needs = [i_from[(rel, chunk)] for chunk in (2 * matrix, 2 * matrix + 1)] if any(rel) else []
            run = counted(
                ("grown", matrix), len(RELS),
                lambda fresh, last, rel=rel, matrix=matrix: add_grown(rel, matrix, fresh, last),
            )
            units.append(("grown", rel, matrix))
            flow.task(needs, 0.9, run, rank=3, after=(("e",), ("inner", matrix)), name=units[-1])
        flow.task((), 0.0, None, rank=3, after=units, name=("grown", matrix))

    def square_rows():
        row = lax.broadcasted_iota(jnp.int32, squares.shape, 0)
        squares[...] = jnp.where(row == 1, row_sums(x_pad), 0.0)
        squares[...] = jnp.where(row == 0, row_sums(raw), squares[...])

    square_sends = [
        flow.send(
            ("S", number), "s", 0, 0.03, lambda: squares, lambda number=number: squares_in.at[number],
            lambda rel=rel: (place.dp_at(rel), place.tensor),
        )
        for number, rel in enumerate(DP_PEERS)
    ]
    flow.task((), 2.5, square_rows, square_sends, rank=4, after=raw_units, name=("squares",))
    ge_cuts = ((0, slab, slot_of((1, 2))), (slab, new_cols - slab, slot_of((0, 2))))

    def ge_copies():
        return [
            pltpu.make_async_copy(
                x_all.at[slot, :, pl.ds(0, size)], ge_ref.at[:, pl.ds(start, size)], local_sem.at[6 + number]
            )
            for number, (start, size, slot) in enumerate(ge_cuts)
        ]

    def rescale():
        flow.wait_left([name for name in flow.sends if name[0] == "X"])
        sums = squares[...]
        for number in range(len(DP_PEERS)):
            sums = sums + squares_in[number]
        factor = jnp.sqrt((sums[1:2] / old_width + EMBED_EPSILON) / (sums[0:1] / new_width + EMBED_EPSILON))
        column = jnp.broadcast_to(factor, (128, factor.shape[1])).T[:vocab_rows]
        for start, size, slot in ge_cuts:
            for at in range(0, size, 128):
                scaled = raw[:, start + at:start + at + 128] * column
                x_all[slot, :, at:at + 128] = scaled.astype(jnp.bfloat16)
        for copy in ge_copies():
            copy.start()

    flow.task(square_sends, 2.5, rescale, rank=5, name=("scaled",), after=(("squares",),))

    def seq_rows(rel):
        return aligned(place.dp_at(rel) * per_seq, per_seq)

    def partial(rel, matrix):
        block = hidden[seq_rows(rel), :]
        return jnp.dot(block, grown[matrix][...], preferred_element_type=jnp.float32)

    def put_query(number, rel):
        q_out[number] = partial(rel, 0).astype(jnp.bfloat16)

    def put_key(number, rel):
        k_out[number] = partial(rel, 1).astype(jnp.bfloat16)

    gathered = ["h2", "a+", "a-", "f+", "f-"] + [("c", shift) for shift in range(4)]
    arrivals = []
    for matrix, (put, out, into) in enumerate(((put_query, q_out, q_in), (put_key, k_out, k_in))):
        for number, rel in enumerate(DP_PEERS):
            name = flow.send(
                ("P", matrix, number), "far", 0, per_seq * out.shape[2] * 2e-6,
                lambda out=out, number=number: out.at[number], lambda into=into, number=number: into.at[number],
                lambda rel=rel: (place.dp_at(rel), place.tensor), PEER_OVER[rel],
            )
            arrivals.append(name)
            flow.task(
                gathered, 0.4, lambda put=put, number=number, rel=rel: put(number, rel), (name,),
                rank=2.5, after=(("grown", matrix), ("hidden",)),
            )

    def keep_own(matrix):
        own_part[:, matrix * head_cols:(matrix + 1) * head_cols] = partial((0, 0), matrix)

    for matrix in range(2):
        flow.task(
            gathered, 0.4, lambda matrix=matrix: keep_own(matrix), rank=3.5,
            after=(("grown", matrix), ("hidden",)), name=("own", matrix),
        )

    def add_up():
        for matrix, into in enumerate((q_in, k_in)):
            columns = pl.ds(matrix * head_cols, head_cols)
            sums = own_part[:, columns]
            for number in range(len(DP_PEERS)):
                sums = sums + into[number].astype(jnp.float32)
            (queries_ref, keys_ref)[matrix][...] = sums

    flow.task(arrivals, 1.0, add_up, rank=9, after=(("own", 0), ("own", 1)))
    order = flow.arrange()
    flow.emit(order, send_sem, recv_sem)
    for copy in ge_copies():
        copy.wait()


def grow_and_check(token_ids, old_embed, expand_in, query_out, key_out, old_query, old_key):
    vocab_rows, slab = old_embed.shape
    in_slab, out_slab = old_query.shape
    new_cols = expand_in.shape[0]
    head_cols = query_out.shape[0]
    tokens = token_ids.shape[0]
    padded = -(-vocab_rows // 128) * 128
    per_seq = tokens // N_DP
    anywhere = pl.BlockSpec(memory_space=pl.ANY)
    inside = pl.BlockSpec(memory_space=pltpu.VMEM)
    bf16, f32 = jnp.bfloat16, jnp.float32
    count = (2 * W_PARTS * 15) + 7 * X_CUTS + 7 * len(INNER_MODES) + 7 + 1 + 4 + 1 + 9 + 7 + 14 + 7
    return pl.pallas_call(
        lambda *refs: whole_kernel(D_NEW, *refs),
        out_shape=(
            jax.ShapeDtypeStruct((vocab_rows, new_cols), bf16),
            jax.ShapeDtypeStruct((new_cols, head_cols), bf16),
            jax.ShapeDtypeStruct((new_cols, head_cols), bf16),
            jax.ShapeDtypeStruct((per_seq, head_cols), f32),
            jax.ShapeDtypeStruct((per_seq, head_cols), f32),
        ),
        in_specs=[anywhere] * 6 + [inside],
        out_specs=(anywhere, inside, inside, inside, inside),
        scratch_shapes=[
            pltpu.VMEM((padded, slab), bf16),
            pltpu.VMEM((N_DP - 1, vocab_rows, slab), bf16),
            pltpu.VMEM((vocab_rows, new_cols), f32),
            pltpu.VMEM((2, N_TENSOR, out_slab, in_slab), bf16),
            pltpu.VMEM(expand_in.shape, bf16),
            pltpu.VMEM((2,) + query_out.shape, bf16),
            pltpu.VMEM((2, head_cols, in_slab), f32),
            pltpu.VMEM((2, head_cols, in_slab), bf16),
            pltpu.VMEM((N_DP - 1, 2, head_cols, in_slab), bf16),
            pltpu.VMEM((2, new_cols, head_cols), f32),
            pltpu.VMEM((padded, 128), f32),
            pltpu.VMEM((8, padded), f32),
            pltpu.VMEM((7, 8, padded), f32),
            pltpu.VMEM((tokens, slab), bf16),
            pltpu.VMEM((tokens // 2, slab), bf16),
            pltpu.VMEM((tokens // 16, slab), bf16),
            pltpu.VMEM((tokens // 16, slab), bf16),
            pltpu.VMEM((tokens // 8, slab), bf16),
            pltpu.VMEM((tokens // 8, slab), bf16),
            pltpu.VMEM((tokens // 16, slab), bf16),
            pltpu.VMEM((N_DP, tokens // 16, slab), bf16),
            pltpu.VMEM((tokens // 16, new_cols), f32),
            pltpu.VMEM((tokens, new_cols), bf16),
            pltpu.VMEM((7, per_seq, head_cols), bf16),
            pltpu.VMEM((7, per_seq, head_cols), bf16),
            pltpu.VMEM((7, per_seq, head_cols), bf16),
            pltpu.VMEM((7, per_seq, head_cols), bf16),
            pltpu.VMEM((per_seq, 2 * head_cols), f32),
            pltpu.VMEM((8, 128), f32),
            pltpu.VMEM((7, 8, 128), f32),
            pltpu.SemaphoreType.DMA((count,)),
            pltpu.SemaphoreType.DMA((count,)),
            pltpu.SemaphoreType.DMA((8,)),
        ],
        compiler_params=pltpu.CompilerParams(
            collective_id=1, has_side_effects=True, vmem_limit_bytes=VMEM_LIMIT
        ),
        name="grow_and_check",
    )(old_embed, old_query.T, old_key.T, expand_in, query_out, key_out, token_ids.reshape(1, tokens))


def rotate(values, head_count):
    row_count = values.shape[0]
    shaped = values.reshape(row_count, head_count, HEAD)
    half_size = HEAD // 2
    position = jnp.arange(row_count).astype(jnp.float32)
    frequency = jnp.exp(
        -math.log(10000.0) * jnp.arange(half_size).astype(jnp.float32) * (2.0 / HEAD)
    )
    angles = position[:, None] * frequency[None, :]
    cosine = jnp.cos(angles)[:, None, :]
    sine_table = jnp.sin(angles)[:, None, :]
    first_half = shaped[..., :half_size]
    second = shaped[..., half_size:]
    return jnp.concatenate(
        [first_half * cosine - second * sine_table, second * cosine + first_half * sine_table],
        axis=-1,
    )


def entropy_of(queries, key_proj, head_count):
    rotated_q = rotate(queries, head_count).astype(jnp.bfloat16)
    rotated_k = rotate(key_proj, head_count).astype(jnp.bfloat16)
    scores = jnp.einsum(
        "ihd,jhd->hij", rotated_q, rotated_k, preferred_element_type=jnp.float32
    ) * HEAD ** (-0.5)
    row_count = queries.shape[0]
    causal = jnp.arange(row_count)[:, None] >= jnp.arange(row_count)[None, :]
    weights = jnp.where(causal[None], jnp.exp(scores), 0.0)
    weight_sum = jnp.sum(weights, axis=-1)
    entropy = jnp.log(weight_sum) - jnp.sum(weights * scores, axis=-1) / weight_sum
    return entropy.T


def on_device(token_ids, old_embed, expand_in, query_out, key_out, old_query, old_key):
    head_cols = query_out.shape[0]
    grown_embedding, grown_query, grown_key, queries, keys = grow_and_check(
        token_ids, old_embed, expand_in, query_out, key_out, old_query, old_key
    )
    attention_entropy = entropy_of(queries, keys, head_cols // HEAD)
    return (grown_embedding, grown_query, grown_key, attention_entropy)


def solution(mesh):
    placed = (
        P(),
        P("tensor", "dp"),
        P("dp", None),
        P("tensor", None),
        P("tensor", None),
        P("dp", "tensor"),
        P("dp", "tensor"),
    )
    return jax.shard_map(
        on_device,
        mesh=mesh,
        in_specs=placed,
        out_specs=(P("tensor", "dp"), P("dp", "tensor"), P("dp", "tensor"), P("dp", "tensor")),
        check_vma=False,
    )
```
